32 devices in a mesh: grp: 2 (over y), ep: 4 (over z), tp: 4 (over x, core).
Axes of the slice: x: 2, y: 2, z: 4, core: 2. Of those that a mesh axis runs over, the one named last changes fastest.
Arguments:
- question_q: bfloat16 [1024, 32, 128], P(('grp', 'ep'), 'tp'), parts along dimension 0, may hold values from -125 to 125
- question_kv: bfloat16 [1024, 4, 2, 128], P(('grp', 'ep')), parts along dimension 0, may hold values from -6 to 6
- doc_kv: bfloat16 [16, 128, 4, 2, 128], P(('grp', 'ep')), parts along dimension 0, may hold values from -6 to 6
- doc_lens: int32 [16], P('grp'), parts along dimension 0, may hold values from 1 to 128, as said below
- query_docs: int32 [8, 4], P('grp'), parts along dimension 0, may hold values from 0 to 7, as said below
- ctx_pos: int32 [8, 5], P('grp'), parts along dimension 0, may hold values from 0 to 827, as said below
- hidden: bfloat16 [1024, 4096], P(('grp', 'ep'), 'tp'), parts along dimension 0, may hold values from -1.5 to 1.5
- out_proj: bfloat16 [4096, 4096], P('ep', 'tp'), may hold values from -0.0234375 to 0.0234375
- norm_gain: bfloat16 [4096], P('tp'), may hold values from 0.5 to 1.5
- router_weight: bfloat16 [4096, 16], P('tp'), may hold values from -0.046875 to 0.046875
- w_gate_up: bfloat16 [16, 4096, 2, 1024], P('ep', 'tp'), may hold values from -0.09375 to 0.09375
- w_down: bfloat16 [16, 1024, 4096], P('ep', None, 'tp'), may hold values from -0.1875 to 0.1875
- expert_ids: int32 [1024, 8], P(('grp', 'ep')), parts along dimension 0, may hold values from 0 to 15, all different within a row; in each aligned block of 128 rows (0 to 127, 128 to 255, ...) at most 64 rows name the same one
Outputs:
- layer_out: bfloat16 [1024, 4096], P(('grp', 'ep'), 'tp'), parts along dimension 0
The draws below stay inside these ranges and needn't reach their ends.
There are 2 independent parts, one for each index of `grp`. The reference program is written for one: setup_inputs(seed, part) draws one part's arguments, and reference() takes and returns one part's arrays. A program takes and returns all parts, laid end to end along the dimension named above; an argument that names none is the same for every part. Nothing has to cross between parts.
Inputs may be any that keep to these rules, and one draw needn't show every extreme that they name: `doc_lens`: document d is held at row d of doc_kv; some document of some query's list has exactly 128 tokens. `query_docs`: the 4 documents of a query lie in 4 different blocks of 2 consecutive documents. `ctx_pos`: in each row, every entry is at least the one before it plus the length of the document before it. `expert_ids`: each query's 128 tokens name every expert exactly 64 times.
All inputs are finite; a program needn't handle non-finite values.
Results may differ from the reference program's by a relative error of at most 0.017.
Values may be sent and summed in bfloat16 or wider, within the bound.
A program may use at most 128 MiB of HBM per device.

```python
import math
import jax
import jax.numpy as jnp
import numpy as np
from jax import lax

D = 4096
QH = 32
KVH = 4
HD = 128
HID = 1024
TOP = 8
QLEN = 128
DOC_MAX = 128
POOL_DEV = 2
EXPERTS = 16
CAP = 64
DPQ = 4
QUERIES = 4
TOKENS = 512
POOL_DOCS = 8
N_TP = 4


def pool_plan(key):
    base = jax.random.fold_in(key, 11)
    owner_key, local_key, length_key, gap_key = jax.random.split(base, 4)
    owners_all = POOL_DOCS // POOL_DEV
    scores = jax.random.randint(owner_key, (QUERIES, owners_all), 0, 1 << 20) * owners_all + jnp.arange(owners_all, dtype=jnp.int32)[None, :]
    owners = jnp.argsort(scores, axis=1)[:, :DPQ].astype(jnp.int32)
    local = jax.random.randint(local_key, (QUERIES, DPQ), 0, POOL_DEV)
    docs = owners * POOL_DEV + local
    lengths = jax.random.randint(length_key, (POOL_DOCS,), 1, DOC_MAX + 1)
    lengths = lengths.at[docs[0]].set(DOC_MAX)
    gaps = jax.random.randint(gap_key, (QUERIES, DPQ + 1), 0, 64)
    gaps = gaps.at[0].set(63)
    spans = jnp.concatenate([jnp.zeros((QUERIES, 1), jnp.int32), lengths[docs]], axis=1)
    positions = jnp.cumsum(gaps + spans, axis=1).astype(jnp.int32)
    return (docs.astype(jnp.int32), lengths.astype(jnp.int32), positions)


def draw_doc_lens(key, part):
    return pool_plan(key)[1]


def draw_query_docs(key, part):
    return pool_plan(key)[0]


def draw_ctx_pos(key, part):
    return pool_plan(key)[2]


def draw_question_q(key, part):
    shape = (TOKENS, QH, HD)
    base_key = jax.random.fold_in(jax.random.fold_in(key, 3), 0)
    values = jnp.clip(3.0 * jax.random.normal(base_key, shape, jnp.float32), -12.0, 12.0)
    return values.astype(jnp.bfloat16)


def level_of(stream_key, dims, pieces, least, largest):
    loudness = 1.0
    for dim, shards_of in pieces:
        heights = jax.random.uniform(jax.random.fold_in(jax.random.fold_in(stream_key, 6), dim), (shards_of,), jnp.float32, least / len(pieces), largest / len(pieces))
        loudness = loudness * jnp.repeat(jnp.exp(heights), dims[dim] // shards_of).reshape((-1,) + (1,) * (len(dims) - 1 - dim))
    return loudness


def shared_out(rng, own, number, rows, count, top, reach, lean):
    ranking = jax.random.permutation(rng, count)
    heavy_load, common = portions_of(count, rows * top, reach, lean, True), portions_of(count, rows * top, reach, lean, False)
    places = jnp.arange(count)

    def named(sizes, offset_by):
        used = int((sizes > 0).sum())
        fixed = max(1, used // 4)
        passed = fixed + (places - fixed + offset_by * (used - fixed)) % max(1, count - fixed)
        return jnp.zeros((count,), jnp.int32).at[ranking[jnp.where(places < fixed, places, passed)]].set(jnp.asarray(sizes, jnp.int32))

    sizes = jnp.where(number % 4 == 0, named(heavy_load, number // 4), named(common, number - number // 4 - 1))
    mixed = jax.random.permutation(jax.random.fold_in(own, 3), count)
    donor, receiver = mixed[0:count // 2 * 2:2], mixed[1:count // 2 * 2:2]
    slack = jnp.minimum(sizes[donor] - 1, reach - sizes[receiver]) // 2
    slack = jnp.where((donor == ranking[0]) | (receiver == ranking[0]) | (sizes[receiver] == 0), 0, jnp.maximum(slack, 0))
    passed = jax.random.randint(jax.random.fold_in(own, 4), (count // 2,), 0, 1 << 20) % (slack + 1)
    sizes = sizes.at[donor].add(-passed).at[receiver].add(passed)
    members = jnp.searchsorted(jnp.cumsum(sizes), jnp.arange(rows * top), side="right").astype(jnp.int32)
    grid = members.reshape(top, rows).T
    grid = grid[jax.random.permutation(jax.random.fold_in(own, 1), rows)]
    offset_by = jax.random.randint(jax.random.fold_in(own, 2), (rows, 1), 0, top)
    return jnp.take_along_axis(grid, (jnp.arange(top)[None, :] + offset_by) % top, axis=1)


def portions_of(number_of, total, limit, lean, full):
    weights = [(1 << 20) // math.isqrt(grade ** lean) + 1 for grade in range(1, number_of + 1)]
    largest = limit if full else min(limit, max(-(-total // number_of), total * weights[0] // sum(weights)))
    least = 1 if total - largest >= number_of - 1 else 0
    given, surplus = [largest] + [least] * (number_of - 1), total - largest - least * (number_of - 1)
    while surplus > 0:
        candidates = [i for i in range(1, number_of) if given[i] < largest] or [i for i in range(1, number_of) if given[i] < limit]
        pool, budget = sum([weights[i] for i in candidates]), surplus
        for i in candidates:
            extra = min(limit - given[i], max(1, budget * weights[i] // pool), surplus)
            given[i] = given[i] + extra
            surplus = surplus - extra
    return np.array(given)


def bell_draw(rng, shape, scale, limit, shards=(), kind=jnp.bfloat16):
    level = level_of(rng, shape, shards, -0.22, 0.18) if shards else 1.0
    values = jax.random.normal(rng, shape, jnp.float32) * scale * level
    return jnp.minimum(jnp.maximum(values, -limit), limit).astype(kind)


def setup_inputs(seed: int = 0, part: int = 0) -> dict:
    splits = jax.random.split(jax.random.key(seed), 14)
    part_keys = jax.random.split(jax.random.fold_in(splits[13], part), 14)
    question_q = draw_question_q(jax.random.fold_in(jax.random.fold_in(splits[13], part), 71), part)
    question_kv = bell_draw(part_keys[1], (TOKENS, KVH, 2, HD), 1.0, 6.0, ((0, 4),))
    doc_kv = bell_draw(part_keys[2], (POOL_DOCS, DOC_MAX, KVH, 2, HD), 1.0, 6.0, ((0, 4),))
    doc_lens = draw_doc_lens(jax.random.fold_in(jax.random.fold_in(splits[13], part), 71), part)
    query_docs = draw_query_docs(jax.random.fold_in(jax.random.fold_in(splits[13], part), 71), part)
    ctx_pos = draw_ctx_pos(jax.random.fold_in(jax.random.fold_in(splits[13], part), 71), part)
    hidden = bell_draw(part_keys[6], (TOKENS, D), 0.25, 1.5, ((0, 4), (1, 4)))
    out_proj = bell_draw(splits[7], (QH * HD, D), (16 * QH * HD) ** -0.5, 0.0234375, ((0, 4), (1, 4)))
    norm_gain = jnp.clip(1.0 + 0.1 * jax.random.normal(splits[8], (D,), jnp.float32), 0.5, 1.5).astype(jnp.bfloat16)
    router_weight = bell_draw(splits[9], (D, EXPERTS), (4 * D) ** -0.5, 0.046875, ((0, 4),))
    w_gate_up = bell_draw(splits[10], (EXPERTS, D, 2, HID), D ** -0.5, 0.09375, ((0, 4), (1, 4)))
    w_down = bell_draw(splits[11], (EXPERTS, HID, D), HID ** -0.5, 0.1875, ((0, 4), (2, 4)))
    expert_ids_keys = jax.random.split(jax.random.fold_in(part_keys[12], 1), TOKENS // QLEN)
    expert_ids_turns = jax.random.permutation(jax.random.fold_in(part_keys[12], 3), TOKENS // QLEN)
    expert_ids = jax.vmap(lambda own, number: shared_out(jax.random.fold_in(part_keys[12], 2), own, number, QLEN, EXPERTS, TOP, CAP, 0))(expert_ids_keys, expert_ids_turns).reshape((TOKENS, TOP))
    return {"question_q": question_q, "question_kv": question_kv, "doc_kv": doc_kv, "doc_lens": doc_lens, "query_docs": query_docs, "ctx_pos": ctx_pos, "hidden": hidden, "out_proj": out_proj, "norm_gain": norm_gain, "router_weight": router_weight, "w_gate_up": w_gate_up, "w_down": w_down, "expert_ids": expert_ids}


rope_theta = 1000000.0
norm_eps = 1e-06

def narrow(values):
    return lax.optimization_barrier(values.astype(jnp.bfloat16))

def rotate(values, positions):
    half = values.shape[-1] // 2
    freq = jnp.exp(jnp.arange(half, dtype=jnp.float32) * (-2.0 * math.log(rope_theta) / values.shape[-1]))
    angle = positions.astype(jnp.float32)[:, None] * freq[None, :]
    shape = (values.shape[0],) + (1,) * (values.ndim - 2) + (half,)
    cosine = jnp.cos(angle).reshape(shape)
    sine = jnp.sin(angle).reshape(shape)
    floats = values.astype(jnp.float32)
    first = floats[..., :half]
    second = floats[..., half:]
    return jnp.concatenate([first * cosine - second * sine, second * cosine + first * sine], axis=-1)

def attend(q_rows, kv_rows, context, lengths, starts):
    doc_pos = jnp.repeat(starts[:DPQ], DOC_MAX, total_repeat_length=DPQ * DOC_MAX)
    doc_keys = rotate(context[:, :, :, 0].reshape(DPQ * DOC_MAX, KVH, HD), doc_pos).astype(jnp.bfloat16)
    doc_values = context[:, :, :, 1].reshape(DPQ * DOC_MAX, KVH, HD)
    question_pos = starts[DPQ] + jnp.arange(QLEN, dtype=jnp.int32)
    queries = rotate(q_rows, question_pos).astype(jnp.bfloat16)
    own_keys = rotate(kv_rows[:, :, 0], question_pos).astype(jnp.bfloat16)
    keys = jnp.concatenate([doc_keys, own_keys], axis=0)
    values = jnp.concatenate([doc_values, kv_rows[:, :, 1]], axis=0)
    valid = (jnp.arange(DOC_MAX, dtype=jnp.int32)[None, :] < lengths[:, None]).reshape(DPQ * DOC_MAX)
    causal = jnp.arange(QLEN)[:, None] >= jnp.arange(QLEN)[None, :]
    allowed = jnp.concatenate([jnp.broadcast_to(valid[None, :], (QLEN, DPQ * DOC_MAX)), causal], axis=1)
    grouped = queries.reshape(QLEN, KVH, QH // KVH, HD)
    scores = jnp.einsum('ighd,jgd->ghij', grouped.astype(jnp.float32), keys.astype(jnp.float32)) * HD ** (-0.5)
    scores = jnp.where(allowed[None, None], scores, -jnp.inf)
    ceiling = lax.optimization_barrier(jnp.max(scores, axis=-1, keepdims=True))
    probs = jnp.exp(scores - ceiling)
    denominator = lax.optimization_barrier(jnp.sum(probs, axis=-1, keepdims=True))
    mixed = jnp.einsum('ghij,jgd->ghid', narrow(probs).astype(jnp.float32), values.astype(jnp.float32)) / denominator
    return jnp.transpose(mixed, (2, 0, 1, 3)).reshape(QLEN, QH * HD).astype(jnp.bfloat16)

def reference(question_q, question_kv, doc_kv, doc_lens, query_docs, ctx_pos, hidden, out_proj, norm_gain, router_weight, w_gate_up, w_down, expert_ids):

    def one_query(index):
        q_rows = lax.dynamic_slice_in_dim(question_q, index * QLEN, QLEN, 0)
        kv_rows = lax.dynamic_slice_in_dim(question_kv, index * QLEN, QLEN, 0)
        docs = query_docs[index]
        return attend(q_rows, kv_rows, doc_kv[docs], doc_lens[docs], ctx_pos[index])
    attended = lax.map(one_query, jnp.arange(QUERIES, dtype=jnp.int32)).reshape(TOKENS, QH * HD)
    projected = jnp.dot(attended, out_proj, preferred_element_type=jnp.float32)
    residual = narrow(hidden.astype(jnp.float32) + projected).astype(jnp.float32)
    gain = norm_gain.astype(jnp.float32)
    inv_rms = lax.rsqrt(lax.optimization_barrier(jnp.mean(residual * residual, axis=1)) + norm_eps)
    normed = narrow(residual * inv_rms[:, None] * gain[None, :])
    logits = jnp.dot(residual * gain[None, :], router_weight.astype(jnp.float32), precision=lax.Precision.HIGHEST) * inv_rms[:, None]
    mix = jax.nn.softmax(jnp.take_along_axis(logits, expert_ids, axis=1), axis=1)
    flat = expert_ids.reshape(TOKENS * TOP)
    per_expert = QUERIES * CAP

    def one_expert(expert):
        rows = jnp.nonzero(flat == expert, size=per_expert)[0].astype(jnp.int32)
        inputs = jnp.take(normed, rows // TOP, axis=0).astype(jnp.float32).reshape(per_expert, N_TP, D // N_TP)
        weights = w_gate_up[expert].astype(jnp.float32).reshape(N_TP, D // N_TP, 2 * HID)
        parts = narrow(jnp.einsum('rbd,bdh->brh', inputs, weights)).astype(jnp.float32)
        summed = lax.optimization_barrier(jnp.sum(parts, axis=0))
        activated = (jax.nn.silu(summed[:, :HID]) * summed[:, HID:]).astype(jnp.bfloat16)
        output = jnp.dot(activated, w_down[expert], preferred_element_type=jnp.float32).astype(jnp.bfloat16)
        return (rows, output)
    rows, outputs = lax.map(one_expert, jnp.arange(EXPERTS, dtype=jnp.int32))
    gathered = jnp.zeros((TOKENS * TOP, D), jnp.bfloat16).at[rows.reshape(-1)].set(outputs.reshape(-1, D))
    combined = jnp.einsum('tk,tkd->td', mix, gathered.reshape(TOKENS, TOP, D).astype(jnp.float32))
    return (residual + combined).astype(jnp.bfloat16)
```

```python
import math

import jax
import jax.numpy as jnp
from jax import lax
from jax.experimental import pallas as pl
from jax.experimental.pallas import tpu as pltpu
from jax.sharding import PartitionSpec as P

D = 4096
HID = 1024


rope_theta = 1000000.0
norm_eps = 1e-06


def narrow(values):
    return lax.optimization_barrier(values.astype(jnp.bfloat16))


def rotate(values, positions):
    half = values.shape[-1] // 2
    freq = jnp.exp(
        jnp.arange(half, dtype=jnp.float32) * (-2.0 * math.log(rope_theta) / values.shape[-1])
    )
    angle = positions.astype(jnp.float32)[:, None] * freq[None, :]
    shape = (values.shape[0],) + (1,) * (values.ndim - 2) + (half,)
    cosine = jnp.cos(angle).reshape(shape)
    sine = jnp.sin(angle).reshape(shape)
    floats = values.astype(jnp.float32)
    first = floats[..., :half]
    second = floats[..., half:]
    return jnp.concatenate(
        [first * cosine - second * sine, second * cosine + first * sine], axis=-1
    )


def fetch_context(doc_kv, doc_lens, query_docs, row_pos, device, kv_pick):
    pool_dev, doc_max, kv_heads, pair, head_dim = doc_kv.shape
    docs_per = query_docs.shape[1]
    pool_head = lax.dynamic_index_in_dim(doc_kv, kv_pick, 2, keepdims=False).reshape(
        pool_dev, doc_max, pair * head_dim
    )
    held = device * pool_dev + jnp.arange(pool_dev, dtype=jnp.int32)
    wanted = jnp.sum((query_docs[:, :, None] == held[None, None, :]).astype(jnp.float32), axis=1)
    sending = jnp.einsum(
        "rl,lkc->rkc", wanted.astype(jnp.bfloat16), pool_head, preferred_element_type=jnp.float32
    ).astype(jnp.bfloat16)
    received = lax.all_to_all(sending, "ep", split_axis=0, concat_axis=0, tiled=True)
    my_docs = lax.dynamic_index_in_dim(query_docs, device, 0, keepdims=False)
    from_dev = jnp.arange(received.shape[0], dtype=jnp.int32)
    pick_dev = ((my_docs // pool_dev)[:, None] == from_dev[None, :]).astype(jnp.bfloat16)
    context = jnp.einsum(
        "jr,rkc->jkc", pick_dev, received, preferred_element_type=jnp.float32
    ).astype(jnp.bfloat16)
    every_doc = jnp.arange(doc_lens.shape[0], dtype=jnp.int32)
    lengths = jnp.sum(
        jnp.where(my_docs[:, None] == every_doc[None, :], doc_lens[None, :], 0), axis=1
    )
    positions = jnp.repeat(row_pos[:docs_per], doc_max, total_repeat_length=docs_per * doc_max)
    keys = rotate(context[:, :, :head_dim].reshape(docs_per * doc_max, head_dim), positions).astype(
        jnp.bfloat16
    )
    values = context[:, :, head_dim:].reshape(docs_per * doc_max, head_dim)
    valid = (jnp.arange(doc_max, dtype=jnp.int32)[None, :] < lengths[:, None]).reshape(
        docs_per * doc_max
    )
    return (keys, values, valid)


def project(attended, out_proj):
    lanes = lax.axis_size("tp")
    groups = lax.axis_size("ep")
    length = attended.shape[0]
    if lanes == groups:
        swap = [(e * lanes + t, t * lanes + e) for e in range(groups) for t in range(lanes)]
        block = lax.ppermute(attended, ("ep", "tp"), swap)
        tokens = lax.all_gather(block, "tp", axis=0, tiled=True)
    else:
        all_heads = lax.all_gather(attended, "tp", axis=1, tiled=True)
        split = jnp.swapaxes(all_heads.reshape(length, groups, -1), 0, 1)
        tokens = lax.all_to_all(split, "ep", split_axis=0, concat_axis=0, tiled=True)
        tokens = tokens.reshape(groups * length, -1)
    part = jnp.dot(tokens, out_proj, preferred_element_type=jnp.float32)
    summed = lax.psum_scatter(
        part.astype(jnp.bfloat16), "ep", scatter_dimension=0, tiled=True
    ).astype(jnp.float32)
    return summed


MESH = pl.DeviceIdType.MESH


def when(condition):
    return pl.when(condition)


def near_order(z, rank):
    base = lambda p: jnp.where(rank == 0, p, jnp.where(rank == 1, 1 - p, rank))
    return jnp.where(z < 2, base(z), 3 - base(3 - z))


def unit_of(z, count, u):
    units = 4 * count
    v = lax.rem(u + (units - count // 2), units)
    rank = lax.rem(v // count + 1, 4)
    return rank, near_order(z, rank), lax.rem(v, count)


def experts_kernel(
    normed, routes, resid, wgu_hbm, wd_hbm, out,
    stage, w_gate, w_up, w_down, blocks, seats, sent, first, pair, second, acts,
    total, leaving, coming,
    stage_sem, down_sem, ag_send, ag_recv, tp_send, tp_recv, rs_send, rs_recv,
):
    count, width = w_down.shape[:2]
    length = normed.shape[0]
    cap = sent.shape[3]
    quarter = acts.shape[4]
    units = 4 * count
    bf16 = jnp.bfloat16
    f32 = jnp.float32
    z = lax.axis_index("ep")
    lane = lax.axis_index("tp")
    chip = lane // 2
    core = lane % 2
    partner = chip * 2 + (1 - core)
    across = (1 - chip) * 2 + core

    def load_in(u):
        _, _, j = unit_of(z, count, u)
        return pltpu.make_async_copy(wgu_hbm.at[j], stage.at[u % 2], stage_sem.at[u % 2])

    def load_down(j):
        return pltpu.make_async_copy(wd_hbm.at[j], w_down.at[j], down_sem.at[j])

    load_in(0).start()
    load_in(1).start()
    for j in range(count):
        load_down(j).start()

    barrier = pltpu.get_barrier_semaphore()
    for other in (partner, across):
        pl.semaphore_signal(barrier, inc=1, device_id={"tp": other}, device_id_type=MESH)
    for k in range(1, 4):
        pl.semaphore_signal(
            barrier, inc=1, device_id={"ep": lax.rem(z + k, 4)}, device_id_type=MESH
        )
    blocks[z] = normed[...]
    seats[z] = routes[z]
    total[...] = jnp.zeros_like(total)
    pl.semaphore_wait(barrier, 5)

    def gather_copies(dest, source):
        return [
            pltpu.make_async_remote_copy(
                src_ref=normed,
                dst_ref=blocks.at[source],
                send_sem=ag_send.at[0, dest],
                recv_sem=ag_recv.at[0, source],
                device_id={"ep": dest},
                device_id_type=MESH,
            ),
            pltpu.make_async_remote_copy(
                src_ref=routes.at[dest],
                dst_ref=seats.at[source],
                send_sem=ag_send.at[1, dest],
                recv_sem=ag_recv.at[1, source],
                device_id={"ep": dest},
                device_id_type=MESH,
            ),
        ]

    def spread(distance):
        for off in (-distance, distance):
            dest = z + off

            @when((dest >= 0) & (dest < 4))
            def _():
                for copy in gather_copies(dest, z):
                    copy.start()

    spread(1)

    def remote(kind, u, source, target, other):
        return pltpu.make_async_remote_copy(
            src_ref=source,
            dst_ref=target,
            send_sem=tp_send.at[kind, u],
            recv_sem=tp_recv.at[kind, u],
            device_id={"tp": other},
            device_id_type=MESH,
        )

    def tp_copies(u):
        return [
            remote(0, u, sent.at[u, 1 - core], first.at[u], partner),
            remote(1, u, pair.at[u], second.at[u], across),
            remote(2, u, acts.at[u, core, chip], acts.at[u, core, chip], across),
            remote(3, u, acts.at[u, core, chip], acts.at[u, core, chip], partner),
            remote(4, u, acts.at[u, core, 1 - chip], acts.at[u, core, 1 - chip], partner),
        ]

    def back_copy(rank, source):
        return pltpu.make_async_remote_copy(
            src_ref=leaving.at[rank],
            dst_ref=coming.at[z],
            send_sem=rs_send.at[rank],
            recv_sem=rs_recv.at[z],
            device_id={"ep": source},
            device_id_type=MESH,
        )

    def arrival(source):
        return pltpu.make_async_remote_copy(
            src_ref=leaving.at[0],
            dst_ref=coming.at[source],
            send_sem=rs_send.at[0],
            recv_sem=rs_recv.at[source],
            device_id={"ep": source},
            device_id_type=MESH,
        )

    def row_of(source, row):
        table = seats[source].astype(f32)
        rows = lax.broadcasted_iota(jnp.int32, table.shape, 0)
        return jnp.sum(jnp.where(rows == row, table, 0.0), axis=0, keepdims=True)

    places = lax.broadcasted_iota(jnp.int32, (cap, length), 0).astype(f32)

    def multiply_in(u):
        rank, source, j = unit_of(z, count, u)

        @when(u < count)
        def _():
            load_in(u).wait()
            step = width // 8

            def relay(i, carry):
                rows = pl.ds(pl.multiple_of(i * step, step), step)
                block = jnp.transpose(stage[u % 2, rows], (1, 0, 2))
                w_gate[j, rows, :] = block[0]
                w_up[j, rows, :] = block[1]
                return carry

            lax.fori_loop(0, 8, relay, 0)

            @when(u + 2 < count)
            def _():
                load_in(u + 2).start()

        @when((rank > 0) & (j == 0))
        def _():
            for copy in gather_copies(source, source):
                copy.wait_recv()

        pick = (places == row_of(source, j)).astype(bf16)
        rows = jnp.dot(pick, blocks[source], preferred_element_type=f32).astype(bf16)
        for kind, weights in enumerate((w_gate, w_up)):
            part = jnp.dot(rows, weights[j], preferred_element_type=f32).astype(bf16)
            for q in range(4):
                sent[u, q % 2, q // 2, :, kind * quarter : (kind + 1) * quarter] = part[
                    :, q * quarter : (q + 1) * quarter
                ]
        tp_copies(u)[0].start()

    def add_pair(u):
        copies = tp_copies(u)
        copies[0].wait_recv()
        both = sent[u, core, 1 - chip].astype(f32) + first[u, 1 - chip].astype(f32)
        pair[u] = both.astype(bf16)
        copies[1].start()

    def activate(u):
        copies = tp_copies(u)
        copies[1].wait_recv()
        value = (
            sent[u, core, chip].astype(f32)
            + first[u, chip].astype(f32)
            + second[u].astype(f32)
        )
        gate = value[:, :quarter]
        acts[u, core, chip] = (gate / (1.0 + jnp.exp(-gate)) * value[:, quarter:]).astype(bf16)
        copies[2].start()
        copies[3].start()

    def forward(u):
        copies = tp_copies(u)
        copies[2].wait_recv()
        copies[4].start()

    def multiply_out(u):
        rank, source, j = unit_of(z, count, u)
        copies = tp_copies(u)
        copies[3].wait_recv()
        copies[4].wait_recv()

        @when(u < count)
        def _():
            load_down(j).wait()

        joined = jnp.concatenate([acts[u, q % 2, q // 2] for q in range(4)], axis=1)
        result = jnp.dot(joined, w_down[j], preferred_element_type=f32).astype(bf16)
        share = jnp.where(
            places == row_of(source, j), row_of(source, count + j), 0.0
        ).astype(bf16)
        total[source] += lax.dot_general(
            share, result, (((0,), (0,)), ((), ())), preferred_element_type=f32
        )

        @when((rank > 0) & (j == count - 1))
        def _():
            leaving[rank] = total[source].astype(bf16)
            back_copy(rank, source).start()

    def tick(i, carry):
        @when(i == 2)
        def _():
            spread(2)

        @when(i == 5)
        def _():
            spread(3)

        for stage_of, delay in (
            (multiply_in, 0), (activate, 2), (forward, 3), (multiply_out, 4), (add_pair, 0),
        ):
            @when((i >= delay) & (i < units + delay))
            def _():
                stage_of(i - delay)

        return carry

    lax.fori_loop(0, units + 4, tick, 0)

    answer = resid[...].astype(f32) + total[z]
    for k in range(1, 4):
        source = lax.rem(z + k, 4)
        arrival(source).wait_recv()
        answer = answer + coming[source].astype(f32)
    out[...] = answer.astype(bf16)

    def settle(u, carry):
        for copy in tp_copies(u):
            copy.wait_send()
        return carry

    lax.fori_loop(0, units, settle, 0)
    for k in range(1, 4):
        other = lax.rem(z + k, 4)
        for copy in gather_copies(other, z):
            copy.wait_send()
        back_copy(k, other).wait_send()


def fused_experts(normed, chosen, mix, residual, w_gate_up, w_down, capacity):
    length, width = normed.shape
    count = w_gate_up.shape[0]
    hidden = w_gate_up.shape[3]
    experts = chosen.shape[1]
    bf16 = jnp.bfloat16
    earlier = (jnp.arange(length)[:, None] < jnp.arange(length)[None, :]).astype(bf16)
    chosen_t = jnp.swapaxes(chosen, 0, 1)
    rank = jnp.dot(chosen_t.astype(bf16), earlier, preferred_element_type=jnp.float32)
    seat = jnp.where(chosen_t, rank, -1.0)
    routes = jnp.concatenate(
        [
            seat.reshape(4, count, length),
            jnp.swapaxes(mix, 0, 1).reshape(4, count, length),
            jnp.zeros((4, 16 - 2 * count, length), jnp.float32),
        ],
        axis=1,
    ).astype(bf16)
    units = 4 * count
    quarter = hidden // 4
    vmem = pl.BlockSpec(memory_space=pltpu.VMEM)
    anywhere = pl.BlockSpec(memory_space=pl.ANY)
    dma = pltpu.SemaphoreType.DMA
    return pl.pallas_call(
        experts_kernel,
        out_shape=jax.ShapeDtypeStruct((length, width), bf16),
        in_specs=[vmem, vmem, vmem, anywhere, anywhere],
        out_specs=vmem,
        scratch_shapes=[
            pltpu.VMEM((2,) + w_gate_up.shape[1:], bf16),
            pltpu.VMEM((count, width, hidden), bf16),
            pltpu.VMEM((count, width, hidden), bf16),
            pltpu.VMEM(w_down.shape, bf16),
            pltpu.VMEM((4, length, width), bf16),
            pltpu.VMEM((4, 16, length), bf16),
            pltpu.VMEM((units, 2, 2, capacity, 2 * quarter), bf16),
            pltpu.VMEM((units, 2, capacity, 2 * quarter), bf16),
            pltpu.VMEM((units, capacity, 2 * quarter), bf16),
            pltpu.VMEM((units, capacity, 2 * quarter), bf16),
            pltpu.VMEM((units, 2, 2, capacity, quarter), bf16),
            pltpu.VMEM((4, length, width), jnp.float32),
            pltpu.VMEM((4, length, width), bf16),
            pltpu.VMEM((4, length, width), bf16),
            dma((2,)),
            dma((count,)),
            dma((2, 4)),
            dma((2, 4)),
            dma((5, units)),
            dma((5, units)),
            dma((4,)),
            dma((4,)),
        ],
        compiler_params=pltpu.CompilerParams(
            collective_id=1, has_side_effects=True, vmem_limit_bytes=58 << 20
        ),
    )(normed, routes, residual.astype(bf16), w_gate_up, w_down)


def feed_forward(arrived, w_gate_up, w_down):
    term = jnp.einsum("erd,edgh->hegr", arrived, w_gate_up, preferred_element_type=jnp.float32)
    summed = lax.psum_scatter(
        term.astype(jnp.bfloat16), "tp", scatter_dimension=0, tiled=True
    ).astype(jnp.float32)
    activated = (jax.nn.silu(summed[:, :, 0]) * summed[:, :, 1]).astype(jnp.bfloat16)
    piece = lax.all_gather(activated, "tp", axis=0, tiled=True)
    return jnp.einsum(
        "her,ehd->erd", piece, w_down, preferred_element_type=jnp.float32
    ).astype(jnp.bfloat16)


def per_device(
    question_q,
    question_kv,
    doc_kv,
    doc_lens,
    query_docs,
    ctx_pos,
    hidden,
    out_proj,
    norm_gain,
    router_weight,
    w_gate_up,
    w_down,
    expert_ids,
):
    lanes = lax.axis_size("tp")
    groups = lax.axis_size("ep")
    lane = lax.axis_index("tp")
    device = lax.axis_index("ep")
    length, heads_here, head_dim = question_q.shape
    kv_heads = question_kv.shape[1]
    kv_pick = lane * kv_heads // lanes
    scale = head_dim ** (-0.5)
    docs_per = query_docs.shape[1]
    row_pos = lax.dynamic_index_in_dim(ctx_pos, device, 0, keepdims=False)
    question_pos = row_pos[docs_per] + jnp.arange(length, dtype=jnp.int32)
    queries = rotate(question_q, question_pos).astype(jnp.bfloat16)
    own_kv = lax.dynamic_index_in_dim(question_kv, kv_pick, 1, keepdims=False)
    own_keys = rotate(own_kv[:, 0], question_pos).astype(jnp.bfloat16)
    own_values = own_kv[:, 1]
    causal = jnp.arange(length)[:, None] >= jnp.arange(length)[None, :]
    doc_keys, doc_values, valid = fetch_context(
        doc_kv, doc_lens, query_docs, row_pos, device, kv_pick
    )
    keys = jnp.concatenate([doc_keys, own_keys], axis=0)
    values = jnp.concatenate([doc_values, own_values], axis=0)
    allowed = jnp.concatenate(
        [jnp.broadcast_to(valid[None, :], (length, valid.shape[0])), causal], axis=1
    )
    scores = jnp.einsum("ihd,jd->hij", queries, keys, preferred_element_type=jnp.float32) * scale
    scores = jnp.where(allowed[None], scores, -jnp.inf)
    ceiling = jnp.max(scores, axis=-1, keepdims=True)
    probs = jnp.exp(scores - ceiling)
    denominator = jnp.sum(probs, axis=-1, keepdims=True)
    mixed = jnp.einsum(
        "hij,jd->hid", probs.astype(jnp.bfloat16), values, preferred_element_type=jnp.float32
    )
    attended = (
        jnp.transpose(mixed / denominator, (1, 0, 2))
        .reshape(length, heads_here * head_dim)
        .astype(jnp.bfloat16)
    )
    width_here = hidden.shape[1]
    projected = project(attended, out_proj)
    residual_wide = narrow(hidden.astype(jnp.float32) + projected).astype(jnp.float32)
    gain = norm_gain.astype(jnp.float32)
    squares, logit_part = lax.psum(
        (
            jnp.sum(residual_wide * residual_wide, axis=1),
            jnp.dot(
                residual_wide * gain[None, :],
                router_weight.astype(jnp.float32),
                precision=lax.Precision.HIGHEST,
            ),
        ),
        "tp",
    )
    inv_rms = lax.rsqrt(squares / D + norm_eps)
    normed = (residual_wide * inv_rms[:, None] * gain[None, :]).astype(jnp.bfloat16)
    logits = logit_part * inv_rms[:, None]
    local_experts = w_gate_up.shape[0]
    capacity = length * expert_ids.shape[1] // (local_experts * groups)
    experts = logits.shape[1]
    chosen = jnp.any(expert_ids[:, :, None] == jnp.arange(experts, dtype=jnp.int32), axis=1)
    top = jnp.max(jnp.where(chosen, logits, -jnp.inf), axis=1, keepdims=True)
    raised = jnp.where(chosen, jnp.exp(jnp.where(chosen, logits - top, 0.0)), 0.0)
    mix = raised / jnp.sum(raised, axis=1, keepdims=True)
    if lanes == 4 and groups == 4:
        return fused_experts(normed, chosen, mix, residual_wide, w_gate_up, w_down, capacity)
    mix_high = mix.astype(jnp.bfloat16)
    mix_low = (mix - mix_high.astype(jnp.float32)).astype(jnp.bfloat16)
    notes = jnp.concatenate([chosen.astype(jnp.bfloat16), mix_high, mix_low], axis=1)
    notes = jnp.pad(notes, ((0, 0), (0, -notes.shape[1] % 128)))
    packed = lax.all_gather(jnp.concatenate([normed, notes], axis=1), "ep", axis=0)
    normed_all = packed[:, :, :width_here]

    def mine(index):
        start = width_here + index * experts + device * local_experts
        return lax.dynamic_slice_in_dim(packed, start, local_experts, axis=2)

    member = mine(0) > 0
    share_high = jnp.swapaxes(mine(1), 1, 2)
    share_low = jnp.swapaxes(mine(2), 1, 2)
    earlier = jnp.arange(length)[:, None] > jnp.arange(length)[None, :]
    rank = jnp.einsum(
        "nm,sme->sen",
        earlier.astype(jnp.bfloat16),
        member.astype(jnp.bfloat16),
        preferred_element_type=jnp.float32,
    )
    seat = jnp.where(jnp.swapaxes(member, 1, 2), rank.astype(jnp.int32), -1)
    picks = (seat[:, :, None, :] == jnp.arange(capacity, dtype=jnp.int32)[:, None]).astype(
        jnp.bfloat16
    )
    arrived = jnp.einsum(
        "secn,snd->escd", picks, normed_all, preferred_element_type=jnp.float32
    ).astype(jnp.bfloat16)
    rows = groups * capacity
    arrived = arrived.reshape(local_experts, rows, width_here)
    expert_out = feed_forward(arrived, w_gate_up, w_down)
    weights = jnp.stack([picks * share_high[:, :, None, :], picks * share_low[:, :, None, :]])
    partial = jnp.einsum(
        "psecn,escd->snd",
        weights,
        expert_out.reshape(local_experts, groups, capacity, width_here),
        preferred_element_type=jnp.float32,
    )
    combined = lax.psum_scatter(
        partial.astype(jnp.bfloat16).reshape(groups * length, width_here),
        "ep",
        scatter_dimension=0,
        tiled=True,
    )
    return (residual_wide + combined.astype(jnp.float32)).astype(jnp.bfloat16)


def solution(mesh):
    placed = (
        P(("grp", "ep"), "tp", None),
        P(("grp", "ep"), None, None, None),
        P(("grp", "ep"), None, None, None, None),
        P("grp"),
        P("grp", None),
        P("grp", None),
        P(("grp", "ep"), "tp"),
        P("ep", "tp"),
        P("tp"),
        P("tp", None),
        P("ep", "tp", None, None),
        P("ep", None, "tp"),
        P(("grp", "ep"), None),
    )
    return jax.shard_map(
        per_device, mesh=mesh, in_specs=placed, out_specs=P(("grp", "ep"), "tp"), check_vma=False
    )
```

```python
import math

import jax
import jax.numpy as jnp
from jax import lax
from jax.experimental import pallas as pl
from jax.experimental.pallas import tpu as pltpu
from jax.sharding import PartitionSpec as P

D = 4096
HID = 1024


rope_theta = 1000000.0
norm_eps = 1e-06


def narrow(values):
    return lax.optimization_barrier(values.astype(jnp.bfloat16))


def rotate(values, positions):
    half = values.shape[-1] // 2
    freq = jnp.exp(
        jnp.arange(half, dtype=jnp.float32) * (-2.0 * math.log(rope_theta) / values.shape[-1])
    )
    angle = positions.astype(jnp.float32)[:, None] * freq[None, :]
    shape = (values.shape[0],) + (1,) * (values.ndim - 2) + (half,)
    cosine = jnp.cos(angle).reshape(shape)
    sine = jnp.sin(angle).reshape(shape)
    floats = values.astype(jnp.float32)
    first = floats[..., :half]
    second = floats[..., half:]
    return jnp.concatenate(
        [first * cosine - second * sine, second * cosine + first * sine], axis=-1
    )


def fetch_context(doc_kv, doc_lens, query_docs, row_pos, device, kv_pick):
    pool_dev, doc_max, kv_heads, pair, head_dim = doc_kv.shape
    docs_per = query_docs.shape[1]
    pool_head = lax.dynamic_index_in_dim(doc_kv, kv_pick, 2, keepdims=False).reshape(
        pool_dev, doc_max, pair * head_dim
    )
    held = device * pool_dev + jnp.arange(pool_dev, dtype=jnp.int32)
    wanted = jnp.sum((query_docs[:, :, None] == held[None, None, :]).astype(jnp.float32), axis=1)
    sending = jnp.einsum(
        "rl,lkc->rkc", wanted.astype(jnp.bfloat16), pool_head, preferred_element_type=jnp.float32
    ).astype(jnp.bfloat16)
    received = lax.all_to_all(sending, "ep", split_axis=0, concat_axis=0, tiled=True)
    my_docs = lax.dynamic_index_in_dim(query_docs, device, 0, keepdims=False)
    from_dev = jnp.arange(received.shape[0], dtype=jnp.int32)
    pick_dev = ((my_docs // pool_dev)[:, None] == from_dev[None, :]).astype(jnp.bfloat16)
    context = jnp.einsum(
        "jr,rkc->jkc", pick_dev, received, preferred_element_type=jnp.float32
    ).astype(jnp.bfloat16)
    every_doc = jnp.arange(doc_lens.shape[0], dtype=jnp.int32)
    lengths = jnp.sum(
        jnp.where(my_docs[:, None] == every_doc[None, :], doc_lens[None, :], 0), axis=1
    )
    positions = jnp.repeat(row_pos[:docs_per], doc_max, total_repeat_length=docs_per * doc_max)
    keys = rotate(context[:, :, :head_dim].reshape(docs_per * doc_max, head_dim), positions).astype(
        jnp.bfloat16
    )
    values = context[:, :, head_dim:].reshape(docs_per * doc_max, head_dim)
    valid = (jnp.arange(doc_max, dtype=jnp.int32)[None, :] < lengths[:, None]).reshape(
        docs_per * doc_max
    )
    return (keys, values, valid)


def project(attended, out_proj):
    lanes = lax.axis_size("tp")
    groups = lax.axis_size("ep")
    length = attended.shape[0]
    if lanes == groups:
        swap = [(e * lanes + t, t * lanes + e) for e in range(groups) for t in range(lanes)]
        block = lax.ppermute(attended, ("ep", "tp"), swap)
        tokens = lax.all_gather(block, "tp", axis=0, tiled=True)
    else:
        all_heads = lax.all_gather(attended, "tp", axis=1, tiled=True)
        split = jnp.swapaxes(all_heads.reshape(length, groups, -1), 0, 1)
        tokens = lax.all_to_all(split, "ep", split_axis=0, concat_axis=0, tiled=True)
        tokens = tokens.reshape(groups * length, -1)
    part = jnp.dot(tokens, out_proj, preferred_element_type=jnp.float32)
    summed = lax.psum_scatter(
        part.astype(jnp.bfloat16), "ep", scatter_dimension=0, tiled=True
    ).astype(jnp.float32)
    return summed


MESH = pl.DeviceIdType.MESH


def when(condition):
    return pl.when(condition)


def near_order(z, rank):
    base = lambda p: jnp.where(rank == 0, p, jnp.where(rank == 1, 1 - p, rank))
    return jnp.where(z < 2, base(z), 3 - base(3 - z))


def unit_of(z, count, u):
    units = 4 * count
    v = lax.rem(u + (units - count // 2), units)
    rank = lax.rem(v // count + 1, 4)
    return rank, near_order(z, rank), lax.rem(v, count)


def experts_kernel(
    normed, routes, resid, wgu_hbm, wd_hbm, out,
    stage, w_gate, w_up, w_down, blocks, seats, sent, first, pair, second, acts,
    total, leaving, coming,
    stage_sem, down_sem, ag_send, ag_recv, tp_send, tp_recv, rs_send, rs_recv,
):
    count, width = w_down.shape[:2]
    length = normed.shape[0]
    cap = sent.shape[3]
    quarter = acts.shape[4]
    units = 4 * count
    bf16 = jnp.bfloat16
    f32 = jnp.float32
    z = lax.axis_index("ep")
    lane = lax.axis_index("tp")
    chip = lane // 2
    core = lane % 2
    partner = chip * 2 + (1 - core)
    across = (1 - chip) * 2 + core

    def load_in(u):
        _, _, j = unit_of(z, count, u)
        return pltpu.make_async_copy(wgu_hbm.at[j], stage.at[u % 2], stage_sem.at[u % 2])

    def load_down(j):
        return pltpu.make_async_copy(wd_hbm.at[j], w_down.at[j], down_sem.at[j])

    load_in(0).start()
    load_in(1).start()
    for j in range(count):
        load_down(j).start()

    barrier = pltpu.get_barrier_semaphore()
    for other in (partner, across):
        pl.semaphore_signal(barrier, inc=1, device_id={"tp": other}, device_id_type=MESH)
    for k in range(1, 4):
        pl.semaphore_signal(
            barrier, inc=1, device_id={"ep": lax.rem(z + k, 4)}, device_id_type=MESH
        )
    blocks[z] = normed[...]
    seats[z] = routes[z]
    total[...] = jnp.zeros_like(total)
    pl.semaphore_wait(barrier, 5)

    def gather_copies(dest, source):
        return [
            pltpu.make_async_remote_copy(
                src_ref=normed,
                dst_ref=blocks.at[source],
                send_sem=ag_send.at[0, dest],
                recv_sem=ag_recv.at[0, source],
                device_id={"ep": dest},
                device_id_type=MESH,
            ),
            pltpu.make_async_remote_copy(
                src_ref=routes.at[dest],
                dst_ref=seats.at[source],
                send_sem=ag_send.at[1, dest],
                recv_sem=ag_recv.at[1, source],
                device_id={"ep": dest},
                device_id_type=MESH,
            ),
        ]

    def spread(distance):
        for off in (-distance, distance):
            dest = z + off

            @when((dest >= 0) & (dest < 4))
            def _():
                for copy in gather_copies(dest, z):
                    copy.start()

    spread(1)

    def remote(kind, u, source, target, other):
        return pltpu.make_async_remote_copy(
            src_ref=source,
            dst_ref=target,
            send_sem=tp_send.at[kind, u],
            recv_sem=tp_recv.at[kind, u],
            device_id={"tp": other},
            device_id_type=MESH,
        )

    def tp_copies(u):
        return [
            remote(0, u, sent.at[u, 1 - core], first.at[u], partner),
            remote(1, u, pair.at[u], second.at[u], across),
            remote(2, u, acts.at[u, core, chip], acts.at[u, core, chip], across),
            remote(3, u, acts.at[u, core, chip], acts.at[u, core, chip], partner),
            remote(4, u, acts.at[u, core, 1 - chip], acts.at[u, core, 1 - chip], partner),
        ]

    def back_copy(rank, source):
        return pltpu.make_async_remote_copy(
            src_ref=leaving.at[rank],
            dst_ref=coming.at[z],
            send_sem=rs_send.at[rank],
            recv_sem=rs_recv.at[z],
            device_id={"ep": source},
            device_id_type=MESH,
        )

    def arrival(source):
        return pltpu.make_async_remote_copy(
            src_ref=leaving.at[0],
            dst_ref=coming.at[source],
            send_sem=rs_send.at[0],
            recv_sem=rs_recv.at[source],
            device_id={"ep": source},
            device_id_type=MESH,
        )

    def row_of(source, row):
        table = seats[source].astype(f32)
        rows = lax.broadcasted_iota(jnp.int32, table.shape, 0)
        return jnp.sum(jnp.where(rows == row, table, 0.0), axis=0, keepdims=True)

    places = lax.broadcasted_iota(jnp.int32, (cap, length), 0).astype(f32)

    def multiply_in(u):
        rank, source, j = unit_of(z, count, u)

        @when(u < count)
        def _():
            load_in(u).wait()
            step = width // 8

            def relay(i, carry):
                rows = pl.ds(pl.multiple_of(i * step, step), step)
                block = jnp.transpose(stage[u % 2, rows], (1, 0, 2))
                w_gate[j, rows, :] = block[0]
                w_up[j, rows, :] = block[1]
                return carry

            lax.fori_loop(0, 8, relay, 0)

            @when(u + 2 < count)
            def _():
                load_in(u + 2).start()

        @when((rank > 0) & (j == 0))
        def _():
            for copy in gather_copies(source, source):
                copy.wait_recv()

        pick = (places == row_of(source, j)).astype(bf16)
        rows = jnp.dot(pick, blocks[source], preferred_element_type=f32).astype(bf16)
        for kind, weights in enumerate((w_gate, w_up)):
            part = jnp.dot(rows, weights[j], preferred_element_type=f32).astype(bf16)
            for q in range(4):
                sent[u, q % 2, q // 2, :, kind * quarter : (kind + 1) * quarter] = part[
                    :, q * quarter : (q + 1) * quarter
                ]
        tp_copies(u)[0].start()

    def add_pair(u):
        copies = tp_copies(u)
        copies[0].wait_recv()
        both = sent[u, core, 1 - chip].astype(f32) + first[u, 1 - chip].astype(f32)
        pair[u] = both.astype(bf16)
        copies[1].start()

    def activate(u):
        copies = tp_copies(u)
        copies[1].wait_recv()
        value = (
            sent[u, core, chip].astype(f32)
            + first[u, chip].astype(f32)
            + second[u].astype(f32)
        )
        gate = value[:, :quarter]
        acts[u, core, chip] = (gate / (1.0 + jnp.exp(-gate)) * value[:, quarter:]).astype(bf16)
        copies[2].start()
        copies[3].start()

    def forward(u):
        copies = tp_copies(u)
        copies[2].wait_recv()
        copies[4].start()

    def multiply_out(u):
        rank, source, j = unit_of(z, count, u)
        copies = tp_copies(u)
        copies[3].wait_recv()
        copies[4].wait_recv()

        @when(u < count)
        def _():
            load_down(j).wait()

        joined = jnp.concatenate([acts[u, q % 2, q // 2] for q in range(4)], axis=1)
        result = jnp.dot(joined, w_down[j], preferred_element_type=f32).astype(bf16)
        share = jnp.where(
            places == row_of(source, j), row_of(source, count + j), 0.0
        ).astype(bf16)
        total[source] += lax.dot_general(
            share, result, (((0,), (0,)), ((), ())), preferred_element_type=f32
        )

        @when((rank > 0) & (j == count - 1))
        def _():
            leaving[rank] = total[source].astype(bf16)
            back_copy(rank, source).start()

    def tick(i, carry):
        @when(i == 2)
        def _():
            spread(2)

        @when(i == 5)
        def _():
            spread(3)

        for stage_of, delay in (
            (multiply_in, 0), (activate, 2), (forward, 3), (multiply_out, 4), (add_pair, 0),
        ):
            @when((i >= delay) & (i < units + delay))
            def _():
                stage_of(i - delay)

        return carry

    lax.fori_loop(0, units + 4, tick, 0)

    answer = resid[...].astype(f32) + total[z]
    for k in range(1, 4):
        source = lax.rem(z + k, 4)
        arrival(source).wait_recv()
        answer = answer + coming[source].astype(f32)
    out[...] = answer.astype(bf16)

    def settle(u, carry):
        for copy in tp_copies(u):
            copy.wait_send()
        return carry

    lax.fori_loop(0, units, settle, 0)
    for k in range(1, 4):
        other = lax.rem(z + k, 4)
        for copy in gather_copies(other, z):
            copy.wait_send()
        back_copy(k, other).wait_send()


def halves_turn(index):
    return 2 * lax.rem(index, 2) + index // 2


def context_kernel(
    q, own_kv, docs, rope, notes, hidden, gain, router, ids, wo_hbm,
    resid, normed, routes,
    wo, sending, context, queries, keys, values, own_att, att, parts,
    go_up, go_down, from_below, from_above, sums,
    wo_sem, doc_send, doc_recv, swap_send, swap_recv, tp_send, tp_recv,
    up_send, up_recv, down_send, down_recv, sum_send, sum_recv,
):
    bf16 = jnp.bfloat16
    f32 = jnp.float32
    z = lax.axis_index("ep")
    lane = lax.axis_index("tp")
    chip = lane // 2
    core = lane % 2
    partner = chip * 2 + (1 - core)
    across = (1 - chip) * 2 + core
    length = hidden.shape[0]
    width = hidden.shape[1]
    heads = q.shape[1]
    head_dim = q.shape[2]
    features = width * 4
    some = heads // 2

    load_wo = pltpu.make_async_copy(wo_hbm, wo, wo_sem)
    load_wo.start()

    swap_to = {"ep": lane, "tp": halves_turn(z)}
    swap_from = {"ep": halves_turn(lane), "tp": z}
    moves = (lane != z) | (halves_turn(z) != lane)
    barrier = pltpu.get_barrier_semaphore()
    for k in range(1, 4):
        for axis, here in (("ep", z), ("tp", lane)):
            pl.semaphore_signal(
                barrier, inc=1, device_id={axis: lax.rem(here + k, 4)}, device_id_type=MESH
            )

    @when(moves)
    def _():
        for other in (swap_to, swap_from):
            pl.semaphore_signal(barrier, inc=1, device_id=other, device_id_type=MESH)

    found = []
    for l in range(2):
        block = jnp.transpose(docs[l, :, lane], (1, 0, 2)).astype(f32)
        found.append(block)
    for r in range(4):
        chosen = found[0] * notes[4 + 2 * r : 5 + 2 * r][None] + (
            found[1] * notes[5 + 2 * r : 6 + 2 * r][None]
        )
        sending[r] = chosen.astype(bf16)

    pl.semaphore_wait(barrier, jnp.where(moves, 8, 6))

    def doc_copy(dest, source):
        return pltpu.make_async_remote_copy(
            src_ref=sending.at[dest],
            dst_ref=context.at[source],
            send_sem=doc_send.at[dest],
            recv_sem=doc_recv.at[source],
            device_id={"ep": dest},
            device_id_type=MESH,
        )

    for k in range(1, 4):
        doc_copy(lax.rem(z + k, 4), z).start()
    context[z] = sending[z]

    def rotate_rows(rows, cosine, sine):
        return (rows * cosine + pltpu.roll(rows, head_dim // 2, 1) * sine).astype(bf16)

    turned = jnp.transpose(q[...], (1, 0, 2))
    for h in range(heads):
        queries[h] = rotate_rows(turned[h].astype(f32), rope[0, :length], rope[1, :length])
    own = jnp.transpose(own_kv[:, lane], (1, 0, 2))
    last = pl.ds(4 * length, length)
    keys[last, :] = rotate_rows(own[0].astype(f32), rope[0, :length], rope[1, :length])
    values[last, :] = own[1]

    experts = router.shape[0]
    count = experts // 4
    expert = lax.broadcasted_iota(jnp.int32, (experts, length), 0)
    picked = jnp.zeros((experts, length), f32)
    for k in range(ids.shape[0]):
        picked = picked + jnp.where(ids[k : k + 1, :] == expert, 1.0, 0.0)
    before = (
        lax.broadcasted_iota(jnp.int32, (length, length), 0)
        < lax.broadcasted_iota(jnp.int32, (length, length), 1)
    )
    rank = jnp.dot(
        picked.astype(bf16),
        jnp.where(before, 1.0, 0.0).astype(bf16),
        preferred_element_type=f32,
    )
    seat = jnp.where(picked > 0.0, rank, -1.0)

    for k in range(1, 4):
        source = lax.rem(z + k, 4)
        doc_copy(source, source).wait_recv()
    for s in range(4):
        row = pl.ds(s * length, length)
        keys[row, :] = rotate_rows(
            context[s, 0].astype(f32),
            rope[0, length + s : length + s + 1],
            rope[1, length + s : length + s + 1],
        )
        values[row, :] = context[s, 1]

    column = lax.broadcasted_iota(jnp.int32, (length, length), 1)
    line = lax.broadcasted_iota(jnp.int32, (length, length), 0)
    scale = head_dim ** (-0.5)

    def swap_copy(c, query):
        return pltpu.make_async_remote_copy(
            src_ref=own_att.at[c],
            dst_ref=att.at[query, c],
            send_sem=swap_send.at[c],
            recv_sem=swap_recv.at[c],
            device_id=swap_to,
            device_id_type=MESH,
        )

    allowed = [
        jnp.where(column.astype(f32) < notes[s : s + 1], 0.0, -jnp.inf) for s in range(4)
    ] + [jnp.where(column <= line, 0.0, -jnp.inf)]
    bias = jnp.concatenate(allowed, axis=1)

    def one_head(c, h):
        scores = lax.dot_general(
            queries[c * some + h], keys[...], (((1,), (1,)), ((), ())),
            preferred_element_type=f32,
        )
        scores = scores * scale + bias
        ceiling = jnp.max(scores, axis=1, keepdims=True)
        probs = jnp.exp(scores - ceiling)
        denominator = jnp.sum(probs, axis=1, keepdims=True)
        mixed = jnp.dot(probs.astype(bf16), values[...], preferred_element_type=f32)
        own_att[c, h] = (mixed / denominator).astype(bf16)

    for c in range(2):
        def body(h, carry):
            one_head(c, h)
            return carry

        lax.fori_loop(0, some, body, 0)

        @when(moves)
        def _():
            swap_copy(c, z).start()

        @when(jnp.logical_not(moves))
        def _():
            att[z, c] = own_att[c]

    mine = halves_turn(lane)
    theirs = halves_turn(across)

    def tp_copy(kind, c, query, other):
        return pltpu.make_async_remote_copy(
            src_ref=att.at[query, c],
            dst_ref=att.at[query, c],
            send_sem=tp_send.at[kind, c],
            recv_sem=tp_recv.at[kind, c],
            device_id={"tp": other},
            device_id_type=MESH,
        )

    def att_copies(c):
        return [
            tp_copy(0, c, mine, across),
            tp_copy(1, c, mine, partner),
            tp_copy(2, c, theirs, partner),
        ]

    for c in range(2):
        @when(moves)
        def _():
            swap_copy(c, mine).wait_recv()

        att_copies(c)[0].start()
        att_copies(c)[1].start()
    for c in range(2):
        tp_copy(0, c, theirs, across).wait_recv()
        att_copies(c)[2].start()
    load_wo.wait()
    for c in range(2):
        tp_copy(1, c, halves_turn(partner), partner).wait_recv()
        tp_copy(2, c, halves_turn(3 - lane), partner).wait_recv()

    def up_copy(b):
        return pltpu.make_async_remote_copy(
            src_ref=go_up.at[b],
            dst_ref=from_below.at[b],
            send_sem=up_send.at[b],
            recv_sem=up_recv.at[b],
            device_id={"ep": jnp.minimum(z + 1, 3)},
            device_id_type=MESH,
        )

    def down_copy(b):
        return pltpu.make_async_remote_copy(
            src_ref=go_down.at[b],
            dst_ref=from_above.at[b],
            send_sem=down_send.at[b],
            recv_sem=down_recv.at[b],
            device_id={"ep": jnp.maximum(z - 1, 0)},
            device_id_type=MESH,
        )

    def project_block(b):
        rows = jnp.concatenate([att[b, h // some, h % some] for h in range(heads)], axis=1)
        parts[b] = jnp.dot(rows, wo[...], preferred_element_type=f32)

    def send_up(b):
        @when(z == 0)
        def _():
            go_up[b] = parts[b].astype(bf16)

        @when((z > 0) & (z < b))
        def _():
            up_copy(b).wait_recv()
            go_up[b] = (parts[b] + from_below[b].astype(f32)).astype(bf16)

        @when(z < b)
        def _():
            up_copy(b).start()

    def send_down(b):
        @when(z == 3)
        def _():
            go_down[b] = parts[b].astype(bf16)

        @when((z < 3) & (z > b))
        def _():
            down_copy(b).wait_recv()
            go_down[b] = (parts[b] + from_above[b].astype(f32)).astype(bf16)

        @when(z > b)
        def _():
            down_copy(b).start()

    project_block(3)

    @when(z == 0)
    def _():
        send_up(3)

    project_block(0)

    @when(z == 3)
    def _():
        send_down(0)

    project_block(2)
    project_block(1)

    @when(z > 0)
    def _():
        send_up(3)

    @when(z < 3)
    def _():
        send_down(0)

    send_up(2)
    send_down(1)
    send_up(1)
    send_down(2)

    parts[z] += hidden[...].astype(f32)

    @when(z > 0)
    def _():
        up_copy(z).wait_recv()
        parts[z] += from_below[z].astype(f32)

    @when(z < 3)
    def _():
        down_copy(z).wait_recv()
        parts[z] += from_above[z].astype(f32)

    residual = parts[z].astype(bf16)
    resid[...] = residual
    wide = residual.astype(f32)
    gains = gain[...].astype(f32)
    raised = wide * gains
    logit_part = lax.dot_general(
        router[...].astype(f32), raised, (((1,), (1,)), ((), ())),
        precision=lax.Precision.HIGHEST, preferred_element_type=f32,
    )
    square_part = lax.dot_general(
        jnp.ones((8, width), f32), wide * wide, (((1,), (1,)), ((), ())),
        precision=lax.Precision.HIGHEST, preferred_element_type=f32,
    )
    sums[lane] = jnp.concatenate([logit_part, square_part], axis=0)

    def sum_copy(dest, source):
        return pltpu.make_async_remote_copy(
            src_ref=sums.at[source],
            dst_ref=sums.at[source],
            send_sem=sum_send.at[dest],
            recv_sem=sum_recv.at[source],
            device_id={"tp": dest},
            device_id_type=MESH,
        )

    for k in range(1, 4):
        sum_copy(lax.rem(lane + k, 4), lane).start()
    for k in range(1, 4):
        source = lax.rem(lane + k, 4)
        sum_copy(source, source).wait_recv()
    added = (sums[0] + sums[1]) + (sums[2] + sums[3])
    inverse = lax.rsqrt(added[experts : experts + 1] / features + norm_eps)
    logits = added[:experts] * inverse
    inside = picked > 0.0
    top = jnp.max(jnp.where(inside, logits, -jnp.inf), axis=0, keepdims=True)
    lifted = jnp.where(inside, jnp.exp(jnp.where(inside, logits - top, 0.0)), 0.0)
    mix = lifted / jnp.sum(lifted, axis=0, keepdims=True)
    blank = jnp.zeros((16 - 2 * count, length), f32)
    for d in range(4):
        rows = slice(d * count, (d + 1) * count)
        routes[d] = jnp.concatenate([seat[rows], mix[rows], blank], axis=0).astype(bf16)
    tall = jnp.transpose(jnp.broadcast_to(inverse, (length, length)), (1, 0))
    for i in range(width // length):
        part = slice(i * length, (i + 1) * length)
        normed[:, part] = (wide[:, part] * tall * gains[:, part]).astype(bf16)

    for k in range(1, 4):
        doc_copy(lax.rem(z + k, 4), z).wait_send()
        sum_copy(lax.rem(lane + k, 4), lane).wait_send()
    for c in range(2):
        @when(moves)
        def _():
            swap_copy(c, z).wait_send()

        for copy in att_copies(c):
            copy.wait_send()
    for b in range(4):
        @when(z < b)
        def _():
            up_copy(b).wait_send()

        @when(z > b)
        def _():
            down_copy(b).wait_send()


def fused_context(
    question_q, question_kv, doc_kv, doc_lens, query_docs, ctx_pos, hidden, out_proj,
    norm_gain, router_weight, expert_ids,
):
    bf16 = jnp.bfloat16
    f32 = jnp.float32
    device = lax.axis_index("ep")
    length, heads, head_dim = question_q.shape
    width = hidden.shape[1]
    experts = router_weight.shape[1]
    pool_dev = doc_kv.shape[0]
    docs_per = query_docs.shape[1]
    row_pos = lax.dynamic_index_in_dim(ctx_pos, device, 0, keepdims=False)
    my_docs = lax.dynamic_index_in_dim(query_docs, device, 0, keepdims=False)
    blocks = jnp.arange(4, dtype=jnp.int32)
    from_block = (my_docs // pool_dev)[None, :] == blocks[:, None]
    starts = jnp.sum(jnp.where(from_block, row_pos[None, :docs_per], 0), axis=1)
    which = jnp.sum(jnp.where(from_block, my_docs[None, :], 0), axis=1)
    every = jnp.arange(doc_lens.shape[0], dtype=jnp.int32)
    lengths = jnp.sum(jnp.where(which[:, None] == every[None, :], doc_lens[None, :], 0), axis=1)
    held = device * pool_dev + jnp.arange(pool_dev, dtype=jnp.int32)
    wanted = jnp.any(query_docs[:, :, None] == held[None, None, :], axis=1)
    column = jnp.concatenate(
        [lengths.astype(f32), wanted.astype(f32).reshape(-1), jnp.zeros((4,), f32)]
    )
    notes = jnp.broadcast_to(column[:, None], (16, 128))
    positions = jnp.concatenate(
        [row_pos[docs_per] + jnp.arange(length, dtype=jnp.int32), starts, jnp.zeros((4,), jnp.int32)]
    )
    half = head_dim // 2
    freq = jnp.exp(jnp.arange(half, dtype=f32) * (-2.0 * math.log(rope_theta) / head_dim))
    angle = positions.astype(f32)[:, None] * freq[None, :]
    cosine = jnp.cos(angle)
    sine = jnp.sin(angle)
    rope = jnp.stack(
        [jnp.concatenate([cosine, cosine], axis=1), jnp.concatenate([-sine, sine], axis=1)]
    )
    vmem = pl.BlockSpec(memory_space=pltpu.VMEM)
    dma = pltpu.SemaphoreType.DMA
    some = heads // 2
    block = (4, length, width)
    return pl.pallas_call(
        context_kernel,
        out_shape=[
            jax.ShapeDtypeStruct((length, width), bf16),
            jax.ShapeDtypeStruct((length, width), bf16),
            jax.ShapeDtypeStruct((4, 16, length), bf16),
        ],
        in_specs=[vmem] * 9 + [pl.BlockSpec(memory_space=pl.ANY)],
        out_specs=[vmem] * 3,
        scratch_shapes=[
            pltpu.VMEM(out_proj.shape, bf16),
            pltpu.VMEM((4, 2, length, head_dim), bf16),
            pltpu.VMEM((4, 2, length, head_dim), bf16),
            pltpu.VMEM((heads, length, head_dim), bf16),
            pltpu.VMEM((5 * length, head_dim), bf16),
            pltpu.VMEM((5 * length, head_dim), bf16),
            pltpu.VMEM((2, some, length, head_dim), bf16),
            pltpu.VMEM((4, 2, some, length, head_dim), bf16),
            pltpu.VMEM(block, f32),
            pltpu.VMEM(block, bf16),
            pltpu.VMEM(block, bf16),
            pltpu.VMEM(block, bf16),
            pltpu.VMEM(block, bf16),
            pltpu.VMEM((4, experts + 8, length), f32),
            dma,
            dma((4,)),
            dma((4,)),
            dma((2,)),
            dma((2,)),
            dma((3, 2)),
            dma((3, 2)),
            dma((4,)),
            dma((4,)),
            dma((4,)),
            dma((4,)),
            dma((4,)),
            dma((4,)),
        ],
        compiler_params=pltpu.CompilerParams(
            collective_id=0, has_side_effects=True, vmem_limit_bytes=40 << 20
        ),
    )(
        question_q, question_kv, doc_kv, rope, notes, hidden, norm_gain[None, :],
        jnp.swapaxes(router_weight, 0, 1), jnp.swapaxes(expert_ids, 0, 1), out_proj,
    )


def fused_experts(normed, routes, residual, w_gate_up, w_down, capacity):
    length, width = normed.shape
    count = w_gate_up.shape[0]
    hidden = w_gate_up.shape[3]
    bf16 = jnp.bfloat16
    units = 4 * count
    quarter = hidden // 4
    vmem = pl.BlockSpec(memory_space=pltpu.VMEM)
    anywhere = pl.BlockSpec(memory_space=pl.ANY)
    dma = pltpu.SemaphoreType.DMA
    return pl.pallas_call(
        experts_kernel,
        out_shape=jax.ShapeDtypeStruct((length, width), bf16),
        in_specs=[vmem, vmem, vmem, anywhere, anywhere],
        out_specs=vmem,
        scratch_shapes=[
            pltpu.VMEM((2,) + w_gate_up.shape[1:], bf16),
            pltpu.VMEM((count, width, hidden), bf16),
            pltpu.VMEM((count, width, hidden), bf16),
            pltpu.VMEM(w_down.shape, bf16),
            pltpu.VMEM((4, length, width), bf16),
            pltpu.VMEM((4, 16, length), bf16),
            pltpu.VMEM((units, 2, 2, capacity, 2 * quarter), bf16),
            pltpu.VMEM((units, 2, capacity, 2 * quarter), bf16),
            pltpu.VMEM((units, capacity, 2 * quarter), bf16),
            pltpu.VMEM((units, capacity, 2 * quarter), bf16),
            pltpu.VMEM((units, 2, 2, capacity, quarter), bf16),
            pltpu.VMEM((4, length, width), jnp.float32),
            pltpu.VMEM((4, length, width), bf16),
            pltpu.VMEM((4, length, width), bf16),
            dma((2,)),
            dma((count,)),
            dma((2, 4)),
            dma((2, 4)),
            dma((5, units)),
            dma((5, units)),
            dma((4,)),
            dma((4,)),
        ],
        compiler_params=pltpu.CompilerParams(
            collective_id=1, has_side_effects=True, vmem_limit_bytes=58 << 20
        ),
    )(normed, routes, residual, w_gate_up, w_down)


def feed_forward(arrived, w_gate_up, w_down):
    term = jnp.einsum("erd,edgh->hegr", arrived, w_gate_up, preferred_element_type=jnp.float32)
    summed = lax.psum_scatter(
        term.astype(jnp.bfloat16), "tp", scatter_dimension=0, tiled=True
    ).astype(jnp.float32)
    activated = (jax.nn.silu(summed[:, :, 0]) * summed[:, :, 1]).astype(jnp.bfloat16)
    piece = lax.all_gather(activated, "tp", axis=0, tiled=True)
    return jnp.einsum(
        "her,ehd->erd", piece, w_down, preferred_element_type=jnp.float32
    ).astype(jnp.bfloat16)


def per_device(
    question_q,
    question_kv,
    doc_kv,
    doc_lens,
    query_docs,
    ctx_pos,
    hidden,
    out_proj,
    norm_gain,
    router_weight,
    w_gate_up,
    w_down,
    expert_ids,
):
    lanes = lax.axis_size("tp")
    groups = lax.axis_size("ep")
    lane = lax.axis_index("tp")
    device = lax.axis_index("ep")
    length, heads_here, head_dim = question_q.shape
    kv_heads = question_kv.shape[1]
    if lanes == 4 and groups == 4:
        residual, normed, routes = fused_context(
            question_q, question_kv, doc_kv, doc_lens, query_docs, ctx_pos, hidden, out_proj,
            norm_gain, router_weight, expert_ids,
        )
        capacity = length * expert_ids.shape[1] // (w_gate_up.shape[0] * groups)
        return fused_experts(normed, routes, residual, w_gate_up, w_down, capacity)
    kv_pick = lane * kv_heads // lanes
    scale = head_dim ** (-0.5)
    docs_per = query_docs.shape[1]
    row_pos = lax.dynamic_index_in_dim(ctx_pos, device, 0, keepdims=False)
    question_pos = row_pos[docs_per] + jnp.arange(length, dtype=jnp.int32)
    queries = rotate(question_q, question_pos).astype(jnp.bfloat16)
    own_kv = lax.dynamic_index_in_dim(question_kv, kv_pick, 1, keepdims=False)
    own_keys = rotate(own_kv[:, 0], question_pos).astype(jnp.bfloat16)
    own_values = own_kv[:, 1]
    causal = jnp.arange(length)[:, None] >= jnp.arange(length)[None, :]
    doc_keys, doc_values, valid = fetch_context(
        doc_kv, doc_lens, query_docs, row_pos, device, kv_pick
    )
    keys = jnp.concatenate([doc_keys, own_keys], axis=0)
    values = jnp.concatenate([doc_values, own_values], axis=0)
    allowed = jnp.concatenate(
        [jnp.broadcast_to(valid[None, :], (length, valid.shape[0])), causal], axis=1
    )
    scores = jnp.einsum("ihd,jd->hij", queries, keys, preferred_element_type=jnp.float32) * scale
    scores = jnp.where(allowed[None], scores, -jnp.inf)
    ceiling = jnp.max(scores, axis=-1, keepdims=True)
    probs = jnp.exp(scores - ceiling)
    denominator = jnp.sum(probs, axis=-1, keepdims=True)
    mixed = jnp.einsum(
        "hij,jd->hid", probs.astype(jnp.bfloat16), values, preferred_element_type=jnp.float32
    )
    attended = (
        jnp.transpose(mixed / denominator, (1, 0, 2))
        .reshape(length, heads_here * head_dim)
        .astype(jnp.bfloat16)
    )
    width_here = hidden.shape[1]
    projected = project(attended, out_proj)
    residual_wide = narrow(hidden.astype(jnp.float32) + projected).astype(jnp.float32)
    gain = norm_gain.astype(jnp.float32)
    squares, logit_part = lax.psum(
        (
            jnp.sum(residual_wide * residual_wide, axis=1),
            jnp.dot(
                residual_wide * gain[None, :],
                router_weight.astype(jnp.float32),
                precision=lax.Precision.HIGHEST,
            ),
        ),
        "tp",
    )
    inv_rms = lax.rsqrt(squares / D + norm_eps)
    normed = (residual_wide * inv_rms[:, None] * gain[None, :]).astype(jnp.bfloat16)
    logits = logit_part * inv_rms[:, None]
    local_experts = w_gate_up.shape[0]
    capacity = length * expert_ids.shape[1] // (local_experts * groups)
    experts = logits.shape[1]
    chosen = jnp.any(expert_ids[:, :, None] == jnp.arange(experts, dtype=jnp.int32), axis=1)
    top = jnp.max(jnp.where(chosen, logits, -jnp.inf), axis=1, keepdims=True)
    raised = jnp.where(chosen, jnp.exp(jnp.where(chosen, logits - top, 0.0)), 0.0)
    mix = raised / jnp.sum(raised, axis=1, keepdims=True)
    mix_high = mix.astype(jnp.bfloat16)
    mix_low = (mix - mix_high.astype(jnp.float32)).astype(jnp.bfloat16)
    notes = jnp.concatenate([chosen.astype(jnp.bfloat16), mix_high, mix_low], axis=1)
    notes = jnp.pad(notes, ((0, 0), (0, -notes.shape[1] % 128)))
    packed = lax.all_gather(jnp.concatenate([normed, notes], axis=1), "ep", axis=0)
    normed_all = packed[:, :, :width_here]

    def mine(index):
        start = width_here + index * experts + device * local_experts
        return lax.dynamic_slice_in_dim(packed, start, local_experts, axis=2)

    member = mine(0) > 0
    share_high = jnp.swapaxes(mine(1), 1, 2)
    share_low = jnp.swapaxes(mine(2), 1, 2)
    earlier = jnp.arange(length)[:, None] > jnp.arange(length)[None, :]
    rank = jnp.einsum(
        "nm,sme->sen",
        earlier.astype(jnp.bfloat16),
        member.astype(jnp.bfloat16),
        preferred_element_type=jnp.float32,
    )
    seat = jnp.where(jnp.swapaxes(member, 1, 2), rank.astype(jnp.int32), -1)
    picks = (seat[:, :, None, :] == jnp.arange(capacity, dtype=jnp.int32)[:, None]).astype(
        jnp.bfloat16
    )
    arrived = jnp.einsum(
        "secn,snd->escd", picks, normed_all, preferred_element_type=jnp.float32
    ).astype(jnp.bfloat16)
    rows = groups * capacity
    arrived = arrived.reshape(local_experts, rows, width_here)
    expert_out = feed_forward(arrived, w_gate_up, w_down)
    weights = jnp.stack([picks * share_high[:, :, None, :], picks * share_low[:, :, None, :]])
    partial = jnp.einsum(
        "psecn,escd->snd",
        weights,
        expert_out.reshape(local_experts, groups, capacity, width_here),
        preferred_element_type=jnp.float32,
    )
    combined = lax.psum_scatter(
        partial.astype(jnp.bfloat16).reshape(groups * length, width_here),
        "ep",
        scatter_dimension=0,
        tiled=True,
    )
    return (residual_wide + combined.astype(jnp.float32)).astype(jnp.bfloat16)


def solution(mesh):
    placed = (
        P(("grp", "ep"), "tp", None),
        P(("grp", "ep"), None, None, None),
        P(("grp", "ep"), None, None, None, None),
        P("grp"),
        P("grp", None),
        P("grp", None),
        P(("grp", "ep"), "tp"),
        P("ep", "tp"),
        P("tp"),
        P("tp", None),
        P("ep", "tp", None, None),
        P("ep", None, "tp"),
        P(("grp", "ep"), None),
    )
    return jax.shard_map(
        per_device, mesh=mesh, in_specs=placed, out_specs=P(("grp", "ep"), "tp"), check_vma=False
    )
```

```python
import math

import jax
import jax.numpy as jnp
from jax import lax
from jax.experimental import pallas as pl
from jax.experimental.pallas import tpu as pltpu
from jax.sharding import PartitionSpec as P

D = 4096
HID = 1024


rope_theta = 1000000.0
norm_eps = 1e-06


def narrow(values):
    return lax.optimization_barrier(values.astype(jnp.bfloat16))


def rotate(values, positions):
    half = values.shape[-1] // 2
    freq = jnp.exp(
        jnp.arange(half, dtype=jnp.float32) * (-2.0 * math.log(rope_theta) / values.shape[-1])
    )
    angle = positions.astype(jnp.float32)[:, None] * freq[None, :]
    shape = (values.shape[0],) + (1,) * (values.ndim - 2) + (half,)
    cosine = jnp.cos(angle).reshape(shape)
    sine = jnp.sin(angle).reshape(shape)
    floats = values.astype(jnp.float32)
    first = floats[..., :half]
    second = floats[..., half:]
    return jnp.concatenate(
        [first * cosine - second * sine, second * cosine + first * sine], axis=-1
    )


def fetch_context(doc_kv, doc_lens, query_docs, row_pos, device, kv_pick):
    pool_dev, doc_max, kv_heads, pair, head_dim = doc_kv.shape
    docs_per = query_docs.shape[1]
    pool_head = lax.dynamic_index_in_dim(doc_kv, kv_pick, 2, keepdims=False).reshape(
        pool_dev, doc_max, pair * head_dim
    )
    held = device * pool_dev + jnp.arange(pool_dev, dtype=jnp.int32)
    wanted = jnp.sum((query_docs[:, :, None] == held[None, None, :]).astype(jnp.float32), axis=1)
    sending = jnp.einsum(
        "rl,lkc->rkc", wanted.astype(jnp.bfloat16), pool_head, preferred_element_type=jnp.float32
    ).astype(jnp.bfloat16)
    received = lax.all_to_all(sending, "ep", split_axis=0, concat_axis=0, tiled=True)
    my_docs = lax.dynamic_index_in_dim(query_docs, device, 0, keepdims=False)
    from_dev = jnp.arange(received.shape[0], dtype=jnp.int32)
    pick_dev = ((my_docs // pool_dev)[:, None] == from_dev[None, :]).astype(jnp.bfloat16)
    context = jnp.einsum(
        "jr,rkc->jkc", pick_dev, received, preferred_element_type=jnp.float32
    ).astype(jnp.bfloat16)
    every_doc = jnp.arange(doc_lens.shape[0], dtype=jnp.int32)
    lengths = jnp.sum(
        jnp.where(my_docs[:, None] == every_doc[None, :], doc_lens[None, :], 0), axis=1
    )
    positions = jnp.repeat(row_pos[:docs_per], doc_max, total_repeat_length=docs_per * doc_max)
    keys = rotate(context[:, :, :head_dim].reshape(docs_per * doc_max, head_dim), positions).astype(
        jnp.bfloat16
    )
    values = context[:, :, head_dim:].reshape(docs_per * doc_max, head_dim)
    valid = (jnp.arange(doc_max, dtype=jnp.int32)[None, :] < lengths[:, None]).reshape(
        docs_per * doc_max
    )
    return (keys, values, valid)


def project(attended, out_proj):
    lanes = lax.axis_size("tp")
    groups = lax.axis_size("ep")
    length = attended.shape[0]
    if lanes == groups:
        swap = [(e * lanes + t, t * lanes + e) for e in range(groups) for t in range(lanes)]
        block = lax.ppermute(attended, ("ep", "tp"), swap)
        tokens = lax.all_gather(block, "tp", axis=0, tiled=True)
    else:
        all_heads = lax.all_gather(attended, "tp", axis=1, tiled=True)
        split = jnp.swapaxes(all_heads.reshape(length, groups, -1), 0, 1)
        tokens = lax.all_to_all(split, "ep", split_axis=0, concat_axis=0, tiled=True)
        tokens = tokens.reshape(groups * length, -1)
    part = jnp.dot(tokens, out_proj, preferred_element_type=jnp.float32)
    summed = lax.psum_scatter(
        part.astype(jnp.bfloat16), "ep", scatter_dimension=0, tiled=True
    ).astype(jnp.float32)
    return summed


MESH = pl.DeviceIdType.MESH


def when(condition):
    return pl.when(condition)


def halves_turn(index):
    return 2 * lax.rem(index, 2) + index // 2


def source_of(z, rank):
    low = z < 2
    near = z + 1 - 2 * lax.rem(z, 2)
    inner = jnp.where(low, 2, 1)
    outer = jnp.where(low, 3, 0)
    return jnp.where(
        rank == 0, z, jnp.where(rank == 1, inner, jnp.where(rank == 2, outer, near))
    )


def unit_of(z, u):
    step = jnp.maximum(u - 2, 0)
    rank = jnp.where((u < 2) | (u >= 14), 0, lax.rem(step // 4 + 2, 3) + 1)
    j = jnp.where(u < 2, u + 2, lax.rem(step, 4))
    return rank, source_of(z, rank), j


def layer_kernel(
    q_hbm, kv_hbm, docs_hbm, lens_hbm, lists_hbm, ctx_hbm, hidden_hbm, gain_hbm, router_hbm,
    ids_hbm, wo_hbm, wgu_hbm, wd_hbm, out,
    q, own_kv, docs, lens, lists, ctx, hidden, gain, router, ids, load_sem,
    wo, sending, context, queries, keys, values, own_att, att, parts,
    go_up, go_down, from_below, from_above, sums,
    wo_sem, doc_send, doc_recv, swap_send, swap_recv, att_send, att_recv,
    up_send, up_recv, down_send, down_recv, sum_send, sum_recv,
    stage, w_gate, w_up, w_down, resid, my_seats, my_mixes, blocks, seats, mixes,
    sent, first, pair, second, acts, total, leaving, relayed, coming,
    stage_sem, down_sem, hop_up, hop_down, hop_recv, table_send, table_recv,
    tp_send, tp_recv, rs_send, relay_recv, rs_recv,
):
    bf16 = jnp.bfloat16
    f32 = jnp.float32
    z = lax.axis_index("ep")
    lane = lax.axis_index("tp")
    chip = lane // 2
    core = lane % 2
    partner = chip * 2 + (1 - core)
    across = (1 - chip) * 2 + core
    length, width = hidden.shape
    heads = q.shape[1]
    head_dim = q.shape[2]
    features = width * 4
    some = heads // 2

    loads = [
        pltpu.make_async_copy(source, target, load_sem.at[i])
        for i, (source, target) in enumerate(
            (
                (docs_hbm.at[:, :, lane], docs),
                (lists_hbm, lists),
                (ctx_hbm, ctx),
                (lens_hbm, lens),
                (q_hbm, q),
                (kv_hbm.at[:, lane], own_kv),
                (ids_hbm, ids),
                (hidden_hbm, hidden),
                (gain_hbm, gain),
                (router_hbm, router),
            )
        )
    ]
    for load in loads:
        load.start()
    load_wo = pltpu.make_async_copy(wo_hbm, wo, wo_sem)
    load_wo.start()
    count, inner = w_down.shape[:2]
    cap = sent.shape[3]
    quarter = acts.shape[4]
    units = 4 * count
    piece = stage.shape[1]
    pieces = inner // piece

    def load_in(i):
        rows = pl.ds((i % pieces) * piece, piece)
        return pltpu.make_async_copy(
            wgu_hbm.at[i // pieces, rows], stage.at[i % 2], stage_sem.at[i % 2]
        )

    load_in(0).start()
    load_in(1).start()
    load_down = pltpu.make_async_copy(wd_hbm, w_down, down_sem)
    load_down.start()

    def relay(i):
        load_in(i).wait()
        step = 128

        def body(k, carry):
            rows = pl.ds(pl.multiple_of(k * step, step), step)
            place = pl.ds(pl.multiple_of((i % pieces) * piece + k * step, step), step)
            block = jnp.transpose(stage[i % 2, rows], (1, 0, 2))
            w_gate[i // pieces, place, :] = block[0]
            w_up[i // pieces, place, :] = block[1]
            return carry

        lax.fori_loop(0, piece // step, body, 0)
        if i + 2 < count * pieces:
            load_in(i + 2).start()

    swap_to = {"ep": lane, "tp": halves_turn(z)}
    swap_from = {"ep": halves_turn(lane), "tp": z}
    moves = (lane != z) | (halves_turn(z) != lane)
    barrier = pltpu.get_barrier_semaphore()
    for k in range(1, 4):
        for axis, here in (("ep", z), ("tp", lane)):
            pl.semaphore_signal(
                barrier, inc=1, device_id={axis: lax.rem(here + k, 4)}, device_id_type=MESH
            )

    @when(moves)
    def _():
        for other in (swap_to, swap_from):
            pl.semaphore_signal(barrier, inc=1, device_id=other, device_id_type=MESH)

    for load in loads[:3]:
        load.wait()
    found = [jnp.transpose(docs[l], (1, 0, 2)).astype(f32) for l in range(2)]
    for r in range(4):
        shares = []
        for l in range(2):
            hit = lists[r, 0] == 2 * z + l
            for j in range(1, 4):
                hit = hit | (lists[r, j] == 2 * z + l)
            shares.append(jnp.where(hit, 1.0, 0.0).astype(f32))
        sending[r] = (found[0] * shares[0] + found[1] * shares[1]).astype(bf16)

    pl.semaphore_wait(barrier, jnp.where(moves, 8, 6))

    def doc_copy(dest, source):
        return pltpu.make_async_remote_copy(
            src_ref=sending.at[dest],
            dst_ref=context.at[source],
            send_sem=doc_send.at[dest],
            recv_sem=doc_recv.at[source],
            device_id={"ep": dest},
            device_id_type=MESH,
        )

    for k in range(1, 4):
        doc_copy(lax.rem(z + k, 4), z).start()
    context[z] = sending[z]

    def rotate_rows(rows, cosine, sine):
        return (rows * cosine + pltpu.roll(rows, head_dim // 2, 1) * sine).astype(bf16)

    for load in loads[3:]:
        load.wait()
    half = head_dim // 2
    lanes = lax.broadcasted_iota(jnp.int32, (1, head_dim), 1)
    freq = jnp.exp(
        lax.rem(lanes, half).astype(f32) * (-2.0 * math.log(rope_theta) / head_dim)
    )
    sign = jnp.where(lanes < half, -1.0, 1.0)
    steps = lax.broadcasted_iota(jnp.int32, (length, head_dim), 0)
    angle = (ctx[z, 4] + steps).astype(f32) * freq
    cosine = jnp.cos(angle)
    sine = jnp.sin(angle) * sign
    starts = []
    limits = []
    for s in range(4):
        start = jnp.int32(0)
        which = jnp.int32(0)
        for j in range(4):
            here = lists[z, j] // 2 == s
            start = start + jnp.where(here, ctx[z, j], 0)
            which = which + jnp.where(here, lists[z, j], 0)
        limit = jnp.int32(0)
        for d in range(8):
            limit = limit + jnp.where(which == d, lens[d], 0)
        starts.append(start)
        limits.append(limit)
    row = lax.broadcasted_iota(jnp.int32, (8, head_dim), 0)
    begin = jnp.zeros((8, head_dim), jnp.int32)
    for s in range(4):
        begin = jnp.where(row == s, starts[s], begin)
    doc_angle = begin.astype(f32) * freq
    doc_cosine = jnp.cos(doc_angle)
    doc_sine = jnp.sin(doc_angle) * sign
    turned = jnp.transpose(q[...], (1, 0, 2))
    for h in range(heads):
        queries[h] = rotate_rows(turned[h].astype(f32), cosine, sine)
    own = jnp.transpose(own_kv[...], (1, 0, 2))
    last = pl.ds(4 * length, length)
    keys[last, :] = rotate_rows(own[0].astype(f32), cosine, sine)
    values[last, :] = own[1]

    experts = router.shape[0]
    expert = lax.broadcasted_iota(jnp.int32, (experts, length), 0)
    picked = jnp.zeros((experts, length), f32)
    for k in range(ids.shape[0]):
        picked = picked + jnp.where(ids[k : k + 1, :] == expert, 1.0, 0.0)
    before = (
        lax.broadcasted_iota(jnp.int32, (length, length), 0)
        < lax.broadcasted_iota(jnp.int32, (length, length), 1)
    )
    rank = jnp.dot(
        picked.astype(bf16),
        jnp.where(before, 1.0, 0.0).astype(bf16),
        preferred_element_type=f32,
    )
    seat = jnp.where(picked > 0.0, rank, -1.0)
    blank = jnp.zeros((8 - count, length), f32)
    for d in range(4):
        my_seats[d] = jnp.concatenate([seat[d * count : (d + 1) * count], blank], axis=0)
    seats[z] = my_seats[z]

    def table_copy(kind, dest, source):
        mine_, theirs_ = ((my_seats, seats), (my_mixes, mixes))[kind]
        return pltpu.make_async_remote_copy(
            src_ref=mine_.at[dest],
            dst_ref=theirs_.at[source],
            send_sem=table_send.at[kind, dest],
            recv_sem=table_recv.at[kind, source],
            device_id={"ep": dest},
            device_id_type=MESH,
        )

    for k in range(1, 4):
        table_copy(0, lax.rem(z + k, 4), z).start()

    for i in range(count * pieces // 2):
        relay(i)
    for k in range(1, 4):
        source = lax.rem(z + k, 4)
        doc_copy(source, source).wait_recv()
    for s in range(4):
        row = pl.ds(s * length, length)
        keys[row, :] = rotate_rows(
            context[s, 0].astype(f32),
            doc_cosine[s : s + 1],
            doc_sine[s : s + 1],
        )
        values[row, :] = context[s, 1]

    column = lax.broadcasted_iota(jnp.int32, (length, length), 1)
    line = lax.broadcasted_iota(jnp.int32, (length, length), 0)
    scale = head_dim ** (-0.5)

    def swap_copy(c, query):
        return pltpu.make_async_remote_copy(
            src_ref=own_att.at[c],
            dst_ref=att.at[query, c],
            send_sem=swap_send.at[c],
            recv_sem=swap_recv.at[c],
            device_id=swap_to,
            device_id_type=MESH,
        )

    allowed = [
        jnp.where(column < limits[s], 0.0, -jnp.inf) for s in range(4)
    ] + [jnp.where(column <= line, 0.0, -jnp.inf)]
    bias = jnp.concatenate(allowed, axis=1)

    def one_head(c, h):
        scores = lax.dot_general(
            queries[c * some + h], keys[...], (((1,), (1,)), ((), ())),
            preferred_element_type=f32,
        )
        scores = scores * scale + bias
        ceiling = jnp.max(scores, axis=1, keepdims=True)
        probs = jnp.exp(scores - ceiling)
        denominator = jnp.sum(probs, axis=1, keepdims=True)
        mixed = jnp.dot(probs.astype(bf16), values[...], preferred_element_type=f32)
        own_att[c, h] = (mixed / denominator).astype(bf16)

    for c in range(2):
        def body(h, carry):
            one_head(c, h)
            return carry

        lax.fori_loop(0, some, body, 0)

        @when(moves)
        def _():
            swap_copy(c, z).start()

        @when(jnp.logical_not(moves))
        def _():
            att[z, c] = own_att[c]

    mine = halves_turn(lane)
    theirs = halves_turn(across)

    def att_copy(kind, c, query, other):
        return pltpu.make_async_remote_copy(
            src_ref=att.at[query, c],
            dst_ref=att.at[query, c],
            send_sem=att_send.at[kind, c],
            recv_sem=att_recv.at[kind, c],
            device_id={"tp": other},
            device_id_type=MESH,
        )

    def att_copies(c):
        return [
            att_copy(0, c, mine, across),
            att_copy(1, c, mine, partner),
            att_copy(2, c, theirs, partner),
        ]

    for i in range(count * pieces // 2, count * pieces):
        relay(i)
    for c in range(2):
        @when(moves)
        def _():
            swap_copy(c, mine).wait_recv()

        att_copies(c)[0].start()
        att_copies(c)[1].start()
    for c in range(2):
        att_copy(0, c, theirs, across).wait_recv()
        att_copies(c)[2].start()
    load_wo.wait()
    for c in range(2):
        att_copy(1, c, halves_turn(partner), partner).wait_recv()
        att_copy(2, c, halves_turn(3 - lane), partner).wait_recv()

    def up_copy(b):
        return pltpu.make_async_remote_copy(
            src_ref=go_up.at[b],
            dst_ref=from_below.at[b],
            send_sem=up_send.at[b],
            recv_sem=up_recv.at[b],
            device_id={"ep": jnp.minimum(z + 1, 3)},
            device_id_type=MESH,
        )

    def down_copy(b):
        return pltpu.make_async_remote_copy(
            src_ref=go_down.at[b],
            dst_ref=from_above.at[b],
            send_sem=down_send.at[b],
            recv_sem=down_recv.at[b],
            device_id={"ep": jnp.maximum(z - 1, 0)},
            device_id_type=MESH,
        )

    def project_block(b):
        rows = jnp.concatenate([att[b, h // some, h % some] for h in range(heads)], axis=1)
        parts[b] = jnp.dot(rows, wo[...], preferred_element_type=f32)

    def send_up(b):
        @when(z == 0)
        def _():
            go_up[b] = parts[b].astype(bf16)

        @when((z > 0) & (z < b))
        def _():
            up_copy(b).wait_recv()
            go_up[b] = (parts[b] + from_below[b].astype(f32)).astype(bf16)

        @when(z < b)
        def _():
            up_copy(b).start()

    def send_down(b):
        @when(z == 3)
        def _():
            go_down[b] = parts[b].astype(bf16)

        @when((z < 3) & (z > b))
        def _():
            down_copy(b).wait_recv()
            go_down[b] = (parts[b] + from_above[b].astype(f32)).astype(bf16)

        @when(z > b)
        def _():
            down_copy(b).start()

    project_block(3)

    @when(z == 0)
    def _():
        send_up(3)

    project_block(0)

    @when(z == 3)
    def _():
        send_down(0)

    project_block(2)
    project_block(1)

    @when(z > 0)
    def _():
        send_up(3)

    @when(z < 3)
    def _():
        send_down(0)

    send_up(2)
    send_down(1)
    send_up(1)
    send_down(2)

    parts[z] += hidden[...].astype(f32)

    @when(z > 0)
    def _():
        up_copy(z).wait_recv()
        parts[z] += from_below[z].astype(f32)

    @when(z < 3)
    def _():
        down_copy(z).wait_recv()
        parts[z] += from_above[z].astype(f32)

    residual = parts[z].astype(bf16)
    resid[...] = residual
    wide = residual.astype(f32)
    gain_rows = gain[...].astype(f32)
    gains = jnp.concatenate([gain_rows[i : i + 1] for i in range(gain.shape[0])], axis=1)
    raised = wide * gains
    blocks[z] = raised.astype(bf16)

    def hop_copy(source, dest, sem):
        return pltpu.make_async_remote_copy(
            src_ref=blocks.at[source],
            dst_ref=blocks.at[source],
            send_sem=sem,
            recv_sem=hop_recv.at[source],
            device_id={"ep": dest},
            device_id_type=MESH,
        )

    def hop_pair(h, act_on):
        @when((z - h >= 0) & (z < 3))
        def _():
            act_on(hop_copy(jnp.maximum(z - h, 0), jnp.minimum(z + 1, 3), hop_up.at[h]))

        @when((z + h <= 3) & (z > 0))
        def _():
            act_on(hop_copy(jnp.minimum(z + h, 3), jnp.maximum(z - 1, 0), hop_down.at[h]))

    def hop(h):
        if h > 0:
            for off in (-h, h):
                source = z + off

                @when((source >= 0) & (source <= 3))
                def _():
                    hop_copy(source, source, hop_up.at[0]).wait_recv()

        if h < 3:
            hop_pair(h, lambda copy: copy.start())

    hop(0)
    logit_part = lax.dot_general(
        router[...].astype(f32), raised, (((1,), (1,)), ((), ())),
        precision=lax.Precision.HIGHEST, preferred_element_type=f32,
    )
    square_part = lax.dot_general(
        jnp.ones((8, width), f32), wide * wide, (((1,), (1,)), ((), ())),
        precision=lax.Precision.HIGHEST, preferred_element_type=f32,
    )
    sums[lane] = jnp.concatenate([logit_part, square_part], axis=0)

    def sum_copy(dest, source):
        return pltpu.make_async_remote_copy(
            src_ref=sums.at[source],
            dst_ref=sums.at[source],
            send_sem=sum_send.at[dest],
            recv_sem=sum_recv.at[source],
            device_id={"tp": dest},
            device_id_type=MESH,
        )

    for k in range(1, 4):
        sum_copy(lax.rem(lane + k, 4), lane).start()
    total[...] = jnp.zeros_like(total)
    load_down.wait()

    def finish_sums():
        for k in range(1, 4):
            source = lax.rem(lane + k, 4)
            sum_copy(source, source).wait_recv()
        added = (sums[0] + sums[1]) + (sums[2] + sums[3])
        inverse = lax.rsqrt(added[experts : experts + 1] / features + norm_eps)
        logits = added[:experts] * inverse
        inside = picked > 0.0
        top = jnp.max(jnp.where(inside, logits, -jnp.inf), axis=0, keepdims=True)
        lifted = jnp.where(inside, jnp.exp(jnp.where(inside, logits - top, 0.0)), 0.0)
        mix = lifted / jnp.sum(lifted, axis=0, keepdims=True)
        rest = jnp.broadcast_to(inverse, (8 - count, length))
        for d in range(4):
            my_mixes[d] = jnp.concatenate([mix[d * count : (d + 1) * count], rest], axis=0)
        mixes[z] = my_mixes[z]
        for k in range(1, 4):
            table_copy(1, lax.rem(z + k, 4), z).start()

    def remote(kind, u, source, target, other):
        return pltpu.make_async_remote_copy(
            src_ref=source,
            dst_ref=target,
            send_sem=tp_send.at[kind, u],
            recv_sem=tp_recv.at[kind, u],
            device_id={"tp": other},
            device_id_type=MESH,
        )

    def tp_copies(u):
        return [
            remote(0, u, sent.at[u, 1 - core], first.at[u], partner),
            remote(1, u, pair.at[u], second.at[u], across),
            remote(2, u, acts.at[u, core, chip], acts.at[u, core, chip], across),
            remote(3, u, acts.at[u, core, chip], acts.at[u, core, chip], partner),
            remote(4, u, acts.at[u, core, 1 - chip], acts.at[u, core, 1 - chip], partner),
        ]

    outside = (z == 0) | (z == 3)
    rows_half = length // 2

    def near_copy(part):
        return pltpu.make_async_remote_copy(
            src_ref=leaving.at[3, part],
            dst_ref=coming.at[0, part],
            send_sem=rs_send.at[3, part],
            recv_sem=rs_recv.at[0, part],
            device_id={"ep": source_of(z, 3)},
            device_id_type=MESH,
        )

    def relay_copy(rank, part):
        return pltpu.make_async_remote_copy(
            src_ref=leaving.at[rank, part],
            dst_ref=relayed.at[rank, part],
            send_sem=rs_send.at[rank, part],
            recv_sem=relay_recv.at[rank, part],
            device_id={"ep": source_of(z, 3)},
            device_id_type=MESH,
        )

    def far_copy(rank, part):
        return pltpu.make_async_remote_copy(
            src_ref=leaving.at[rank, part],
            dst_ref=coming.at[1, part],
            send_sem=rs_send.at[rank, part],
            recv_sem=rs_recv.at[1, part],
            device_id={"ep": source_of(z, rank)},
            device_id_type=MESH,
        )

    def part_rows(part):
        return pl.ds(part * rows_half, rows_half)

    def leave(rank):
        source = source_of(z, rank)

        @when((rank == 3) | outside)
        def _():
            for part in range(2):
                leaving[rank, part] = total[source, part_rows(part)].astype(bf16)

        @when(rank == 3)
        def _():
            for part in range(2):
                near_copy(part).start()

        @when((rank < 3) & outside)
        def _():
            for part in range(2):
                relay_copy(rank, part).start()

    def relay_on(rank):
        source = source_of(z, rank)

        @when(jnp.logical_not(outside))
        def _():
            for part in range(2):
                relay_copy(rank, part).wait_recv()
                leaving[rank, part] = (
                    total[source, part_rows(part)] + relayed[rank, part].astype(f32)
                ).astype(bf16)
                far_copy(rank, part).start()

    def row_of(tables, source, row):
        table = tables[source]
        rows = lax.broadcasted_iota(jnp.int32, table.shape, 0)
        return jnp.sum(jnp.where(rows == row, table, 0.0), axis=0, keepdims=True)

    places = lax.broadcasted_iota(jnp.int32, (cap, length), 0).astype(f32)

    def multiply_in(u):
        rank, source, j = unit_of(z, u)

        @when((rank > 0) & (j == 0))
        def _():
            table_copy(0, source, source).wait_recv()

        pick = (places == row_of(seats, source, j)).astype(bf16)
        rows = jnp.dot(pick, blocks[source], preferred_element_type=f32).astype(bf16)
        for kind, weights in enumerate((w_gate, w_up)):
            part = jnp.dot(rows, weights[j], preferred_element_type=f32).astype(bf16)
            for q in range(4):
                sent[u, q % 2, q // 2, :, kind * quarter : (kind + 1) * quarter] = part[
                    :, q * quarter : (q + 1) * quarter
                ]
        tp_copies(u)[0].start()

    def add_pair(u):
        copies = tp_copies(u)
        copies[0].wait_recv()
        both = sent[u, core, 1 - chip].astype(f32) + first[u, 1 - chip].astype(f32)
        pair[u] = both.astype(bf16)
        copies[1].start()

    def activate(u):
        rank, source, j = unit_of(z, u)

        @when((rank > 0) & (j == 0))
        def _():
            table_copy(1, source, source).wait_recv()

        scale_row = row_of(mixes, source, count)
        factor = jnp.sum(
            jnp.where(places == row_of(seats, source, j), scale_row, 0.0), axis=1, keepdims=True
        )
        copies = tp_copies(u)
        copies[1].wait_recv()
        value = (
            sent[u, core, chip].astype(f32)
            + first[u, chip].astype(f32)
            + second[u].astype(f32)
        ) * factor
        gate = value[:, :quarter]
        acts[u, core, chip] = (gate / (1.0 + jnp.exp(-gate)) * value[:, quarter:]).astype(bf16)
        copies[2].start()
        copies[3].start()

    def forward(u):
        copies = tp_copies(u)
        copies[2].wait_recv()
        copies[4].start()

    def multiply_out(u):
        rank, source, j = unit_of(z, u)
        copies = tp_copies(u)
        copies[3].wait_recv()
        copies[4].wait_recv()

        joined = jnp.concatenate([acts[u, q % 2, q // 2] for q in range(4)], axis=1)
        result = jnp.dot(joined, w_down[j], preferred_element_type=f32).astype(bf16)
        share = jnp.where(
            places == row_of(seats, source, j), row_of(mixes, source, j), 0.0
        ).astype(bf16)
        total[source] += lax.dot_general(
            share, result, (((0,), (0,)), ((), ())), preferred_element_type=f32
        )

        @when((rank > 0) & (j == count - 1))
        def _():
            leave(rank)

    def tick(i, carry):
        @when(i == 1)
        def _():
            finish_sums()

        @when(i == 17)
        def _():
            relay_on(1)

        for h, at in ((1, 2), (2, 6), (3, 10)):
            @when(i == at)
            def _():
                hop(h)

        for stage_of, delay in (
            (multiply_in, 0), (activate, 2), (forward, 4), (multiply_out, 5), (add_pair, 0),
        ):
            @when((i >= delay) & (i < units + delay))
            def _():
                stage_of(i - delay)

        return carry

    lax.fori_loop(0, units + 5, tick, 0)

    relay_on(2)
    for part in range(2):
        rows = part_rows(part)
        answer = resid[rows, :].astype(f32) + total[z, rows]
        near_copy(part).wait_recv()
        answer = answer + coming[0, part].astype(f32)
        far_copy(1, part).wait_recv()
        out[rows, :] = (answer + coming[1, part].astype(f32)).astype(bf16)

    def settle(u, carry):
        for copy in tp_copies(u):
            copy.wait_send()
        return carry

    lax.fori_loop(0, units, settle, 0)
    for k in range(1, 4):
        other = lax.rem(z + k, 4)
        table_copy(0, other, z).wait_send()
        table_copy(1, other, z).wait_send()
        for part in range(2):
            near_copy(part).wait_send() if k == 3 else far_copy(k, part).wait_send()
    for h in range(3):
        hop_pair(h, lambda copy: copy.wait_send())
    for k in range(1, 4):
        doc_copy(lax.rem(z + k, 4), z).wait_send()
        sum_copy(lax.rem(lane + k, 4), lane).wait_send()
    for c in range(2):
        @when(moves)
        def _():
            swap_copy(c, z).wait_send()

        for copy in att_copies(c):
            copy.wait_send()
    for b in range(4):
        @when(z < b)
        def _():
            up_copy(b).wait_send()

        @when(z > b)
        def _():
            down_copy(b).wait_send()


def fused_layer(
    question_q, question_kv, doc_kv, doc_lens, query_docs, ctx_pos, hidden, out_proj,
    norm_gain, router_weight, w_gate_up, w_down, expert_ids,
):
    bf16 = jnp.bfloat16
    f32 = jnp.float32
    length, heads, head_dim = question_q.shape
    width = hidden.shape[1]
    experts = router_weight.shape[1]
    pool_dev, doc_max = doc_kv.shape[:2]
    count = w_gate_up.shape[0]
    inner = w_gate_up.shape[3]
    capacity = length * expert_ids.shape[1] // experts
    units = 4 * count
    quarter = inner // 4
    some = heads // 2
    vmem = pltpu.VMEM
    smem = pltpu.SMEM
    dma = pltpu.SemaphoreType.DMA
    block = (4, length, width)
    gain = norm_gain.reshape(width // 128, 128)
    router = jnp.swapaxes(router_weight, 0, 1)
    ids = jnp.swapaxes(expert_ids, 0, 1)
    return pl.pallas_call(
        layer_kernel,
        out_shape=jax.ShapeDtypeStruct((length, width), bf16),
        in_specs=[pl.BlockSpec(memory_space=pl.ANY)] * 13,
        out_specs=pl.BlockSpec(memory_space=vmem),
        scratch_shapes=[
            vmem(question_q.shape, bf16),
            vmem((length, 2, head_dim), bf16),
            vmem((pool_dev, doc_max, 2, head_dim), bf16),
            smem(doc_lens.shape, jnp.int32),
            smem(query_docs.shape, jnp.int32),
            smem(ctx_pos.shape, jnp.int32),
            vmem(hidden.shape, bf16),
            vmem(gain.shape, bf16),
            vmem(router.shape, bf16),
            vmem(ids.shape, jnp.int32),
            dma((10,)),
            vmem(out_proj.shape, bf16),
            vmem((4, 2, length, head_dim), bf16),
            vmem((4, 2, length, head_dim), bf16),
            vmem((heads, length, head_dim), bf16),
            vmem((5 * length, head_dim), bf16),
            vmem((5 * length, head_dim), bf16),
            vmem((2, some, length, head_dim), bf16),
            vmem((4, 2, some, length, head_dim), bf16),
            vmem(block, f32),
            vmem(block, bf16),
            vmem(block, bf16),
            vmem(block, bf16),
            vmem(block, bf16),
            vmem((4, experts + 8, length), f32),
            dma,
            dma((4,)),
            dma((4,)),
            dma((2,)),
            dma((2,)),
            dma((3, 2)),
            dma((3, 2)),
            dma((4,)),
            dma((4,)),
            dma((4,)),
            dma((4,)),
            dma((4,)),
            dma((4,)),
            vmem((2, width // 2, 2, inner), bf16),
            vmem((count, width, inner), bf16),
            vmem((count, width, inner), bf16),
            vmem(w_down.shape, bf16),
            vmem((length, width), bf16),
            vmem((4, 8, length), f32),
            vmem((4, 8, length), f32),
            vmem(block, bf16),
            vmem((4, 8, length), f32),
            vmem((4, 8, length), f32),
            vmem((units, 2, 2, capacity, 2 * quarter), bf16),
            vmem((units, 2, capacity, 2 * quarter), bf16),
            vmem((units, capacity, 2 * quarter), bf16),
            vmem((units, capacity, 2 * quarter), bf16),
            vmem((units, 2, 2, capacity, quarter), bf16),
            vmem(block, f32),
            vmem((4, 2, length // 2, width), bf16),
            vmem((4, 2, length // 2, width), bf16),
            vmem((2, 2, length // 2, width), bf16),
            dma((2,)),
            dma,
            dma((3,)),
            dma((3,)),
            dma((4,)),
            dma((2, 4)),
            dma((2, 4)),
            dma((5, units)),
            dma((5, units)),
            dma((4, 2)),
            dma((4, 2)),
            dma((2, 2)),
        ],
        compiler_params=pltpu.CompilerParams(
            collective_id=0, has_side_effects=True, vmem_limit_bytes=60 << 20
        ),
    )(
        question_q, question_kv, doc_kv, doc_lens, query_docs, ctx_pos, hidden, gain, router,
        ids, out_proj, w_gate_up, w_down,
    )


def feed_forward(arrived, w_gate_up, w_down):
    term = jnp.einsum("erd,edgh->hegr", arrived, w_gate_up, preferred_element_type=jnp.float32)
    summed = lax.psum_scatter(
        term.astype(jnp.bfloat16), "tp", scatter_dimension=0, tiled=True
    ).astype(jnp.float32)
    activated = (jax.nn.silu(summed[:, :, 0]) * summed[:, :, 1]).astype(jnp.bfloat16)
    piece = lax.all_gather(activated, "tp", axis=0, tiled=True)
    return jnp.einsum(
        "her,ehd->erd", piece, w_down, preferred_element_type=jnp.float32
    ).astype(jnp.bfloat16)


def per_device(
    question_q,
    question_kv,
    doc_kv,
    doc_lens,
    query_docs,
    ctx_pos,
    hidden,
    out_proj,
    norm_gain,
    router_weight,
    w_gate_up,
    w_down,
    expert_ids,
):
    lanes = lax.axis_size("tp")
    groups = lax.axis_size("ep")
    lane = lax.axis_index("tp")
    device = lax.axis_index("ep")
    length, heads_here, head_dim = question_q.shape
    kv_heads = question_kv.shape[1]
    if lanes == 4 and groups == 4:
        return fused_layer(
            question_q, question_kv, doc_kv, doc_lens, query_docs, ctx_pos, hidden, out_proj,
            norm_gain, router_weight, w_gate_up, w_down, expert_ids,
        )
    kv_pick = lane * kv_heads // lanes
    scale = head_dim ** (-0.5)
    docs_per = query_docs.shape[1]
    row_pos = lax.dynamic_index_in_dim(ctx_pos, device, 0, keepdims=False)
    question_pos = row_pos[docs_per] + jnp.arange(length, dtype=jnp.int32)
    queries = rotate(question_q, question_pos).astype(jnp.bfloat16)
    own_kv = lax.dynamic_index_in_dim(question_kv, kv_pick, 1, keepdims=False)
    own_keys = rotate(own_kv[:, 0], question_pos).astype(jnp.bfloat16)
    own_values = own_kv[:, 1]
    causal = jnp.arange(length)[:, None] >= jnp.arange(length)[None, :]
    doc_keys, doc_values, valid = fetch_context(
        doc_kv, doc_lens, query_docs, row_pos, device, kv_pick
    )
    keys = jnp.concatenate([doc_keys, own_keys], axis=0)
    values = jnp.concatenate([doc_values, own_values], axis=0)
    allowed = jnp.concatenate(
        [jnp.broadcast_to(valid[None, :], (length, valid.shape[0])), causal], axis=1
    )
    scores = jnp.einsum("ihd,jd->hij", queries, keys, preferred_element_type=jnp.float32) * scale
    scores = jnp.where(allowed[None], scores, -jnp.inf)
    ceiling = jnp.max(scores, axis=-1, keepdims=True)
    probs = jnp.exp(scores - ceiling)
    denominator = jnp.sum(probs, axis=-1, keepdims=True)
    mixed = jnp.einsum(
        "hij,jd->hid", probs.astype(jnp.bfloat16), values, preferred_element_type=jnp.float32
    )
    attended = (
        jnp.transpose(mixed / denominator, (1, 0, 2))
        .reshape(length, heads_here * head_dim)
        .astype(jnp.bfloat16)
    )
    width_here = hidden.shape[1]
    projected = project(attended, out_proj)
    residual_wide = narrow(hidden.astype(jnp.float32) + projected).astype(jnp.float32)
    gain = norm_gain.astype(jnp.float32)
    squares, logit_part = lax.psum(
        (
            jnp.sum(residual_wide * residual_wide, axis=1),
            jnp.dot(
                residual_wide * gain[None, :],
                router_weight.astype(jnp.float32),
                precision=lax.Precision.HIGHEST,
            ),
        ),
        "tp",
    )
    inv_rms = lax.rsqrt(squares / D + norm_eps)
    normed = (residual_wide * inv_rms[:, None] * gain[None, :]).astype(jnp.bfloat16)
    logits = logit_part * inv_rms[:, None]
    local_experts = w_gate_up.shape[0]
    capacity = length * expert_ids.shape[1] // (local_experts * groups)
    experts = logits.shape[1]
    chosen = jnp.any(expert_ids[:, :, None] == jnp.arange(experts, dtype=jnp.int32), axis=1)
    top = jnp.max(jnp.where(chosen, logits, -jnp.inf), axis=1, keepdims=True)
    raised = jnp.where(chosen, jnp.exp(jnp.where(chosen, logits - top, 0.0)), 0.0)
    mix = raised / jnp.sum(raised, axis=1, keepdims=True)
    mix_high = mix.astype(jnp.bfloat16)
    mix_low = (mix - mix_high.astype(jnp.float32)).astype(jnp.bfloat16)
    notes = jnp.concatenate([chosen.astype(jnp.bfloat16), mix_high, mix_low], axis=1)
    notes = jnp.pad(notes, ((0, 0), (0, -notes.shape[1] % 128)))
    packed = lax.all_gather(jnp.concatenate([normed, notes], axis=1), "ep", axis=0)
    normed_all = packed[:, :, :width_here]

    def mine(index):
        start = width_here + index * experts + device * local_experts
        return lax.dynamic_slice_in_dim(packed, start, local_experts, axis=2)

    member = mine(0) > 0
    share_high = jnp.swapaxes(mine(1), 1, 2)
    share_low = jnp.swapaxes(mine(2), 1, 2)
    earlier = jnp.arange(length)[:, None] > jnp.arange(length)[None, :]
    rank = jnp.einsum(
        "nm,sme->sen",
        earlier.astype(jnp.bfloat16),
        member.astype(jnp.bfloat16),
        preferred_element_type=jnp.float32,
    )
    seat = jnp.where(jnp.swapaxes(member, 1, 2), rank.astype(jnp.int32), -1)
    picks = (seat[:, :, None, :] == jnp.arange(capacity, dtype=jnp.int32)[:, None]).astype(
        jnp.bfloat16
    )
    arrived = jnp.einsum(
        "secn,snd->escd", picks, normed_all, preferred_element_type=jnp.float32
    ).astype(jnp.bfloat16)
    rows = groups * capacity
    arrived = arrived.reshape(local_experts, rows, width_here)
    expert_out = feed_forward(arrived, w_gate_up, w_down)
    weights = jnp.stack([picks * share_high[:, :, None, :], picks * share_low[:, :, None, :]])
    partial = jnp.einsum(
        "psecn,escd->snd",
        weights,
        expert_out.reshape(local_experts, groups, capacity, width_here),
        preferred_element_type=jnp.float32,
    )
    combined = lax.psum_scatter(
        partial.astype(jnp.bfloat16).reshape(groups * length, width_here),
        "ep",
        scatter_dimension=0,
        tiled=True,
    )
    return (residual_wide + combined.astype(jnp.float32)).astype(jnp.bfloat16)


def solution(mesh):
    placed = (
        P(("grp", "ep"), "tp", None),
        P(("grp", "ep"), None, None, None),
        P(("grp", "ep"), None, None, None, None),
        P("grp"),
        P("grp", None),
        P("grp", None),
        P(("grp", "ep"), "tp"),
        P("ep", "tp"),
        P("tp"),
        P("tp", None),
        P("ep", "tp", None, None),
        P("ep", None, "tp"),
        P(("grp", "ep"), None),
    )
    return jax.shard_map(
        per_device, mesh=mesh, in_specs=placed, out_specs=P(("grp", "ep"), "tp"), check_vma=False
    )
```

```python
import math

import jax
import jax.numpy as jnp
from jax import lax
from jax.experimental import pallas as pl
from jax.experimental.pallas import tpu as pltpu
from jax.sharding import PartitionSpec as P

D = 4096
HID = 1024


rope_theta = 1000000.0
norm_eps = 1e-06


def narrow(values):
    return lax.optimization_barrier(values.astype(jnp.bfloat16))


def rotate(values, positions):
    half = values.shape[-1] // 2
    freq = jnp.exp(
        jnp.arange(half, dtype=jnp.float32) * (-2.0 * math.log(rope_theta) / values.shape[-1])
    )
    angle = positions.astype(jnp.float32)[:, None] * freq[None, :]
    shape = (values.shape[0],) + (1,) * (values.ndim - 2) + (half,)
    cosine = jnp.cos(angle).reshape(shape)
    sine = jnp.sin(angle).reshape(shape)
    floats = values.astype(jnp.float32)
    first = floats[..., :half]
    second = floats[..., half:]
    return jnp.concatenate(
        [first * cosine - second * sine, second * cosine + first * sine], axis=-1
    )


def fetch_context(doc_kv, doc_lens, query_docs, row_pos, device, kv_pick):
    pool_dev, doc_max, kv_heads, pair, head_dim = doc_kv.shape
    docs_per = query_docs.shape[1]
    pool_head = lax.dynamic_index_in_dim(doc_kv, kv_pick, 2, keepdims=False).reshape(
        pool_dev, doc_max, pair * head_dim
    )
    held = device * pool_dev + jnp.arange(pool_dev, dtype=jnp.int32)
    wanted = jnp.sum((query_docs[:, :, None] == held[None, None, :]).astype(jnp.float32), axis=1)
    sending = jnp.einsum(
        "rl,lkc->rkc", wanted.astype(jnp.bfloat16), pool_head, preferred_element_type=jnp.float32
    ).astype(jnp.bfloat16)
    received = lax.all_to_all(sending, "ep", split_axis=0, concat_axis=0, tiled=True)
    my_docs = lax.dynamic_index_in_dim(query_docs, device, 0, keepdims=False)
    from_dev = jnp.arange(received.shape[0], dtype=jnp.int32)
    pick_dev = ((my_docs // pool_dev)[:, None] == from_dev[None, :]).astype(jnp.bfloat16)
    context = jnp.einsum(
        "jr,rkc->jkc", pick_dev, received, preferred_element_type=jnp.float32
    ).astype(jnp.bfloat16)
    every_doc = jnp.arange(doc_lens.shape[0], dtype=jnp.int32)
    lengths = jnp.sum(
        jnp.where(my_docs[:, None] == every_doc[None, :], doc_lens[None, :], 0), axis=1
    )
    positions = jnp.repeat(row_pos[:docs_per], doc_max, total_repeat_length=docs_per * doc_max)
    keys = rotate(context[:, :, :head_dim].reshape(docs_per * doc_max, head_dim), positions).astype(
        jnp.bfloat16
    )
    values = context[:, :, head_dim:].reshape(docs_per * doc_max, head_dim)
    valid = (jnp.arange(doc_max, dtype=jnp.int32)[None, :] < lengths[:, None]).reshape(
        docs_per * doc_max
    )
    return (keys, values, valid)


def project(attended, out_proj):
    lanes = lax.axis_size("tp")
    groups = lax.axis_size("ep")
    length = attended.shape[0]
    if lanes == groups:
        swap = [(e * lanes + t, t * lanes + e) for e in range(groups) for t in range(lanes)]
        block = lax.ppermute(attended, ("ep", "tp"), swap)
        tokens = lax.all_gather(block, "tp", axis=0, tiled=True)
    else:
        all_heads = lax.all_gather(attended, "tp", axis=1, tiled=True)
        split = jnp.swapaxes(all_heads.reshape(length, groups, -1), 0, 1)
        tokens = lax.all_to_all(split, "ep", split_axis=0, concat_axis=0, tiled=True)
        tokens = tokens.reshape(groups * length, -1)
    part = jnp.dot(tokens, out_proj, preferred_element_type=jnp.float32)
    summed = lax.psum_scatter(
        part.astype(jnp.bfloat16), "ep", scatter_dimension=0, tiled=True
    ).astype(jnp.float32)
    return summed


MESH = pl.DeviceIdType.MESH


def when(condition):
    return pl.when(condition)


def halves_turn(index):
    return 2 * lax.rem(index, 2) + index // 2


def source_of(z, rank):
    low = z < 2
    near = z + 1 - 2 * lax.rem(z, 2)
    inner = jnp.where(low, 2, 1)
    outer = jnp.where(low, 3, 0)
    return jnp.where(
        rank == 0, z, jnp.where(rank == 1, inner, jnp.where(rank == 2, outer, near))
    )


def unit_of(z, u):
    step = jnp.maximum(u - 2, 0)
    rank = jnp.where((u < 2) | (u >= 14), 0, lax.rem(step // 4 + 2, 3) + 1)
    j = jnp.where(u < 2, u + 2, lax.rem(step, 4))
    return rank, source_of(z, rank), j


def layer_kernel(
    q_hbm, kv_hbm, docs_hbm, lens_hbm, lists_hbm, ctx_hbm, hidden_hbm, gain_hbm, router_hbm,
    ids_hbm, wo_hbm, wgu_hbm, wd_hbm, out,
    q, own_kv, docs, lens, lists, ctx, hidden, gain, router, ids, load_sem,
    wo, sending, context, queries, keys, values, own_att, att, parts,
    go_up, go_down, from_below, from_above, sums,
    wo_sem, doc_send, doc_recv, swap_send, swap_recv, att_send, att_recv,
    up_send, up_recv, down_send, down_recv, sum_send, sum_recv,
    stage, w_gate, w_up, w_down, resid, my_seats, my_mixes, blocks, seats, mixes,
    sent, first, pair, second, acts, total, leaving, relayed, coming,
    stage_sem, down_sem, hop_up, hop_down, hop_recv, table_send, table_recv,
    tp_send, tp_recv, rs_send, relay_recv, rs_recv,
):
    bf16 = jnp.bfloat16
    f32 = jnp.float32
    z = lax.axis_index("ep")
    lane = lax.axis_index("tp")
    chip = lane // 2
    core = lane % 2
    partner = chip * 2 + (1 - core)
    across = (1 - chip) * 2 + core
    length, width = hidden.shape
    heads = q.shape[1]
    head_dim = q.shape[2]
    features = width * 4
    some = heads // own_att.shape[0]
    chunks = own_att.shape[0]

    loads = [
        pltpu.make_async_copy(source, target, load_sem.at[i])
        for i, (source, target) in enumerate(
            (
                (docs_hbm.at[:, :, lane], docs),
                (lists_hbm, lists),
                (ctx_hbm, ctx),
                (lens_hbm, lens),
                (q_hbm, q),
                (kv_hbm.at[:, lane], own_kv),
                (ids_hbm, ids),
                (hidden_hbm, hidden),
                (gain_hbm, gain),
                (router_hbm, router),
            )
        )
    ]
    for load in loads:
        load.start()
    load_wo = pltpu.make_async_copy(wo_hbm, wo, wo_sem)
    load_wo.start()
    count, inner = w_down.shape[:2]
    cap = sent.shape[3]
    quarter = acts.shape[4]
    units = 4 * count
    piece = stage.shape[1]
    pieces = inner // piece

    def load_in(i):
        rows = pl.ds((i % pieces) * piece, piece)
        return pltpu.make_async_copy(
            wgu_hbm.at[i // pieces, rows], stage.at[i % 2], stage_sem.at[i % 2]
        )

    load_in(0).start()
    load_in(1).start()
    load_down = pltpu.make_async_copy(wd_hbm, w_down, down_sem)
    load_down.start()

    def relay(i):
        load_in(i).wait()
        step = 128

        def body(k, carry):
            rows = pl.ds(pl.multiple_of(k * step, step), step)
            place = pl.ds(pl.multiple_of((i % pieces) * piece + k * step, step), step)
            block = jnp.transpose(stage[i % 2, rows], (1, 0, 2))
            w_gate[i // pieces, place, :] = block[0]
            w_up[i // pieces, place, :] = block[1]
            return carry

        lax.fori_loop(0, piece // step, body, 0)
        if i + 2 < count * pieces:
            load_in(i + 2).start()

    swap_to = {"ep": lane, "tp": halves_turn(z)}
    swap_from = {"ep": halves_turn(lane), "tp": z}
    moves = (lane != z) | (halves_turn(z) != lane)
    barrier = pltpu.get_barrier_semaphore()
    for k in range(1, 4):
        for axis, here in (("ep", z), ("tp", lane)):
            pl.semaphore_signal(
                barrier, inc=1, device_id={axis: lax.rem(here + k, 4)}, device_id_type=MESH
            )

    @when(moves)
    def _():
        for other in (swap_to, swap_from):
            pl.semaphore_signal(barrier, inc=1, device_id=other, device_id_type=MESH)

    for load in loads[:3]:
        load.wait()
    found = [jnp.transpose(docs[l], (1, 0, 2)).astype(f32) for l in range(2)]
    for r in range(4):
        shares = []
        for l in range(2):
            hit = lists[r, 0] == 2 * z + l
            for j in range(1, 4):
                hit = hit | (lists[r, j] == 2 * z + l)
            shares.append(jnp.where(hit, 1.0, 0.0).astype(f32))
        sending[r] = (found[0] * shares[0] + found[1] * shares[1]).astype(bf16)

    pl.semaphore_wait(barrier, jnp.where(moves, 8, 6))

    def doc_copy(dest, source):
        return pltpu.make_async_remote_copy(
            src_ref=sending.at[dest],
            dst_ref=context.at[source],
            send_sem=doc_send.at[dest],
            recv_sem=doc_recv.at[source],
            device_id={"ep": dest},
            device_id_type=MESH,
        )

    for k in range(1, 4):
        doc_copy(lax.rem(z + k, 4), z).start()
    context[z] = sending[z]

    def rotate_rows(rows, cosine, sine):
        return (rows * cosine + pltpu.roll(rows, head_dim // 2, 1) * sine).astype(bf16)

    for load in loads[3:]:
        load.wait()
    half = head_dim // 2
    lanes = lax.broadcasted_iota(jnp.int32, (1, head_dim), 1)
    freq = jnp.exp(
        lax.rem(lanes, half).astype(f32) * (-2.0 * math.log(rope_theta) / head_dim)
    )
    sign = jnp.where(lanes < half, -1.0, 1.0)
    steps = lax.broadcasted_iota(jnp.int32, (length, head_dim), 0)
    angle = (ctx[z, 4] + steps).astype(f32) * freq
    cosine = jnp.cos(angle)
    sine = jnp.sin(angle) * sign
    starts = []
    limits = []
    for s in range(4):
        start = jnp.int32(0)
        which = jnp.int32(0)
        for j in range(4):
            here = lists[z, j] // 2 == s
            start = start + jnp.where(here, ctx[z, j], 0)
            which = which + jnp.where(here, lists[z, j], 0)
        limit = jnp.int32(0)
        for d in range(8):
            limit = limit + jnp.where(which == d, lens[d], 0)
        starts.append(start)
        limits.append(limit)
    row = lax.broadcasted_iota(jnp.int32, (8, head_dim), 0)
    begin = jnp.zeros((8, head_dim), jnp.int32)
    for s in range(4):
        begin = jnp.where(row == s, starts[s], begin)
    doc_angle = begin.astype(f32) * freq
    doc_cosine = jnp.cos(doc_angle)
    doc_sine = jnp.sin(doc_angle) * sign
    turned = jnp.transpose(q[...], (1, 0, 2))
    for h in range(heads):
        queries[h] = rotate_rows(turned[h].astype(f32), cosine, sine)
    own = jnp.transpose(own_kv[...], (1, 0, 2))
    last = pl.ds(4 * length, length)
    keys[last, :] = rotate_rows(own[0].astype(f32), cosine, sine)
    values[last, :] = own[1]

    experts = router.shape[0]
    expert = lax.broadcasted_iota(jnp.int32, (experts, length), 0)
    picked = jnp.zeros((experts, length), f32)
    for k in range(ids.shape[0]):
        picked = picked + jnp.where(ids[k : k + 1, :] == expert, 1.0, 0.0)
    before = (
        lax.broadcasted_iota(jnp.int32, (length, length), 0)
        < lax.broadcasted_iota(jnp.int32, (length, length), 1)
    )
    rank = jnp.dot(
        picked.astype(bf16),
        jnp.where(before, 1.0, 0.0).astype(bf16),
        preferred_element_type=f32,
    )
    seat = jnp.where(picked > 0.0, rank, -1.0)
    blank = jnp.zeros((8 - count, length), f32)
    for d in range(4):
        my_seats[d] = jnp.concatenate([seat[d * count : (d + 1) * count], blank], axis=0)
    seats[z] = my_seats[z]

    def table_copy(kind, dest, source):
        mine_, theirs_ = ((my_seats, seats), (my_mixes, mixes))[kind]
        return pltpu.make_async_remote_copy(
            src_ref=mine_.at[dest],
            dst_ref=theirs_.at[source],
            send_sem=table_send.at[kind, dest],
            recv_sem=table_recv.at[kind, source],
            device_id={"ep": dest},
            device_id_type=MESH,
        )

    for k in range(1, 4):
        table_copy(0, lax.rem(z + k, 4), z).start()

    for i in range(count * pieces // 2):
        relay(i)
    for k in range(1, 4):
        source = lax.rem(z + k, 4)
        doc_copy(source, source).wait_recv()
    for s in range(4):
        row = pl.ds(s * length, length)
        keys[row, :] = rotate_rows(
            context[s, 0].astype(f32),
            doc_cosine[s : s + 1],
            doc_sine[s : s + 1],
        )
        values[row, :] = context[s, 1]

    column = lax.broadcasted_iota(jnp.int32, (length, length), 1)
    line = lax.broadcasted_iota(jnp.int32, (length, length), 0)
    scale = head_dim ** (-0.5)

    def swap_copy(c, query):
        return pltpu.make_async_remote_copy(
            src_ref=own_att.at[c],
            dst_ref=att.at[query, c],
            send_sem=swap_send.at[c],
            recv_sem=swap_recv.at[c],
            device_id=swap_to,
            device_id_type=MESH,
        )

    allowed = [
        jnp.where(column < limits[s], 0.0, -jnp.inf) for s in range(4)
    ] + [jnp.where(column <= line, 0.0, -jnp.inf)]
    bias = jnp.concatenate(allowed, axis=1)

    def one_head(c, h):
        scores = lax.dot_general(
            queries[c * some + h], keys[...], (((1,), (1,)), ((), ())),
            preferred_element_type=f32,
        )
        scores = scores * scale + bias
        ceiling = jnp.max(scores, axis=1, keepdims=True)
        probs = jnp.exp(scores - ceiling)
        denominator = jnp.sum(probs, axis=1, keepdims=True)
        mixed = jnp.dot(probs.astype(bf16), values[...], preferred_element_type=f32)
        own_att[c, h] = (mixed / denominator).astype(bf16)

    for c in range(chunks):
        for h in range(some):
            one_head(c, h)

        @when(moves)
        def _():
            swap_copy(c, z).start()

        @when(jnp.logical_not(moves))
        def _():
            att[z, c] = own_att[c]

    mine = halves_turn(lane)
    theirs = halves_turn(across)

    def att_copy(kind, c, query, other):
        return pltpu.make_async_remote_copy(
            src_ref=att.at[query, c],
            dst_ref=att.at[query, c],
            send_sem=att_send.at[kind, c],
            recv_sem=att_recv.at[kind, c],
            device_id={"tp": other},
            device_id_type=MESH,
        )

    def att_copies(c):
        return [
            att_copy(0, c, mine, across),
            att_copy(1, c, mine, partner),
            att_copy(2, c, theirs, partner),
        ]

    for i in range(count * pieces // 2, count * pieces):
        relay(i)
    for c in range(chunks):
        @when(moves)
        def _():
            swap_copy(c, mine).wait_recv()

        att_copies(c)[0].start()
        att_copies(c)[1].start()
    for c in range(chunks):
        att_copy(0, c, theirs, across).wait_recv()
        att_copies(c)[2].start()
    load_wo.wait()
    for c in range(chunks):
        att_copy(1, c, halves_turn(partner), partner).wait_recv()
        att_copy(2, c, halves_turn(3 - lane), partner).wait_recv()

    def up_copy(b, p):
        return pltpu.make_async_remote_copy(
            src_ref=go_up.at[b, p],
            dst_ref=from_below.at[b, p],
            send_sem=up_send.at[b, p],
            recv_sem=up_recv.at[b, p],
            device_id={"ep": jnp.minimum(z + 1, 3)},
            device_id_type=MESH,
        )

    def down_copy(b, p):
        return pltpu.make_async_remote_copy(
            src_ref=go_down.at[b, p],
            dst_ref=from_above.at[b, p],
            send_sem=down_send.at[b, p],
            recv_sem=down_recv.at[b, p],
            device_id={"ep": jnp.maximum(z - 1, 0)},
            device_id_type=MESH,
        )

    def band(p):
        return pl.ds(p * (length // 2), length // 2)

    def project_block(b):
        rows = jnp.concatenate([att[b, h // some, h % some] for h in range(heads)], axis=1)
        parts[b] = jnp.dot(rows, wo[...], preferred_element_type=f32)

    def send_up(b):
        for p in range(2):
            @when(z == 0)
            def _():
                go_up[b, p] = parts[b, band(p)].astype(bf16)

            @when((z > 0) & (z < b))
            def _():
                up_copy(b, p).wait_recv()
                go_up[b, p] = (parts[b, band(p)] + from_below[b, p].astype(f32)).astype(bf16)

            @when(z < b)
            def _():
                up_copy(b, p).start()

    def send_down(b):
        for p in range(2):
            @when(z == 3)
            def _():
                go_down[b, p] = parts[b, band(p)].astype(bf16)

            @when((z < 3) & (z > b))
            def _():
                down_copy(b, p).wait_recv()
                go_down[b, p] = (parts[b, band(p)] + from_above[b, p].astype(f32)).astype(bf16)

            @when(z > b)
            def _():
                down_copy(b, p).start()

    project_block(3)

    @when(z == 0)
    def _():
        send_up(3)

    project_block(0)

    @when(z == 3)
    def _():
        send_down(0)

    project_block(2)
    project_block(1)

    @when(z > 0)
    def _():
        send_up(3)

    @when(z < 3)
    def _():
        send_down(0)

    send_up(2)
    send_down(1)
    send_up(1)
    send_down(2)

    parts[z] += hidden[...].astype(f32)

    for p in range(2):
        @when(z > 0)
        def _():
            up_copy(z, p).wait_recv()
            parts[z, band(p)] += from_below[z, p].astype(f32)

        @when(z < 3)
        def _():
            down_copy(z, p).wait_recv()
            parts[z, band(p)] += from_above[z, p].astype(f32)

    residual = parts[z].astype(bf16)
    resid[...] = residual
    wide = residual.astype(f32)
    gain_rows = gain[...].astype(f32)
    gains = jnp.concatenate([gain_rows[i : i + 1] for i in range(gain.shape[0])], axis=1)
    raised = wide * gains
    blocks[z] = raised.astype(bf16)

    def hop_copy(source, dest, sem):
        return pltpu.make_async_remote_copy(
            src_ref=blocks.at[source],
            dst_ref=blocks.at[source],
            send_sem=sem,
            recv_sem=hop_recv.at[source],
            device_id={"ep": dest},
            device_id_type=MESH,
        )

    def hop_pair(h, act_on):
        @when((z - h >= 0) & (z < 3))
        def _():
            act_on(hop_copy(jnp.maximum(z - h, 0), jnp.minimum(z + 1, 3), hop_up.at[h]))

        @when((z + h <= 3) & (z > 0))
        def _():
            act_on(hop_copy(jnp.minimum(z + h, 3), jnp.maximum(z - 1, 0), hop_down.at[h]))

    def hop(h):
        if h > 0:
            for off in (-h, h):
                source = z + off

                @when((source >= 0) & (source <= 3))
                def _():
                    hop_copy(source, source, hop_up.at[0]).wait_recv()

        if h < 3:
            hop_pair(h, lambda copy: copy.start())

    hop(0)
    def sum_copy(dest, source):
        return pltpu.make_async_remote_copy(
            src_ref=sums.at[source],
            dst_ref=sums.at[source],
            send_sem=sum_send.at[dest],
            recv_sem=sum_recv.at[source],
            device_id={"tp": dest},
            device_id_type=MESH,
        )

    def start_sums():
        wide = resid[...].astype(f32)
        raised = wide * gains
        logit_part = lax.dot_general(
            router[...].astype(f32), raised, (((1,), (1,)), ((), ())),
            precision=lax.Precision.HIGHEST, preferred_element_type=f32,
        )
        square_part = lax.dot_general(
            jnp.ones((8, width), f32), wide * wide, (((1,), (1,)), ((), ())),
            precision=lax.Precision.HIGHEST, preferred_element_type=f32,
        )
        sums[lane] = jnp.concatenate([logit_part, square_part], axis=0)
        for k in range(1, 4):
            sum_copy(lax.rem(lane + k, 4), lane).start()

    total[...] = jnp.zeros_like(total)
    load_down.wait()

    def finish_sums():
        for k in range(1, 4):
            source = lax.rem(lane + k, 4)
            sum_copy(source, source).wait_recv()
        added = (sums[0] + sums[1]) + (sums[2] + sums[3])
        inverse = lax.rsqrt(added[experts : experts + 1] / features + norm_eps)
        logits = added[:experts] * inverse
        inside = picked > 0.0
        top = jnp.max(jnp.where(inside, logits, -jnp.inf), axis=0, keepdims=True)
        lifted = jnp.where(inside, jnp.exp(jnp.where(inside, logits - top, 0.0)), 0.0)
        mix = lifted / jnp.sum(lifted, axis=0, keepdims=True)
        rest = jnp.broadcast_to(inverse, (8 - count, length))
        for d in range(4):
            my_mixes[d] = jnp.concatenate([mix[d * count : (d + 1) * count], rest], axis=0)
        mixes[z] = my_mixes[z]
        for k in range(1, 4):
            table_copy(1, lax.rem(z + k, 4), z).start()

    def remote(kind, u, source, target, other):
        return pltpu.make_async_remote_copy(
            src_ref=source,
            dst_ref=target,
            send_sem=tp_send.at[kind, u],
            recv_sem=tp_recv.at[kind, u],
            device_id={"tp": other},
            device_id_type=MESH,
        )

    def tp_copies(u):
        return [
            remote(0, u, sent.at[u, 1 - core], first.at[u], partner),
            remote(1, u, pair.at[u], second.at[u], across),
            remote(2, u, acts.at[u, core, chip], acts.at[u, core, chip], across),
            remote(3, u, acts.at[u, core, chip], acts.at[u, core, chip], partner),
            remote(4, u, acts.at[u, core, 1 - chip], acts.at[u, core, 1 - chip], partner),
        ]

    outside = (z == 0) | (z == 3)
    rows_half = length // 4

    def near_copy(part):
        return pltpu.make_async_remote_copy(
            src_ref=leaving.at[3, part],
            dst_ref=coming.at[0, part],
            send_sem=rs_send.at[3, part],
            recv_sem=rs_recv.at[0, part],
            device_id={"ep": source_of(z, 3)},
            device_id_type=MESH,
        )

    def relay_copy(rank, part):
        return pltpu.make_async_remote_copy(
            src_ref=leaving.at[rank, part],
            dst_ref=relayed.at[rank, part],
            send_sem=rs_send.at[rank, part],
            recv_sem=relay_recv.at[rank, part],
            device_id={"ep": source_of(z, 3)},
            device_id_type=MESH,
        )

    def far_copy(rank, part):
        return pltpu.make_async_remote_copy(
            src_ref=leaving.at[rank, part],
            dst_ref=coming.at[1, part],
            send_sem=rs_send.at[rank, part],
            recv_sem=rs_recv.at[1, part],
            device_id={"ep": source_of(z, rank)},
            device_id_type=MESH,
        )

    def part_rows(part):
        return pl.ds(part * rows_half, rows_half)

    def leave(rank):
        source = source_of(z, rank)

        @when((rank == 3) | outside)
        def _():
            for part in range(4):
                leaving[rank, part] = total[source, part_rows(part)].astype(bf16)

        @when(rank == 3)
        def _():
            for part in range(4):
                near_copy(part).start()

        @when((rank < 3) & outside)
        def _():
            for part in range(4):
                relay_copy(rank, part).start()

    def relay_on(rank):
        source = source_of(z, rank)

        @when(jnp.logical_not(outside))
        def _():
            for part in range(4):
                relay_copy(rank, part).wait_recv()
                leaving[rank, part] = (
                    total[source, part_rows(part)] + relayed[rank, part].astype(f32)
                ).astype(bf16)
                far_copy(rank, part).start()

    def row_of(tables, source, row):
        table = tables[source]
        rows = lax.broadcasted_iota(jnp.int32, table.shape, 0)
        return jnp.sum(jnp.where(rows == row, table, 0.0), axis=0, keepdims=True)

    places = lax.broadcasted_iota(jnp.int32, (cap, length), 0).astype(f32)

    def multiply_in(u):
        rank, source, j = unit_of(z, u)

        @when((rank > 0) & (j == 0))
        def _():
            table_copy(0, source, source).wait_recv()

        pick = (places == row_of(seats, source, j)).astype(bf16)
        rows = jnp.dot(pick, blocks[source], preferred_element_type=f32).astype(bf16)
        for kind, weights in enumerate((w_gate, w_up)):
            part = jnp.dot(rows, weights[j], preferred_element_type=f32).astype(bf16)
            for q in range(4):
                sent[u, q % 2, q // 2, :, kind * quarter : (kind + 1) * quarter] = part[
                    :, q * quarter : (q + 1) * quarter
                ]
        tp_copies(u)[0].start()

    def add_pair(u):
        copies = tp_copies(u)
        copies[0].wait_recv()
        both = sent[u, core, 1 - chip].astype(f32) + first[u, 1 - chip].astype(f32)
        pair[u] = both.astype(bf16)
        copies[1].start()

    def activate(u):
        rank, source, j = unit_of(z, u)

        @when((rank > 0) & (j == 0))
        def _():
            table_copy(1, source, source).wait_recv()

        scale_row = row_of(mixes, source, count)
        factor = jnp.sum(
            jnp.where(places == row_of(seats, source, j), scale_row, 0.0), axis=1, keepdims=True
        )
        copies = tp_copies(u)
        copies[1].wait_recv()
        value = (
            sent[u, core, chip].astype(f32)
            + first[u, chip].astype(f32)
            + second[u].astype(f32)
        ) * factor
        gate = value[:, :quarter]
        acts[u, core, chip] = (gate / (1.0 + jnp.exp(-gate)) * value[:, quarter:]).astype(bf16)
        copies[2].start()
        copies[3].start()

    def forward(u):
        copies = tp_copies(u)
        copies[2].wait_recv()
        copies[4].start()

    def multiply_out(u):
        rank, source, j = unit_of(z, u)
        copies = tp_copies(u)
        copies[3].wait_recv()
        copies[4].wait_recv()

        joined = jnp.concatenate([acts[u, q % 2, q // 2] for q in range(4)], axis=1)
        result = jnp.dot(joined, w_down[j], preferred_element_type=f32).astype(bf16)
        share = jnp.where(
            places == row_of(seats, source, j), row_of(mixes, source, j), 0.0
        ).astype(bf16)
        total[source] += lax.dot_general(
            share, result, (((0,), (0,)), ((), ())), preferred_element_type=f32
        )

        @when((rank > 0) & (j == count - 1))
        def _():
            leave(rank)

    def tick(i, carry):
        @when(i == 2)
        def _():
            finish_sums()

        @when(i == 17)
        def _():
            relay_on(1)

        for h, at in ((1, 2), (2, 6), (3, 10)):
            @when(i == at)
            def _():
                hop(h)

        for stage_of, delay in (
            (multiply_in, 0), (activate, 2), (forward, 4), (multiply_out, 5), (add_pair, 0),
        ):
            @when((i >= delay) & (i < units + delay))
            def _():
                stage_of(i - delay)

        @when(i == 0)
        def _():
            start_sums()

        return carry

    lax.fori_loop(0, units + 5, tick, 0)

    relay_on(2)
    for part in range(4):
        rows = part_rows(part)
        answer = resid[rows, :].astype(f32) + total[z, rows]
        near_copy(part).wait_recv()
        answer = answer + coming[0, part].astype(f32)
        far_copy(1, part).wait_recv()
        out[rows, :] = (answer + coming[1, part].astype(f32)).astype(bf16)

    def settle(u, carry):
        for copy in tp_copies(u):
            copy.wait_send()
        return carry

    lax.fori_loop(0, units, settle, 0)
    for k in range(1, 4):
        other = lax.rem(z + k, 4)
        table_copy(0, other, z).wait_send()
        table_copy(1, other, z).wait_send()
        for part in range(4):
            near_copy(part).wait_send() if k == 3 else far_copy(k, part).wait_send()
    for h in range(3):
        hop_pair(h, lambda copy: copy.wait_send())
    for k in range(1, 4):
        doc_copy(lax.rem(z + k, 4), z).wait_send()
        sum_copy(lax.rem(lane + k, 4), lane).wait_send()
    for c in range(chunks):
        @when(moves)
        def _():
            swap_copy(c, z).wait_send()

        for copy in att_copies(c):
            copy.wait_send()
    for b in range(4):
        for p in range(2):
            @when(z < b)
            def _():
                up_copy(b, p).wait_send()

            @when(z > b)
            def _():
                down_copy(b, p).wait_send()


def fused_layer(
    question_q, question_kv, doc_kv, doc_lens, query_docs, ctx_pos, hidden, out_proj,
    norm_gain, router_weight, w_gate_up, w_down, expert_ids,
):
    bf16 = jnp.bfloat16
    f32 = jnp.float32
    length, heads, head_dim = question_q.shape
    width = hidden.shape[1]
    experts = router_weight.shape[1]
    pool_dev, doc_max = doc_kv.shape[:2]
    count = w_gate_up.shape[0]
    inner = w_gate_up.shape[3]
    capacity = length * expert_ids.shape[1] // experts
    units = 4 * count
    quarter = inner // 4
    chunks = 4
    some = heads // chunks
    vmem = pltpu.VMEM
    smem = pltpu.SMEM
    dma = pltpu.SemaphoreType.DMA
    block = (4, length, width)
    gain = norm_gain.reshape(width // 128, 128)
    router = jnp.swapaxes(router_weight, 0, 1)
    ids = jnp.swapaxes(expert_ids, 0, 1)
    return pl.pallas_call(
        layer_kernel,
        out_shape=jax.ShapeDtypeStruct((length, width), bf16),
        in_specs=[pl.BlockSpec(memory_space=pl.ANY)] * 13,
        out_specs=pl.BlockSpec(memory_space=vmem),
        scratch_shapes=[
            vmem(question_q.shape, bf16),
            vmem((length, 2, head_dim), bf16),
            vmem((pool_dev, doc_max, 2, head_dim), bf16),
            smem(doc_lens.shape, jnp.int32),
            smem(query_docs.shape, jnp.int32),
            smem(ctx_pos.shape, jnp.int32),
            vmem(hidden.shape, bf16),
            vmem(gain.shape, bf16),
            vmem(router.shape, bf16),
            vmem(ids.shape, jnp.int32),
            dma((10,)),
            vmem(out_proj.shape, bf16),
            vmem((4, 2, length, head_dim), bf16),
            vmem((4, 2, length, head_dim), bf16),
            vmem((heads, length, head_dim), bf16),
            vmem((5 * length, head_dim), bf16),
            vmem((5 * length, head_dim), bf16),
            vmem((chunks, some, length, head_dim), bf16),
            vmem((4, chunks, some, length, head_dim), bf16),
            vmem(block, f32),
            vmem((4, 2, length // 2, width), bf16),
            vmem((4, 2, length // 2, width), bf16),
            vmem((4, 2, length // 2, width), bf16),
            vmem((4, 2, length // 2, width), bf16),
            vmem((4, experts + 8, length), f32),
            dma,
            dma((4,)),
            dma((4,)),
            dma((chunks,)),
            dma((chunks,)),
            dma((3, chunks)),
            dma((3, chunks)),
            dma((4, 2)),
            dma((4, 2)),
            dma((4, 2)),
            dma((4, 2)),
            dma((4,)),
            dma((4,)),
            vmem((2, width // 2, 2, inner), bf16),
            vmem((count, width, inner), bf16),
            vmem((count, width, inner), bf16),
            vmem(w_down.shape, bf16),
            vmem((length, width), bf16),
            vmem((4, 8, length), f32),
            vmem((4, 8, length), f32),
            vmem(block, bf16),
            vmem((4, 8, length), f32),
            vmem((4, 8, length), f32),
            vmem((units, 2, 2, capacity, 2 * quarter), bf16),
            vmem((units, 2, capacity, 2 * quarter), bf16),
            vmem((units, capacity, 2 * quarter), bf16),
            vmem((units, capacity, 2 * quarter), bf16),
            vmem((units, 2, 2, capacity, quarter), bf16),
            vmem(block, f32),
            vmem((4, 4, length // 4, width), bf16),
            vmem((4, 4, length // 4, width), bf16),
            vmem((2, 4, length // 4, width), bf16),
            dma((2,)),
            dma,
            dma((3,)),
            dma((3,)),
            dma((4,)),
            dma((2, 4)),
            dma((2, 4)),
            dma((5, units)),
            dma((5, units)),
            dma((4, 4)),
            dma((4, 4)),
            dma((2, 4)),
        ],
        compiler_params=pltpu.CompilerParams(
            collective_id=0, has_side_effects=True, vmem_limit_bytes=60 << 20
        ),
    )(
        question_q, question_kv, doc_kv, doc_lens, query_docs, ctx_pos, hidden, gain, router,
        ids, out_proj, w_gate_up, w_down,
    )


def feed_forward(arrived, w_gate_up, w_down):
    term = jnp.einsum("erd,edgh->hegr", arrived, w_gate_up, preferred_element_type=jnp.float32)
    summed = lax.psum_scatter(
        term.astype(jnp.bfloat16), "tp", scatter_dimension=0, tiled=True
    ).astype(jnp.float32)
    activated = (jax.nn.silu(summed[:, :, 0]) * summed[:, :, 1]).astype(jnp.bfloat16)
    piece = lax.all_gather(activated, "tp", axis=0, tiled=True)
    return jnp.einsum(
        "her,ehd->erd", piece, w_down, preferred_element_type=jnp.float32
    ).astype(jnp.bfloat16)


def per_device(
    question_q,
    question_kv,
    doc_kv,
    doc_lens,
    query_docs,
    ctx_pos,
    hidden,
    out_proj,
    norm_gain,
    router_weight,
    w_gate_up,
    w_down,
    expert_ids,
):
    lanes = lax.axis_size("tp")
    groups = lax.axis_size("ep")
    lane = lax.axis_index("tp")
    device = lax.axis_index("ep")
    length, heads_here, head_dim = question_q.shape
    kv_heads = question_kv.shape[1]
    if lanes == 4 and groups == 4:
        return fused_layer(
            question_q, question_kv, doc_kv, doc_lens, query_docs, ctx_pos, hidden, out_proj,
            norm_gain, router_weight, w_gate_up, w_down, expert_ids,
        )
    kv_pick = lane * kv_heads // lanes
    scale = head_dim ** (-0.5)
    docs_per = query_docs.shape[1]
    row_pos = lax.dynamic_index_in_dim(ctx_pos, device, 0, keepdims=False)
    question_pos = row_pos[docs_per] + jnp.arange(length, dtype=jnp.int32)
    queries = rotate(question_q, question_pos).astype(jnp.bfloat16)
    own_kv = lax.dynamic_index_in_dim(question_kv, kv_pick, 1, keepdims=False)
    own_keys = rotate(own_kv[:, 0], question_pos).astype(jnp.bfloat16)
    own_values = own_kv[:, 1]
    causal = jnp.arange(length)[:, None] >= jnp.arange(length)[None, :]
    doc_keys, doc_values, valid = fetch_context(
        doc_kv, doc_lens, query_docs, row_pos, device, kv_pick
    )
    keys = jnp.concatenate([doc_keys, own_keys], axis=0)
    values = jnp.concatenate([doc_values, own_values], axis=0)
    allowed = jnp.concatenate(
        [jnp.broadcast_to(valid[None, :], (length, valid.shape[0])), causal], axis=1
    )
    scores = jnp.einsum("ihd,jd->hij", queries, keys, preferred_element_type=jnp.float32) * scale
    scores = jnp.where(allowed[None], scores, -jnp.inf)
    ceiling = jnp.max(scores, axis=-1, keepdims=True)
    probs = jnp.exp(scores - ceiling)
    denominator = jnp.sum(probs, axis=-1, keepdims=True)
    mixed = jnp.einsum(
        "hij,jd->hid", probs.astype(jnp.bfloat16), values, preferred_element_type=jnp.float32
    )
    attended = (
        jnp.transpose(mixed / denominator, (1, 0, 2))
        .reshape(length, heads_here * head_dim)
        .astype(jnp.bfloat16)
    )
    width_here = hidden.shape[1]
    projected = project(attended, out_proj)
    residual_wide = narrow(hidden.astype(jnp.float32) + projected).astype(jnp.float32)
    gain = norm_gain.astype(jnp.float32)
    squares, logit_part = lax.psum(
        (
            jnp.sum(residual_wide * residual_wide, axis=1),
            jnp.dot(
                residual_wide * gain[None, :],
                router_weight.astype(jnp.float32),
                precision=lax.Precision.HIGHEST,
            ),
        ),
        "tp",
    )
    inv_rms = lax.rsqrt(squares / D + norm_eps)
    normed = (residual_wide * inv_rms[:, None] * gain[None, :]).astype(jnp.bfloat16)
    logits = logit_part * inv_rms[:, None]
    local_experts = w_gate_up.shape[0]
    capacity = length * expert_ids.shape[1] // (local_experts * groups)
    experts = logits.shape[1]
    chosen = jnp.any(expert_ids[:, :, None] == jnp.arange(experts, dtype=jnp.int32), axis=1)
    top = jnp.max(jnp.where(chosen, logits, -jnp.inf), axis=1, keepdims=True)
    raised = jnp.where(chosen, jnp.exp(jnp.where(chosen, logits - top, 0.0)), 0.0)
    mix = raised / jnp.sum(raised, axis=1, keepdims=True)
    mix_high = mix.astype(jnp.bfloat16)
    mix_low = (mix - mix_high.astype(jnp.float32)).astype(jnp.bfloat16)
    notes = jnp.concatenate([chosen.astype(jnp.bfloat16), mix_high, mix_low], axis=1)
    notes = jnp.pad(notes, ((0, 0), (0, -notes.shape[1] % 128)))
    packed = lax.all_gather(jnp.concatenate([normed, notes], axis=1), "ep", axis=0)
    normed_all = packed[:, :, :width_here]

    def mine(index):
        start = width_here + index * experts + device * local_experts
        return lax.dynamic_slice_in_dim(packed, start, local_experts, axis=2)

    member = mine(0) > 0
    share_high = jnp.swapaxes(mine(1), 1, 2)
    share_low = jnp.swapaxes(mine(2), 1, 2)
    earlier = jnp.arange(length)[:, None] > jnp.arange(length)[None, :]
    rank = jnp.einsum(
        "nm,sme->sen",
        earlier.astype(jnp.bfloat16),
        member.astype(jnp.bfloat16),
        preferred_element_type=jnp.float32,
    )
    seat = jnp.where(jnp.swapaxes(member, 1, 2), rank.astype(jnp.int32), -1)
    picks = (seat[:, :, None, :] == jnp.arange(capacity, dtype=jnp.int32)[:, None]).astype(
        jnp.bfloat16
    )
    arrived = jnp.einsum(
        "secn,snd->escd", picks, normed_all, preferred_element_type=jnp.float32
    ).astype(jnp.bfloat16)
    rows = groups * capacity
    arrived = arrived.reshape(local_experts, rows, width_here)
    expert_out = feed_forward(arrived, w_gate_up, w_down)
    weights = jnp.stack([picks * share_high[:, :, None, :], picks * share_low[:, :, None, :]])
    partial = jnp.einsum(
        "psecn,escd->snd",
        weights,
        expert_out.reshape(local_experts, groups, capacity, width_here),
        preferred_element_type=jnp.float32,
    )
    combined = lax.psum_scatter(
        partial.astype(jnp.bfloat16).reshape(groups * length, width_here),
        "ep",
        scatter_dimension=0,
        tiled=True,
    )
    return (residual_wide + combined.astype(jnp.float32)).astype(jnp.bfloat16)


def solution(mesh):
    placed = (
        P(("grp", "ep"), "tp", None),
        P(("grp", "ep"), None, None, None),
        P(("grp", "ep"), None, None, None, None),
        P("grp"),
        P("grp", None),
        P("grp", None),
        P(("grp", "ep"), "tp"),
        P("ep", "tp"),
        P("tp"),
        P("tp", None),
        P("ep", "tp", None, None),
        P("ep", None, "tp"),
        P(("grp", "ep"), None),
    )
    return jax.shard_map(
        per_device, mesh=mesh, in_specs=placed, out_specs=P(("grp", "ep"), "tp"), check_vma=False
    )
```

```python
import math

import jax
import jax.numpy as jnp
from jax import lax
from jax.experimental import pallas as pl
from jax.experimental.pallas import tpu as pltpu
from jax.sharding import PartitionSpec as P

D = 4096
HID = 1024


rope_theta = 1000000.0
norm_eps = 1e-06


def narrow(values):
    return lax.optimization_barrier(values.astype(jnp.bfloat16))


def rotate(values, positions):
    half = values.shape[-1] // 2
    freq = jnp.exp(
        jnp.arange(half, dtype=jnp.float32) * (-2.0 * math.log(rope_theta) / values.shape[-1])
    )
    angle = positions.astype(jnp.float32)[:, None] * freq[None, :]
    shape = (values.shape[0],) + (1,) * (values.ndim - 2) + (half,)
    cosine = jnp.cos(angle).reshape(shape)
    sine = jnp.sin(angle).reshape(shape)
    floats = values.astype(jnp.float32)
    first = floats[..., :half]
    second = floats[..., half:]
    return jnp.concatenate(
        [first * cosine - second * sine, second * cosine + first * sine], axis=-1
    )


def fetch_context(doc_kv, doc_lens, query_docs, row_pos, device, kv_pick):
    pool_dev, doc_max, kv_heads, pair, head_dim = doc_kv.shape
    docs_per = query_docs.shape[1]
    pool_head = lax.dynamic_index_in_dim(doc_kv, kv_pick, 2, keepdims=False).reshape(
        pool_dev, doc_max, pair * head_dim
    )
    held = device * pool_dev + jnp.arange(pool_dev, dtype=jnp.int32)
    wanted = jnp.sum((query_docs[:, :, None] == held[None, None, :]).astype(jnp.float32), axis=1)
    sending = jnp.einsum(
        "rl,lkc->rkc", wanted.astype(jnp.bfloat16), pool_head, preferred_element_type=jnp.float32
    ).astype(jnp.bfloat16)
    received = lax.all_to_all(sending, "ep", split_axis=0, concat_axis=0, tiled=True)
    my_docs = lax.dynamic_index_in_dim(query_docs, device, 0, keepdims=False)
    from_dev = jnp.arange(received.shape[0], dtype=jnp.int32)
    pick_dev = ((my_docs // pool_dev)[:, None] == from_dev[None, :]).astype(jnp.bfloat16)
    context = jnp.einsum(
        "jr,rkc->jkc", pick_dev, received, preferred_element_type=jnp.float32
    ).astype(jnp.bfloat16)
    every_doc = jnp.arange(doc_lens.shape[0], dtype=jnp.int32)
    lengths = jnp.sum(
        jnp.where(my_docs[:, None] == every_doc[None, :], doc_lens[None, :], 0), axis=1
    )
    positions = jnp.repeat(row_pos[:docs_per], doc_max, total_repeat_length=docs_per * doc_max)
    keys = rotate(context[:, :, :head_dim].reshape(docs_per * doc_max, head_dim), positions).astype(
        jnp.bfloat16
    )
    values = context[:, :, head_dim:].reshape(docs_per * doc_max, head_dim)
    valid = (jnp.arange(doc_max, dtype=jnp.int32)[None, :] < lengths[:, None]).reshape(
        docs_per * doc_max
    )
    return (keys, values, valid)


def project(attended, out_proj):
    lanes = lax.axis_size("tp")
    groups = lax.axis_size("ep")
    length = attended.shape[0]
    if lanes == groups:
        swap = [(e * lanes + t, t * lanes + e) for e in range(groups) for t in range(lanes)]
        block = lax.ppermute(attended, ("ep", "tp"), swap)
        tokens = lax.all_gather(block, "tp", axis=0, tiled=True)
    else:
        all_heads = lax.all_gather(attended, "tp", axis=1, tiled=True)
        split = jnp.swapaxes(all_heads.reshape(length, groups, -1), 0, 1)
        tokens = lax.all_to_all(split, "ep", split_axis=0, concat_axis=0, tiled=True)
        tokens = tokens.reshape(groups * length, -1)
    part = jnp.dot(tokens, out_proj, preferred_element_type=jnp.float32)
    summed = lax.psum_scatter(
        part.astype(jnp.bfloat16), "ep", scatter_dimension=0, tiled=True
    ).astype(jnp.float32)
    return summed


MESH = pl.DeviceIdType.MESH


def when(condition):
    return pl.when(condition)


def seat_of(query, plane):
    return 2 * lax.rem(query + plane, 2) + query // 2


def query_at(plane, lane):
    return 2 * lax.rem(lane, 2) + lax.rem(lane // 2 + plane, 2)


def source_of(z, rank):
    low = z < 2
    near = z + 1 - 2 * lax.rem(z, 2)
    inner = jnp.where(low, 2, 1)
    outer = jnp.where(low, 3, 0)
    return jnp.where(
        rank == 0, z, jnp.where(rank == 1, inner, jnp.where(rank == 2, outer, near))
    )


def unit_of(z, u):
    step = jnp.maximum(u - 3, 0)
    rank = jnp.where((u < 3) | (u >= 15), 0, lax.rem(step // 4 + 2, 3) + 1)
    j = jnp.where(u < 3, u + 1, lax.rem(step, 4))
    return rank, source_of(z, rank), j


def layer_kernel(
    q_hbm, kv_hbm, docs_hbm, lens_hbm, lists_hbm, ctx_hbm, hidden_hbm, gain_hbm, router_hbm,
    ids_hbm, wo_hbm, wgu_hbm, wd_hbm, out,
    q, own_kv, docs, lens, lists, ctx, hidden, gain, router, ids, load_sem,
    wo, sending, context, queries, keys, values, own_att, att, parts,
    go_up, go_down, from_below, from_above, sums,
    wo_sem, doc_send, doc_recv, swap_send, swap_recv, att_send, att_recv,
    up_send, up_recv, down_send, down_recv, sum_send, sum_recv,
    stage, w_gate, w_up, w_down, resid, my_seats, my_mixes, blocks, seats, mixes,
    sent, first, pair, second, acts, total, leaving, relayed, coming,
    stage_sem, down_sem, hop_up, hop_down, hop_recv, table_send, table_recv,
    tp_send, tp_recv, rs_send, relay_recv, rs_recv,
):
    bf16 = jnp.bfloat16
    f32 = jnp.float32
    z = lax.axis_index("ep")
    lane = lax.axis_index("tp")
    chip = lane // 2
    core = lane % 2
    partner = chip * 2 + (1 - core)
    across = (1 - chip) * 2 + core
    length, width = hidden.shape
    heads = q.shape[1]
    head_dim = q.shape[2]
    features = width * 4
    some = heads // own_att.shape[0]
    chunks = own_att.shape[0]

    loads = [
        pltpu.make_async_copy(source, target, load_sem.at[i])
        for i, (source, target) in enumerate(
            (
                (docs_hbm.at[:, :, lane], docs),
                (lists_hbm, lists),
                (ctx_hbm, ctx),
                (lens_hbm, lens),
                (q_hbm, q),
                (kv_hbm.at[:, lane], own_kv),
                (ids_hbm, ids),
                (hidden_hbm, hidden),
                (gain_hbm, gain),
                (router_hbm, router),
            )
        )
    ]
    for load in loads:
        load.start()
    load_wo = pltpu.make_async_copy(wo_hbm, wo, wo_sem)
    load_wo.start()
    count, inner = w_down.shape[:2]
    cap = sent.shape[3]
    quarter = acts.shape[4]
    units = 4 * count
    piece = stage.shape[1]
    pieces = inner // piece

    def load_in(i):
        rows = pl.ds((i % pieces) * piece, piece)
        return pltpu.make_async_copy(
            wgu_hbm.at[i // pieces, rows], stage.at[i % 2], stage_sem.at[i % 2]
        )

    load_in(0).start()
    load_in(1).start()
    load_down = pltpu.make_async_copy(wd_hbm, w_down, down_sem)
    load_down.start()

    def relay(i):
        load_in(i).wait()
        step = 128

        def body(k, carry):
            rows = pl.ds(pl.multiple_of(k * step, step), step)
            place = pl.ds(pl.multiple_of((i % pieces) * piece + k * step, step), step)
            block = jnp.transpose(stage[i % 2, rows], (1, 0, 2))
            w_gate[i // pieces, place, :] = block[0]
            w_up[i // pieces, place, :] = block[1]
            return carry

        lax.fori_loop(0, piece // step, body, 0)
        if i + 2 < count * pieces:
            load_in(i + 2).start()

    swap_to = {"ep": lane, "tp": seat_of(z, lane)}
    swap_from = {"ep": query_at(z, lane), "tp": z}
    moves = (lane != z) | (seat_of(z, lane) != lane)
    barrier = pltpu.get_barrier_semaphore()
    for k in range(1, 4):
        for axis, here in (("ep", z), ("tp", lane)):
            pl.semaphore_signal(
                barrier, inc=1, device_id={axis: lax.rem(here + k, 4)}, device_id_type=MESH
            )

    @when(moves)
    def _():
        for other in (swap_to, swap_from):
            pl.semaphore_signal(barrier, inc=1, device_id=other, device_id_type=MESH)

    for load in loads[:3]:
        load.wait()
    found = [jnp.transpose(docs[l], (1, 0, 2)).astype(f32) for l in range(2)]
    for r in range(4):
        shares = []
        for l in range(2):
            hit = lists[r, 0] == 2 * z + l
            for j in range(1, 4):
                hit = hit | (lists[r, j] == 2 * z + l)
            shares.append(jnp.where(hit, 1.0, 0.0).astype(f32))
        sending[r] = (found[0] * shares[0] + found[1] * shares[1]).astype(bf16)

    pl.semaphore_wait(barrier, jnp.where(moves, 8, 6))

    def doc_copy(dest, source):
        return pltpu.make_async_remote_copy(
            src_ref=sending.at[dest],
            dst_ref=context.at[source],
            send_sem=doc_send.at[dest],
            recv_sem=doc_recv.at[source],
            device_id={"ep": dest},
            device_id_type=MESH,
        )

    for k in range(1, 4):
        doc_copy(lax.rem(z + k, 4), z).start()
    context[z] = sending[z]

    def rotate_rows(rows, cosine, sine):
        return (rows * cosine + pltpu.roll(rows, head_dim // 2, 1) * sine).astype(bf16)

    for load in loads[3:]:
        load.wait()
    half = head_dim // 2
    lanes = lax.broadcasted_iota(jnp.int32, (1, head_dim), 1)
    freq = jnp.exp(
        lax.rem(lanes, half).astype(f32) * (-2.0 * math.log(rope_theta) / head_dim)
    )
    sign = jnp.where(lanes < half, -1.0, 1.0)
    steps = lax.broadcasted_iota(jnp.int32, (length, head_dim), 0)
    angle = (ctx[z, 4] + steps).astype(f32) * freq
    cosine = jnp.cos(angle)
    sine = jnp.sin(angle) * sign
    starts = []
    limits = []
    for s in range(4):
        start = jnp.int32(0)
        which = jnp.int32(0)
        for j in range(4):
            here = lists[z, j] // 2 == s
            start = start + jnp.where(here, ctx[z, j], 0)
            which = which + jnp.where(here, lists[z, j], 0)
        limit = jnp.int32(0)
        for d in range(8):
            limit = limit + jnp.where(which == d, lens[d], 0)
        starts.append(start)
        limits.append(limit)
    row = lax.broadcasted_iota(jnp.int32, (8, head_dim), 0)
    begin = jnp.zeros((8, head_dim), jnp.int32)
    for s in range(4):
        begin = jnp.where(row == s, starts[s], begin)
    doc_angle = begin.astype(f32) * freq
    doc_cosine = jnp.cos(doc_angle)
    doc_sine = jnp.sin(doc_angle) * sign
    turned = jnp.transpose(q[...], (1, 0, 2))
    for h in range(heads):
        queries[h] = rotate_rows(turned[h].astype(f32), cosine, sine)
    own = jnp.transpose(own_kv[...], (1, 0, 2))
    last = pl.ds(4 * length, length)
    keys[last, :] = rotate_rows(own[0].astype(f32), cosine, sine)
    values[last, :] = own[1]

    experts = router.shape[0]
    expert = lax.broadcasted_iota(jnp.int32, (experts, length), 0)
    picked = jnp.zeros((experts, length), f32)
    for k in range(ids.shape[0]):
        picked = picked + jnp.where(ids[k : k + 1, :] == expert, 1.0, 0.0)
    before = (
        lax.broadcasted_iota(jnp.int32, (length, length), 0)
        < lax.broadcasted_iota(jnp.int32, (length, length), 1)
    )
    rank = jnp.dot(
        picked.astype(bf16),
        jnp.where(before, 1.0, 0.0).astype(bf16),
        preferred_element_type=f32,
    )
    seat = jnp.where(picked > 0.0, rank, -1.0)
    blank = jnp.zeros((8 - count, length), f32)
    for d in range(4):
        my_seats[d] = jnp.concatenate([seat[d * count : (d + 1) * count], blank], axis=0)
    seats[z] = my_seats[z]

    def table_copy(kind, dest, source):
        mine_, theirs_ = ((my_seats, seats), (my_mixes, mixes))[kind]
        return pltpu.make_async_remote_copy(
            src_ref=mine_.at[dest],
            dst_ref=theirs_.at[source],
            send_sem=table_send.at[kind, dest],
            recv_sem=table_recv.at[kind, source],
            device_id={"ep": dest},
            device_id_type=MESH,
        )

    for k in range(1, 4):
        table_copy(0, lax.rem(z + k, 4), z).start()

    for i in range(count * pieces // 2):
        relay(i)
    for k in range(1, 4):
        source = lax.rem(z + k, 4)
        doc_copy(source, source).wait_recv()
    for s in range(4):
        row = pl.ds(s * length, length)
        keys[row, :] = rotate_rows(
            context[s, 0].astype(f32),
            doc_cosine[s : s + 1],
            doc_sine[s : s + 1],
        )
        values[row, :] = context[s, 1]

    column = lax.broadcasted_iota(jnp.int32, (length, length), 1)
    line = lax.broadcasted_iota(jnp.int32, (length, length), 0)
    scale = head_dim ** (-0.5)

    def swap_copy(c, query):
        return pltpu.make_async_remote_copy(
            src_ref=own_att.at[c],
            dst_ref=att.at[query, c],
            send_sem=swap_send.at[c],
            recv_sem=swap_recv.at[c],
            device_id=swap_to,
            device_id_type=MESH,
        )

    allowed = [
        jnp.where(column < limits[s], 0.0, -jnp.inf) for s in range(4)
    ] + [jnp.where(column <= line, 0.0, -jnp.inf)]
    bias = jnp.concatenate(allowed, axis=1)

    def one_head(c, h):
        scores = lax.dot_general(
            queries[c * some + h], keys[...], (((1,), (1,)), ((), ())),
            preferred_element_type=f32,
        )
        scores = scores * scale + bias
        ceiling = jnp.max(scores, axis=1, keepdims=True)
        probs = jnp.exp(scores - ceiling)
        denominator = jnp.sum(probs, axis=1, keepdims=True)
        mixed = jnp.dot(probs.astype(bf16), values[...], preferred_element_type=f32)
        own_att[c, h] = (mixed / denominator).astype(bf16)

    for c in range(chunks):
        for h in range(some):
            one_head(c, h)

        @when(moves)
        def _():
            swap_copy(c, z).start()

        @when(jnp.logical_not(moves))
        def _():
            att[z, c] = own_att[c]

    mine = query_at(z, lane)
    theirs = query_at(z, across)

    def att_copy(kind, c, query, other):
        return pltpu.make_async_remote_copy(
            src_ref=att.at[query, c],
            dst_ref=att.at[query, c],
            send_sem=att_send.at[kind, c],
            recv_sem=att_recv.at[kind, c],
            device_id={"tp": other},
            device_id_type=MESH,
        )

    def att_copies(c):
        return [
            att_copy(0, c, mine, across),
            att_copy(1, c, mine, partner),
            att_copy(2, c, theirs, partner),
        ]

    for i in range(count * pieces // 2, count * pieces):
        relay(i)
    for c in range(chunks):
        @when(moves)
        def _():
            swap_copy(c, mine).wait_recv()

        att_copies(c)[0].start()
        att_copies(c)[1].start()
    for c in range(chunks):
        att_copy(0, c, theirs, across).wait_recv()
        att_copies(c)[2].start()
    load_wo.wait()
    for c in range(chunks):
        att_copy(1, c, query_at(z, partner), partner).wait_recv()
        att_copy(2, c, query_at(z, 3 - lane), partner).wait_recv()

    def up_copy(b, p):
        return pltpu.make_async_remote_copy(
            src_ref=go_up.at[b, p],
            dst_ref=from_below.at[b, p],
            send_sem=up_send.at[b, p],
            recv_sem=up_recv.at[b, p],
            device_id={"ep": jnp.minimum(z + 1, 3)},
            device_id_type=MESH,
        )

    def down_copy(b, p):
        return pltpu.make_async_remote_copy(
            src_ref=go_down.at[b, p],
            dst_ref=from_above.at[b, p],
            send_sem=down_send.at[b, p],
            recv_sem=down_recv.at[b, p],
            device_id={"ep": jnp.maximum(z - 1, 0)},
            device_id_type=MESH,
        )

    def band(p):
        return pl.ds(p * (length // 2), length // 2)

    def project_block(b):
        rows = jnp.concatenate([att[b, h // some, h % some] for h in range(heads)], axis=1)
        parts[b] = jnp.dot(rows, wo[...], preferred_element_type=f32)

    def send_up(b):
        for p in range(2):
            @when(z == 0)
            def _():
                go_up[b, p] = parts[b, band(p)].astype(bf16)

            @when((z > 0) & (z < b))
            def _():
                up_copy(b, p).wait_recv()
                go_up[b, p] = (parts[b, band(p)] + from_below[b, p].astype(f32)).astype(bf16)

            @when(z < b)
            def _():
                up_copy(b, p).start()

    def send_down(b):
        for p in range(2):
            @when(z == 3)
            def _():
                go_down[b, p] = parts[b, band(p)].astype(bf16)

            @when((z < 3) & (z > b))
            def _():
                down_copy(b, p).wait_recv()
                go_down[b, p] = (parts[b, band(p)] + from_above[b, p].astype(f32)).astype(bf16)

            @when(z > b)
            def _():
                down_copy(b, p).start()

    project_block(3)

    @when(z == 0)
    def _():
        send_up(3)

    project_block(0)

    @when(z == 3)
    def _():
        send_down(0)

    project_block(2)
    project_block(1)

    @when(z > 0)
    def _():
        send_up(3)

    @when(z < 3)
    def _():
        send_down(0)

    send_up(2)
    send_down(1)
    send_up(1)
    send_down(2)

    parts[z] += hidden[...].astype(f32)

    for p in range(2):
        @when(z > 0)
        def _():
            up_copy(z, p).wait_recv()
            parts[z, band(p)] += from_below[z, p].astype(f32)

        @when(z < 3)
        def _():
            down_copy(z, p).wait_recv()
            parts[z, band(p)] += from_above[z, p].astype(f32)

    residual = parts[z].astype(bf16)
    resid[...] = residual
    wide = residual.astype(f32)
    gain_rows = gain[...].astype(f32)
    gains = jnp.concatenate([gain_rows[i : i + 1] for i in range(gain.shape[0])], axis=1)
    raised = wide * gains
    blocks[z] = raised.astype(bf16)

    def hop_copy(source, dest, sem):
        return pltpu.make_async_remote_copy(
            src_ref=blocks.at[source],
            dst_ref=blocks.at[source],
            send_sem=sem,
            recv_sem=hop_recv.at[source],
            device_id={"ep": dest},
            device_id_type=MESH,
        )

    def hop_pair(h, act_on):
        @when((z - h >= 0) & (z < 3))
        def _():
            act_on(hop_copy(jnp.maximum(z - h, 0), jnp.minimum(z + 1, 3), hop_up.at[h]))

        @when((z + h <= 3) & (z > 0))
        def _():
            act_on(hop_copy(jnp.minimum(z + h, 3), jnp.maximum(z - 1, 0), hop_down.at[h]))

    def hop(h):
        if h > 0:
            for off in (-h, h):
                source = z + off

                @when((source >= 0) & (source <= 3))
                def _():
                    hop_copy(source, source, hop_up.at[0]).wait_recv()

        if h < 3:
            hop_pair(h, lambda copy: copy.start())

    hop(0)
    def sum_copy(dest, source):
        return pltpu.make_async_remote_copy(
            src_ref=sums.at[source],
            dst_ref=sums.at[source],
            send_sem=sum_send.at[dest],
            recv_sem=sum_recv.at[source],
            device_id={"tp": dest},
            device_id_type=MESH,
        )

    def start_sums():
        wide = resid[...].astype(f32)
        raised = wide * gains
        logit_part = lax.dot_general(
            router[...].astype(f32), raised, (((1,), (1,)), ((), ())),
            precision=lax.Precision.HIGHEST, preferred_element_type=f32,
        )
        square_part = lax.dot_general(
            jnp.ones((8, width), f32), wide * wide, (((1,), (1,)), ((), ())),
            precision=lax.Precision.HIGHEST, preferred_element_type=f32,
        )
        sums[lane] = jnp.concatenate([logit_part, square_part], axis=0)
        for k in range(1, 4):
            sum_copy(lax.rem(lane + k, 4), lane).start()

    total[...] = jnp.zeros_like(total)
    load_down.wait()

    def finish_sums():
        for k in range(1, 4):
            source = lax.rem(lane + k, 4)
            sum_copy(source, source).wait_recv()
        added = (sums[0] + sums[1]) + (sums[2] + sums[3])
        inverse = lax.rsqrt(added[experts : experts + 1] / features + norm_eps)
        logits = added[:experts] * inverse
        inside = picked > 0.0
        top = jnp.max(jnp.where(inside, logits, -jnp.inf), axis=0, keepdims=True)
        lifted = jnp.where(inside, jnp.exp(jnp.where(inside, logits - top, 0.0)), 0.0)
        mix = lifted / jnp.sum(lifted, axis=0, keepdims=True)
        rest = jnp.broadcast_to(inverse, (8 - count, length))
        for d in range(4):
            my_mixes[d] = jnp.concatenate([mix[d * count : (d + 1) * count], rest], axis=0)
        mixes[z] = my_mixes[z]
        for k in range(1, 4):
            table_copy(1, lax.rem(z + k, 4), z).start()

    def remote(kind, u, source, target, other):
        return pltpu.make_async_remote_copy(
            src_ref=source,
            dst_ref=target,
            send_sem=tp_send.at[kind, u],
            recv_sem=tp_recv.at[kind, u],
            device_id={"tp": other},
            device_id_type=MESH,
        )

    def tp_copies(u):
        return [
            remote(0, u, sent.at[u, 1 - core], first.at[u], partner),
            remote(1, u, pair.at[u], second.at[u], across),
            remote(2, u, acts.at[u, core, chip], acts.at[u, core, chip], across),
            remote(3, u, acts.at[u, core, chip], acts.at[u, core, chip], partner),
            remote(4, u, acts.at[u, core, 1 - chip], acts.at[u, core, 1 - chip], partner),
        ]

    outside = (z == 0) | (z == 3)
    rows_half = length // 4

    def near_copy(part):
        return pltpu.make_async_remote_copy(
            src_ref=leaving.at[3, part],
            dst_ref=coming.at[0, part],
            send_sem=rs_send.at[3, part],
            recv_sem=rs_recv.at[0, part],
            device_id={"ep": source_of(z, 3)},
            device_id_type=MESH,
        )

    def relay_copy(rank, part):
        return pltpu.make_async_remote_copy(
            src_ref=leaving.at[rank, part],
            dst_ref=relayed.at[rank, part],
            send_sem=rs_send.at[rank, part],
            recv_sem=relay_recv.at[rank, part],
            device_id={"ep": source_of(z, 3)},
            device_id_type=MESH,
        )

    def far_copy(rank, part):
        return pltpu.make_async_remote_copy(
            src_ref=leaving.at[rank, part],
            dst_ref=coming.at[1, part],
            send_sem=rs_send.at[rank, part],
            recv_sem=rs_recv.at[1, part],
            device_id={"ep": source_of(z, rank)},
            device_id_type=MESH,
        )

    def part_rows(part):
        return pl.ds(part * rows_half, rows_half)

    def leave(rank):
        source = source_of(z, rank)

        @when((rank == 3) | outside)
        def _():
            for part in range(4):
                leaving[rank, part] = total[source, part_rows(part)].astype(bf16)

        @when(rank == 3)
        def _():
            for part in range(4):
                near_copy(part).start()

        @when((rank < 3) & outside)
        def _():
            for part in range(4):
                relay_copy(rank, part).start()

    def relay_on(rank, some_parts=range(4)):
        source = source_of(z, rank)

        @when(jnp.logical_not(outside))
        def _():
            for part in some_parts:
                relay_copy(rank, part).wait_recv()
                leaving[rank, part] = (
                    total[source, part_rows(part)] + relayed[rank, part].astype(f32)
                ).astype(bf16)
                far_copy(rank, part).start()

    def row_of(tables, source, row):
        table = tables[source]
        rows = lax.broadcasted_iota(jnp.int32, table.shape, 0)
        return jnp.sum(jnp.where(rows == row, table, 0.0), axis=0, keepdims=True)

    places = lax.broadcasted_iota(jnp.int32, (cap, length), 0).astype(f32)

    def multiply_in(u):
        rank, source, j = unit_of(z, u)

        @when((rank > 0) & (j == 0))
        def _():
            table_copy(0, source, source).wait_recv()

        pick = (places == row_of(seats, source, j)).astype(bf16)
        rows = jnp.dot(pick, blocks[source], preferred_element_type=f32).astype(bf16)
        for kind, weights in enumerate((w_gate, w_up)):
            part = jnp.dot(rows, weights[j], preferred_element_type=f32).astype(bf16)
            for q in range(4):
                sent[u, q % 2, q // 2, :, kind * quarter : (kind + 1) * quarter] = part[
                    :, q * quarter : (q + 1) * quarter
                ]
        tp_copies(u)[0].start()

    def add_pair(u):
        copies = tp_copies(u)
        copies[0].wait_recv()
        both = sent[u, core, 1 - chip].astype(f32) + first[u, 1 - chip].astype(f32)
        pair[u] = both.astype(bf16)
        copies[1].start()

    def activate(u):
        rank, source, j = unit_of(z, u)

        @when((rank > 0) & (j == 0))
        def _():
            table_copy(1, source, source).wait_recv()

        scale_row = row_of(mixes, source, count)
        factor = jnp.sum(
            jnp.where(places == row_of(seats, source, j), scale_row, 0.0), axis=1, keepdims=True
        )
        copies = tp_copies(u)
        copies[1].wait_recv()
        value = (
            sent[u, core, chip].astype(f32)
            + first[u, chip].astype(f32)
            + second[u].astype(f32)
        ) * factor
        gate = value[:, :quarter]
        acts[u, core, chip] = (gate / (1.0 + jnp.exp(-gate)) * value[:, quarter:]).astype(bf16)
        copies[2].start()
        copies[3].start()

    def forward(u):
        copies = tp_copies(u)
        copies[2].wait_recv()
        copies[4].start()

    def multiply_out(u):
        rank, source, j = unit_of(z, u)
        copies = tp_copies(u)
        copies[3].wait_recv()
        copies[4].wait_recv()

        joined = jnp.concatenate([acts[u, q % 2, q // 2] for q in range(4)], axis=1)
        result = jnp.dot(joined, w_down[j], preferred_element_type=f32).astype(bf16)
        share = jnp.where(
            places == row_of(seats, source, j), row_of(mixes, source, j), 0.0
        ).astype(bf16)
        total[source] += lax.dot_general(
            share, result, (((0,), (0,)), ((), ())), preferred_element_type=f32
        )

        @when((rank > 0) & (j == count - 1))
        def _():
            leave(rank)

    def tick(i, carry):
        @when(i == 2)
        def _():
            finish_sums()

        @when(i == 18)
        def _():
            relay_on(1)

        @when(i == units + 4)
        def _():
            relay_on(2, range(2))

        for h, at in ((1, 3), (2, 7), (3, 11)):
            @when(i == at)
            def _():
                hop(h)

        for stage_of, delay in (
            (multiply_in, 0), (activate, 2), (forward, 4), (multiply_out, 5), (add_pair, 0),
        ):
            @when((i >= delay) & (i < units + delay))
            def _():
                stage_of(i - delay)

        @when(i == 0)
        def _():
            start_sums()

        return carry

    lax.fori_loop(0, units + 5, tick, 0)

    relay_on(2, range(2, 4))
    for part in range(4):
        rows = part_rows(part)
        answer = resid[rows, :].astype(f32) + total[z, rows]
        near_copy(part).wait_recv()
        answer = answer + coming[0, part].astype(f32)
        far_copy(1, part).wait_recv()
        out[rows, :] = (answer + coming[1, part].astype(f32)).astype(bf16)

    def settle(u, carry):
        for copy in tp_copies(u):
            copy.wait_send()
        return carry

    lax.fori_loop(0, units, settle, 0)
    for k in range(1, 4):
        other = lax.rem(z + k, 4)
        table_copy(0, other, z).wait_send()
        table_copy(1, other, z).wait_send()
        for part in range(4):
            near_copy(part).wait_send() if k == 3 else far_copy(k, part).wait_send()
    for h in range(3):
        hop_pair(h, lambda copy: copy.wait_send())
    for k in range(1, 4):
        doc_copy(lax.rem(z + k, 4), z).wait_send()
        sum_copy(lax.rem(lane + k, 4), lane).wait_send()
    for c in range(chunks):
        @when(moves)
        def _():
            swap_copy(c, z).wait_send()

        for copy in att_copies(c):
            copy.wait_send()
    for b in range(4):
        for p in range(2):
            @when(z < b)
            def _():
                up_copy(b, p).wait_send()

            @when(z > b)
            def _():
                down_copy(b, p).wait_send()


def fused_layer(
    question_q, question_kv, doc_kv, doc_lens, query_docs, ctx_pos, hidden, out_proj,
    norm_gain, router_weight, w_gate_up, w_down, expert_ids,
):
    bf16 = jnp.bfloat16
    f32 = jnp.float32
    length, heads, head_dim = question_q.shape
    width = hidden.shape[1]
    experts = router_weight.shape[1]
    pool_dev, doc_max = doc_kv.shape[:2]
    count = w_gate_up.shape[0]
    inner = w_gate_up.shape[3]
    capacity = length * expert_ids.shape[1] // experts
    units = 4 * count
    quarter = inner // 4
    chunks = 4
    some = heads // chunks
    vmem = pltpu.VMEM
    smem = pltpu.SMEM
    dma = pltpu.SemaphoreType.DMA
    block = (4, length, width)
    gain = norm_gain.reshape(width // 128, 128)
    router = jnp.swapaxes(router_weight, 0, 1)
    ids = jnp.swapaxes(expert_ids, 0, 1)
    return pl.pallas_call(
        layer_kernel,
        out_shape=jax.ShapeDtypeStruct((length, width), bf16),
        in_specs=[pl.BlockSpec(memory_space=pl.ANY)] * 13,
        out_specs=pl.BlockSpec(memory_space=vmem),
        scratch_shapes=[
            vmem(question_q.shape, bf16),
            vmem((length, 2, head_dim), bf16),
            vmem((pool_dev, doc_max, 2, head_dim), bf16),
            smem(doc_lens.shape, jnp.int32),
            smem(query_docs.shape, jnp.int32),
            smem(ctx_pos.shape, jnp.int32),
            vmem(hidden.shape, bf16),
            vmem(gain.shape, bf16),
            vmem(router.shape, bf16),
            vmem(ids.shape, jnp.int32),
            dma((10,)),
            vmem(out_proj.shape, bf16),
            vmem((4, 2, length, head_dim), bf16),
            vmem((4, 2, length, head_dim), bf16),
            vmem((heads, length, head_dim), bf16),
            vmem((5 * length, head_dim), bf16),
            vmem((5 * length, head_dim), bf16),
            vmem((chunks, some, length, head_dim), bf16),
            vmem((4, chunks, some, length, head_dim), bf16),
            vmem(block, f32),
            vmem((4, 2, length // 2, width), bf16),
            vmem((4, 2, length // 2, width), bf16),
            vmem((4, 2, length // 2, width), bf16),
            vmem((4, 2, length // 2, width), bf16),
            vmem((4, experts + 8, length), f32),
            dma,
            dma((4,)),
            dma((4,)),
            dma((chunks,)),
            dma((chunks,)),
            dma((3, chunks)),
            dma((3, chunks)),
            dma((4, 2)),
            dma((4, 2)),
            dma((4, 2)),
            dma((4, 2)),
            dma((4,)),
            dma((4,)),
            vmem((2, width // 2, 2, inner), bf16),
            vmem((count, width, inner), bf16),
            vmem((count, width, inner), bf16),
            vmem(w_down.shape, bf16),
            vmem((length, width), bf16),
            vmem((4, 8, length), f32),
            vmem((4, 8, length), f32),
            vmem(block, bf16),
            vmem((4, 8, length), f32),
            vmem((4, 8, length), f32),
            vmem((units, 2, 2, capacity, 2 * quarter), bf16),
            vmem((units, 2, capacity, 2 * quarter), bf16),
            vmem((units, capacity, 2 * quarter), bf16),
            vmem((units, capacity, 2 * quarter), bf16),
            vmem((units, 2, 2, capacity, quarter), bf16),
            vmem(block, f32),
            vmem((4, 4, length // 4, width), bf16),
            vmem((4, 4, length // 4, width), bf16),
            vmem((2, 4, length // 4, width), bf16),
            dma((2,)),
            dma,
            dma((3,)),
            dma((3,)),
            dma((4,)),
            dma((2, 4)),
            dma((2, 4)),
            dma((5, units)),
            dma((5, units)),
            dma((4, 4)),
            dma((4, 4)),
            dma((2, 4)),
        ],
        compiler_params=pltpu.CompilerParams(
            collective_id=0, has_side_effects=True, vmem_limit_bytes=60 << 20
        ),
    )(
        question_q, question_kv, doc_kv, doc_lens, query_docs, ctx_pos, hidden, gain, router,
        ids, out_proj, w_gate_up, w_down,
    )


def feed_forward(arrived, w_gate_up, w_down):
    term = jnp.einsum("erd,edgh->hegr", arrived, w_gate_up, preferred_element_type=jnp.float32)
    summed = lax.psum_scatter(
        term.astype(jnp.bfloat16), "tp", scatter_dimension=0, tiled=True
    ).astype(jnp.float32)
    activated = (jax.nn.silu(summed[:, :, 0]) * summed[:, :, 1]).astype(jnp.bfloat16)
    piece = lax.all_gather(activated, "tp", axis=0, tiled=True)
    return jnp.einsum(
        "her,ehd->erd", piece, w_down, preferred_element_type=jnp.float32
    ).astype(jnp.bfloat16)


def per_device(
    question_q,
    question_kv,
    doc_kv,
    doc_lens,
    query_docs,
    ctx_pos,
    hidden,
    out_proj,
    norm_gain,
    router_weight,
    w_gate_up,
    w_down,
    expert_ids,
):
    lanes = lax.axis_size("tp")
    groups = lax.axis_size("ep")
    lane = lax.axis_index("tp")
    device = lax.axis_index("ep")
    length, heads_here, head_dim = question_q.shape
    kv_heads = question_kv.shape[1]
    if lanes == 4 and groups == 4:
        return fused_layer(
            question_q, question_kv, doc_kv, doc_lens, query_docs, ctx_pos, hidden, out_proj,
            norm_gain, router_weight, w_gate_up, w_down, expert_ids,
        )
    kv_pick = lane * kv_heads // lanes
    scale = head_dim ** (-0.5)
    docs_per = query_docs.shape[1]
    row_pos = lax.dynamic_index_in_dim(ctx_pos, device, 0, keepdims=False)
    question_pos = row_pos[docs_per] + jnp.arange(length, dtype=jnp.int32)
    queries = rotate(question_q, question_pos).astype(jnp.bfloat16)
    own_kv = lax.dynamic_index_in_dim(question_kv, kv_pick, 1, keepdims=False)
    own_keys = rotate(own_kv[:, 0], question_pos).astype(jnp.bfloat16)
    own_values = own_kv[:, 1]
    causal = jnp.arange(length)[:, None] >= jnp.arange(length)[None, :]
    doc_keys, doc_values, valid = fetch_context(
        doc_kv, doc_lens, query_docs, row_pos, device, kv_pick
    )
    keys = jnp.concatenate([doc_keys, own_keys], axis=0)
    values = jnp.concatenate([doc_values, own_values], axis=0)
    allowed = jnp.concatenate(
        [jnp.broadcast_to(valid[None, :], (length, valid.shape[0])), causal], axis=1
    )
    scores = jnp.einsum("ihd,jd->hij", queries, keys, preferred_element_type=jnp.float32) * scale
    scores = jnp.where(allowed[None], scores, -jnp.inf)
    ceiling = jnp.max(scores, axis=-1, keepdims=True)
    probs = jnp.exp(scores - ceiling)
    denominator = jnp.sum(probs, axis=-1, keepdims=True)
    mixed = jnp.einsum(
        "hij,jd->hid", probs.astype(jnp.bfloat16), values, preferred_element_type=jnp.float32
    )
    attended = (
        jnp.transpose(mixed / denominator, (1, 0, 2))
        .reshape(length, heads_here * head_dim)
        .astype(jnp.bfloat16)
    )
    width_here = hidden.shape[1]
    projected = project(attended, out_proj)
    residual_wide = narrow(hidden.astype(jnp.float32) + projected).astype(jnp.float32)
    gain = norm_gain.astype(jnp.float32)
    squares, logit_part = lax.psum(
        (
            jnp.sum(residual_wide * residual_wide, axis=1),
            jnp.dot(
                residual_wide * gain[None, :],
                router_weight.astype(jnp.float32),
                precision=lax.Precision.HIGHEST,
            ),
        ),
        "tp",
    )
    inv_rms = lax.rsqrt(squares / D + norm_eps)
    normed = (residual_wide * inv_rms[:, None] * gain[None, :]).astype(jnp.bfloat16)
    logits = logit_part * inv_rms[:, None]
    local_experts = w_gate_up.shape[0]
    capacity = length * expert_ids.shape[1] // (local_experts * groups)
    experts = logits.shape[1]
    chosen = jnp.any(expert_ids[:, :, None] == jnp.arange(experts, dtype=jnp.int32), axis=1)
    top = jnp.max(jnp.where(chosen, logits, -jnp.inf), axis=1, keepdims=True)
    raised = jnp.where(chosen, jnp.exp(jnp.where(chosen, logits - top, 0.0)), 0.0)
    mix = raised / jnp.sum(raised, axis=1, keepdims=True)
    mix_high = mix.astype(jnp.bfloat16)
    mix_low = (mix - mix_high.astype(jnp.float32)).astype(jnp.bfloat16)
    notes = jnp.concatenate([chosen.astype(jnp.bfloat16), mix_high, mix_low], axis=1)
    notes = jnp.pad(notes, ((0, 0), (0, -notes.shape[1] % 128)))
    packed = lax.all_gather(jnp.concatenate([normed, notes], axis=1), "ep", axis=0)
    normed_all = packed[:, :, :width_here]

    def mine(index):
        start = width_here + index * experts + device * local_experts
        return lax.dynamic_slice_in_dim(packed, start, local_experts, axis=2)

    member = mine(0) > 0
    share_high = jnp.swapaxes(mine(1), 1, 2)
    share_low = jnp.swapaxes(mine(2), 1, 2)
    earlier = jnp.arange(length)[:, None] > jnp.arange(length)[None, :]
    rank = jnp.einsum(
        "nm,sme->sen",
        earlier.astype(jnp.bfloat16),
        member.astype(jnp.bfloat16),
        preferred_element_type=jnp.float32,
    )
    seat = jnp.where(jnp.swapaxes(member, 1, 2), rank.astype(jnp.int32), -1)
    picks = (seat[:, :, None, :] == jnp.arange(capacity, dtype=jnp.int32)[:, None]).astype(
        jnp.bfloat16
    )
    arrived = jnp.einsum(
        "secn,snd->escd", picks, normed_all, preferred_element_type=jnp.float32
    ).astype(jnp.bfloat16)
    rows = groups * capacity
    arrived = arrived.reshape(local_experts, rows, width_here)
    expert_out = feed_forward(arrived, w_gate_up, w_down)
    weights = jnp.stack([picks * share_high[:, :, None, :], picks * share_low[:, :, None, :]])
    partial = jnp.einsum(
        "psecn,escd->snd",
        weights,
        expert_out.reshape(local_experts, groups, capacity, width_here),
        preferred_element_type=jnp.float32,
    )
    combined = lax.psum_scatter(
        partial.astype(jnp.bfloat16).reshape(groups * length, width_here),
        "ep",
        scatter_dimension=0,
        tiled=True,
    )
    return (residual_wide + combined.astype(jnp.float32)).astype(jnp.bfloat16)


def solution(mesh):
    placed = (
        P(("grp", "ep"), "tp", None),
        P(("grp", "ep"), None, None, None),
        P(("grp", "ep"), None, None, None, None),
        P("grp"),
        P("grp", None),
        P("grp", None),
        P(("grp", "ep"), "tp"),
        P("ep", "tp"),
        P("tp"),
        P("tp", None),
        P("ep", "tp", None, None),
        P("ep", None, "tp"),
        P(("grp", "ep"), None),
    )
    return jax.shard_map(
        per_device, mesh=mesh, in_specs=placed, out_specs=P(("grp", "ep"), "tp"), check_vma=False
    )
```

```python
import math

import jax
import jax.numpy as jnp
from jax import lax
from jax.experimental import pallas as pl
from jax.experimental.pallas import tpu as pltpu
from jax.sharding import PartitionSpec as P

D = 4096
HID = 1024


rope_theta = 1000000.0
norm_eps = 1e-06


def narrow(values):
    return lax.optimization_barrier(values.astype(jnp.bfloat16))


def rotate(values, positions):
    half = values.shape[-1] // 2
    freq = jnp.exp(
        jnp.arange(half, dtype=jnp.float32) * (-2.0 * math.log(rope_theta) / values.shape[-1])
    )
    angle = positions.astype(jnp.float32)[:, None] * freq[None, :]
    shape = (values.shape[0],) + (1,) * (values.ndim - 2) + (half,)
    cosine = jnp.cos(angle).reshape(shape)
    sine = jnp.sin(angle).reshape(shape)
    floats = values.astype(jnp.float32)
    first = floats[..., :half]
    second = floats[..., half:]
    return jnp.concatenate(
        [first * cosine - second * sine, second * cosine + first * sine], axis=-1
    )


def fetch_context(doc_kv, doc_lens, query_docs, row_pos, device, kv_pick):
    pool_dev, doc_max, kv_heads, pair, head_dim = doc_kv.shape
    docs_per = query_docs.shape[1]
    pool_head = lax.dynamic_index_in_dim(doc_kv, kv_pick, 2, keepdims=False).reshape(
        pool_dev, doc_max, pair * head_dim
    )
    held = device * pool_dev + jnp.arange(pool_dev, dtype=jnp.int32)
    wanted = jnp.sum((query_docs[:, :, None] == held[None, None, :]).astype(jnp.float32), axis=1)
    sending = jnp.einsum(
        "rl,lkc->rkc", wanted.astype(jnp.bfloat16), pool_head, preferred_element_type=jnp.float32
    ).astype(jnp.bfloat16)
    received = lax.all_to_all(sending, "ep", split_axis=0, concat_axis=0, tiled=True)
    my_docs = lax.dynamic_index_in_dim(query_docs, device, 0, keepdims=False)
    from_dev = jnp.arange(received.shape[0], dtype=jnp.int32)
    pick_dev = ((my_docs // pool_dev)[:, None] == from_dev[None, :]).astype(jnp.bfloat16)
    context = jnp.einsum(
        "jr,rkc->jkc", pick_dev, received, preferred_element_type=jnp.float32
    ).astype(jnp.bfloat16)
    every_doc = jnp.arange(doc_lens.shape[0], dtype=jnp.int32)
    lengths = jnp.sum(
        jnp.where(my_docs[:, None] == every_doc[None, :], doc_lens[None, :], 0), axis=1
    )
    positions = jnp.repeat(row_pos[:docs_per], doc_max, total_repeat_length=docs_per * doc_max)
    keys = rotate(context[:, :, :head_dim].reshape(docs_per * doc_max, head_dim), positions).astype(
        jnp.bfloat16
    )
    values = context[:, :, head_dim:].reshape(docs_per * doc_max, head_dim)
    valid = (jnp.arange(doc_max, dtype=jnp.int32)[None, :] < lengths[:, None]).reshape(
        docs_per * doc_max
    )
    return (keys, values, valid)


def project(attended, out_proj):
    lanes = lax.axis_size("tp")
    groups = lax.axis_size("ep")
    length = attended.shape[0]
    if lanes == groups:
        swap = [(e * lanes + t, t * lanes + e) for e in range(groups) for t in range(lanes)]
        block = lax.ppermute(attended, ("ep", "tp"), swap)
        tokens = lax.all_gather(block, "tp", axis=0, tiled=True)
    else:
        all_heads = lax.all_gather(attended, "tp", axis=1, tiled=True)
        split = jnp.swapaxes(all_heads.reshape(length, groups, -1), 0, 1)
        tokens = lax.all_to_all(split, "ep", split_axis=0, concat_axis=0, tiled=True)
        tokens = tokens.reshape(groups * length, -1)
    part = jnp.dot(tokens, out_proj, preferred_element_type=jnp.float32)
    summed = lax.psum_scatter(
        part.astype(jnp.bfloat16), "ep", scatter_dimension=0, tiled=True
    ).astype(jnp.float32)
    return summed


MESH = pl.DeviceIdType.MESH


def when(condition):
    return pl.when(condition)


def seat_of(query, plane):
    return 2 * lax.rem(query + plane, 2) + query // 2


def query_at(plane, lane):
    return 2 * lax.rem(lane, 2) + lax.rem(lane // 2 + plane, 2)


def source_of(z, rank):
    low = z < 2
    near = z + 1 - 2 * lax.rem(z, 2)
    inner = jnp.where(low, 2, 1)
    outer = jnp.where(low, 3, 0)
    return jnp.where(
        rank == 0, z, jnp.where(rank == 1, inner, jnp.where(rank == 2, outer, near))
    )


def unit_of(z, u):
    step = jnp.maximum(u - 3, 0)
    rank = jnp.where((u < 3) | (u >= 15), 0, lax.rem(step // 4 + 2, 3) + 1)
    j = jnp.where(u < 3, u + 1, lax.rem(step, 4))
    return rank, source_of(z, rank), j


def layer_kernel(
    q_hbm, kv_hbm, docs_hbm, lens_hbm, lists_hbm, ctx_hbm, hidden_hbm, gain_hbm, router_hbm,
    ids_hbm, wo_hbm, wgu_hbm, wd_hbm, out,
    q, own_kv, docs, lens, lists, ctx, hidden, gain, router, ids, load_sem,
    wo, sending, context, queries, keys, values, own_att, att, parts,
    go_up, go_down, from_below, from_above, sums,
    wo_sem, doc_send, doc_recv, swap_send, swap_recv, att_send, att_recv,
    up_send, up_recv, down_send, down_recv, sum_send, sum_recv,
    stage, w_gate, w_up, w_down, resid, my_seats, my_mixes, blocks, seats, mixes,
    sent, first, pair, second, acts, total, leaving, relayed, coming,
    stage_sem, down_sem, hop_up, hop_down, hop_recv, table_send, table_recv,
    tp_send, tp_recv, rs_send, relay_recv, rs_recv,
):
    bf16 = jnp.bfloat16
    f32 = jnp.float32
    z = lax.axis_index("ep")
    lane = lax.axis_index("tp")
    chip = lane // 2
    core = lane % 2
    partner = chip * 2 + (1 - core)
    across = (1 - chip) * 2 + core
    length, width = hidden.shape
    heads = q.shape[1]
    head_dim = q.shape[2]
    features = width * 4
    some = heads // own_att.shape[0]
    chunks = own_att.shape[0]

    loads = [
        pltpu.make_async_copy(source, target, load_sem.at[i])
        for i, (source, target) in enumerate(
            (
                (docs_hbm.at[:, :, lane], docs),
                (lists_hbm, lists),
                (ctx_hbm, ctx),
                (lens_hbm, lens),
                (q_hbm, q),
                (kv_hbm.at[:, lane], own_kv),
                (ids_hbm, ids),
                (hidden_hbm, hidden),
                (gain_hbm, gain),
                (router_hbm, router),
            )
        )
    ]
    for load in loads:
        load.start()
    load_wo = pltpu.make_async_copy(wo_hbm, wo, wo_sem)
    load_wo.start()
    count, inner = w_down.shape[:2]
    cap = sent.shape[3]
    quarter = acts.shape[4]
    units = 4 * count
    piece = stage.shape[1]
    pieces = inner // piece

    def load_in(i):
        rows = pl.ds((i % pieces) * piece, piece)
        return pltpu.make_async_copy(
            wgu_hbm.at[i // pieces, rows], stage.at[i % 2], stage_sem.at[i % 2]
        )

    load_in(0).start()
    load_in(1).start()
    load_down = pltpu.make_async_copy(wd_hbm, w_down, down_sem)
    load_down.start()

    def relay(i):
        load_in(i).wait()
        step = 128

        def body(k, carry):
            rows = pl.ds(pl.multiple_of(k * step, step), step)
            place = pl.ds(pl.multiple_of((i % pieces) * piece + k * step, step), step)
            block = jnp.transpose(stage[i % 2, rows], (1, 0, 2))
            w_gate[i // pieces, place, :] = block[0]
            w_up[i // pieces, place, :] = block[1]
            return carry

        lax.fori_loop(0, piece // step, body, 0)
        if i + 2 < count * pieces:
            load_in(i + 2).start()

    swap_to = {"ep": lane, "tp": seat_of(z, lane)}
    swap_from = {"ep": query_at(z, lane), "tp": z}
    moves = (lane != z) | (seat_of(z, lane) != lane)
    barrier = pltpu.get_barrier_semaphore()
    for k in range(1, 4):
        for axis, here in (("ep", z), ("tp", lane)):
            pl.semaphore_signal(
                barrier, inc=1, device_id={axis: lax.rem(here + k, 4)}, device_id_type=MESH
            )

    @when(moves)
    def _():
        for other in (swap_to, swap_from):
            pl.semaphore_signal(barrier, inc=1, device_id=other, device_id_type=MESH)

    for load in loads[:3]:
        load.wait()
    found = [jnp.transpose(docs[l], (1, 0, 2)).astype(f32) for l in range(2)]
    for r in range(4):
        shares = []
        for l in range(2):
            hit = lists[r, 0] == 2 * z + l
            for j in range(1, 4):
                hit = hit | (lists[r, j] == 2 * z + l)
            shares.append(jnp.where(hit, 1.0, 0.0).astype(f32))
        sending[r] = (found[0] * shares[0] + found[1] * shares[1]).astype(bf16)

    pl.semaphore_wait(barrier, jnp.where(moves, 8, 6))

    def doc_copy(dest, source):
        return pltpu.make_async_remote_copy(
            src_ref=sending.at[dest],
            dst_ref=context.at[source],
            send_sem=doc_send.at[dest],
            recv_sem=doc_recv.at[source],
            device_id={"ep": dest},
            device_id_type=MESH,
        )

    for k in range(1, 4):
        doc_copy(lax.rem(z + k, 4), z).start()
    context[z] = sending[z]

    def rotate_rows(rows, cosine, sine):
        return (rows * cosine + pltpu.roll(rows, head_dim // 2, 1) * sine).astype(bf16)

    for load in loads[3:]:
        load.wait()
    half = head_dim // 2
    lanes = lax.broadcasted_iota(jnp.int32, (1, head_dim), 1)
    freq = jnp.exp(
        lax.rem(lanes, half).astype(f32) * (-2.0 * math.log(rope_theta) / head_dim)
    )
    sign = jnp.where(lanes < half, -1.0, 1.0)
    steps = lax.broadcasted_iota(jnp.int32, (length, head_dim), 0)
    angle = (ctx[z, 4] + steps).astype(f32) * freq
    cosine = jnp.cos(angle)
    sine = jnp.sin(angle) * sign
    starts = []
    limits = []
    for s in range(4):
        start = jnp.int32(0)
        which = jnp.int32(0)
        for j in range(4):
            here = lists[z, j] // 2 == s
            start = start + jnp.where(here, ctx[z, j], 0)
            which = which + jnp.where(here, lists[z, j], 0)
        limit = jnp.int32(0)
        for d in range(8):
            limit = limit + jnp.where(which == d, lens[d], 0)
        starts.append(start)
        limits.append(limit)
    row = lax.broadcasted_iota(jnp.int32, (8, head_dim), 0)
    begin = jnp.zeros((8, head_dim), jnp.int32)
    for s in range(4):
        begin = jnp.where(row == s, starts[s], begin)
    doc_angle = begin.astype(f32) * freq
    doc_cosine = jnp.cos(doc_angle)
    doc_sine = jnp.sin(doc_angle) * sign
    turned = jnp.transpose(q[...], (1, 0, 2))
    for h in range(heads):
        queries[h] = rotate_rows(turned[h].astype(f32), cosine, sine)
    own = jnp.transpose(own_kv[...], (1, 0, 2))
    last = pl.ds(4 * length, length)
    keys[last, :] = rotate_rows(own[0].astype(f32), cosine, sine)
    values[last, :] = own[1]

    experts = router.shape[0]
    expert = lax.broadcasted_iota(jnp.int32, (experts, length), 0)
    picked = jnp.zeros((experts, length), f32)
    for k in range(ids.shape[0]):
        picked = picked + jnp.where(ids[k : k + 1, :] == expert, 1.0, 0.0)
    before = (
        lax.broadcasted_iota(jnp.int32, (length, length), 0)
        < lax.broadcasted_iota(jnp.int32, (length, length), 1)
    )
    rank = jnp.dot(
        picked.astype(bf16),
        jnp.where(before, 1.0, 0.0).astype(bf16),
        preferred_element_type=f32,
    )
    seat = jnp.where(picked > 0.0, rank, -1.0)
    blank = jnp.zeros((8 - count, length), f32)
    for d in range(4):
        my_seats[d] = jnp.concatenate([seat[d * count : (d + 1) * count], blank], axis=0)
    seats[z] = my_seats[z]

    def table_copy(kind, dest, source):
        mine_, theirs_ = ((my_seats, seats), (my_mixes, mixes))[kind]
        return pltpu.make_async_remote_copy(
            src_ref=mine_.at[dest],
            dst_ref=theirs_.at[source],
            send_sem=table_send.at[kind, dest],
            recv_sem=table_recv.at[kind, source],
            device_id={"ep": dest},
            device_id_type=MESH,
        )

    for k in range(1, 4):
        table_copy(0, lax.rem(z + k, 4), z).start()

    for i in range(count * pieces // 2):
        relay(i)
    total[...] = jnp.zeros_like(total)
    for k in range(1, 4):
        source = lax.rem(z + k, 4)
        doc_copy(source, source).wait_recv()
    for s in range(4):
        row = pl.ds(s * length, length)
        keys[row, :] = rotate_rows(
            context[s, 0].astype(f32),
            doc_cosine[s : s + 1],
            doc_sine[s : s + 1],
        )
        values[row, :] = context[s, 1]

    column = lax.broadcasted_iota(jnp.int32, (length, length), 1)
    line = lax.broadcasted_iota(jnp.int32, (length, length), 0)
    scale = head_dim ** (-0.5)

    def swap_copy(c, query):
        return pltpu.make_async_remote_copy(
            src_ref=own_att.at[c],
            dst_ref=att.at[query, c],
            send_sem=swap_send.at[c],
            recv_sem=swap_recv.at[c],
            device_id=swap_to,
            device_id_type=MESH,
        )

    allowed = [
        jnp.where(column < limits[s], 0.0, -jnp.inf) for s in range(4)
    ] + [jnp.where(column <= line, 0.0, -jnp.inf)]
    bias = jnp.concatenate(allowed, axis=1)

    def one_head(c, h):
        scores = lax.dot_general(
            queries[c * some + h], keys[...], (((1,), (1,)), ((), ())),
            preferred_element_type=f32,
        )
        scores = scores * scale + bias
        ceiling = jnp.max(scores, axis=1, keepdims=True)
        probs = jnp.exp(scores - ceiling)
        denominator = jnp.sum(probs, axis=1, keepdims=True)
        mixed = jnp.dot(probs.astype(bf16), values[...], preferred_element_type=f32)
        own_att[c, h] = (mixed / denominator).astype(bf16)

    for c in range(chunks):
        for h in range(some):
            one_head(c, h)

        @when(moves)
        def _():
            swap_copy(c, z).start()

        @when(jnp.logical_not(moves))
        def _():
            att[z, c] = own_att[c]

    mine = query_at(z, lane)
    theirs = query_at(z, across)

    def att_copy(kind, c, query, other):
        return pltpu.make_async_remote_copy(
            src_ref=att.at[query, c],
            dst_ref=att.at[query, c],
            send_sem=att_send.at[kind, c],
            recv_sem=att_recv.at[kind, c],
            device_id={"tp": other},
            device_id_type=MESH,
        )

    def att_copies(c):
        return [
            att_copy(0, c, mine, across),
            att_copy(1, c, mine, partner),
            att_copy(2, c, theirs, partner),
        ]

    for i in range(count * pieces // 2, count * pieces):
        relay(i)
    for c in range(chunks):
        @when(moves)
        def _():
            swap_copy(c, mine).wait_recv()

        att_copies(c)[0].start()
        att_copies(c)[1].start()
    for c in range(chunks):
        att_copy(0, c, theirs, across).wait_recv()
        att_copies(c)[2].start()
    load_wo.wait()
    load_down.wait()
    for c in range(chunks):
        att_copy(1, c, query_at(z, partner), partner).wait_recv()
        att_copy(2, c, query_at(z, 3 - lane), partner).wait_recv()

    def up_copy(b, p):
        return pltpu.make_async_remote_copy(
            src_ref=go_up.at[b, p],
            dst_ref=from_below.at[b, p],
            send_sem=up_send.at[b, p],
            recv_sem=up_recv.at[b, p],
            device_id={"ep": jnp.minimum(z + 1, 3)},
            device_id_type=MESH,
        )

    def down_copy(b, p):
        return pltpu.make_async_remote_copy(
            src_ref=go_down.at[b, p],
            dst_ref=from_above.at[b, p],
            send_sem=down_send.at[b, p],
            recv_sem=down_recv.at[b, p],
            device_id={"ep": jnp.maximum(z - 1, 0)},
            device_id_type=MESH,
        )

    def band(p):
        return pl.ds(p * (length // 2), length // 2)

    def project_block(b):
        rows = jnp.concatenate([att[b, h // some, h % some] for h in range(heads)], axis=1)
        parts[b] = jnp.dot(rows, wo[...], preferred_element_type=f32)

    def send_up(b):
        for p in range(2):
            @when(z == 0)
            def _():
                go_up[b, p] = parts[b, band(p)].astype(bf16)

            @when((z > 0) & (z < b))
            def _():
                up_copy(b, p).wait_recv()
                go_up[b, p] = (parts[b, band(p)] + from_below[b, p].astype(f32)).astype(bf16)

            @when(z < b)
            def _():
                up_copy(b, p).start()

    def send_down(b):
        for p in range(2):
            @when(z == 3)
            def _():
                go_down[b, p] = parts[b, band(p)].astype(bf16)

            @when((z < 3) & (z > b))
            def _():
                down_copy(b, p).wait_recv()
                go_down[b, p] = (parts[b, band(p)] + from_above[b, p].astype(f32)).astype(bf16)

            @when(z > b)
            def _():
                down_copy(b, p).start()

    project_block(3)

    @when(z == 0)
    def _():
        send_up(3)

    project_block(0)

    @when(z == 3)
    def _():
        send_down(0)

    project_block(2)
    project_block(1)

    @when(z > 0)
    def _():
        send_up(3)

    @when(z < 3)
    def _():
        send_down(0)

    send_up(2)
    send_down(1)
    send_up(1)
    send_down(2)

    parts[z] += hidden[...].astype(f32)

    for p in range(2):
        @when(z > 0)
        def _():
            up_copy(z, p).wait_recv()
            parts[z, band(p)] += from_below[z, p].astype(f32)

        @when(z < 3)
        def _():
            down_copy(z, p).wait_recv()
            parts[z, band(p)] += from_above[z, p].astype(f32)

    residual = parts[z].astype(bf16)
    resid[...] = residual
    wide = residual.astype(f32)
    gain_rows = gain[...].astype(f32)
    gains = jnp.concatenate([gain_rows[i : i + 1] for i in range(gain.shape[0])], axis=1)
    raised = wide * gains
    blocks[z] = raised.astype(bf16)

    def hop_copy(source, dest, sem):
        return pltpu.make_async_remote_copy(
            src_ref=blocks.at[source],
            dst_ref=blocks.at[source],
            send_sem=sem,
            recv_sem=hop_recv.at[source],
            device_id={"ep": dest},
            device_id_type=MESH,
        )

    def hop_pair(h, act_on):
        @when((z - h >= 0) & (z < 3))
        def _():
            act_on(hop_copy(jnp.maximum(z - h, 0), jnp.minimum(z + 1, 3), hop_up.at[h]))

        @when((z + h <= 3) & (z > 0))
        def _():
            act_on(hop_copy(jnp.minimum(z + h, 3), jnp.maximum(z - 1, 0), hop_down.at[h]))

    def hop(h):
        if h > 0:
            for off in (-h, h):
                source = z + off

                @when((source >= 0) & (source <= 3))
                def _():
                    hop_copy(source, source, hop_up.at[0]).wait_recv()

        if h < 3:
            hop_pair(h, lambda copy: copy.start())

    hop(0)
    def sum_copy(dest, source):
        return pltpu.make_async_remote_copy(
            src_ref=sums.at[source],
            dst_ref=sums.at[source],
            send_sem=sum_send.at[dest],
            recv_sem=sum_recv.at[source],
            device_id={"tp": dest},
            device_id_type=MESH,
        )

    def start_sums():
        wide = resid[...].astype(f32)
        raised = wide * gains
        logit_part = lax.dot_general(
            router[...].astype(f32), raised, (((1,), (1,)), ((), ())),
            precision=lax.Precision.HIGHEST, preferred_element_type=f32,
        )
        square_part = lax.dot_general(
            jnp.ones((8, width), f32), wide * wide, (((1,), (1,)), ((), ())),
            precision=lax.Precision.HIGHEST, preferred_element_type=f32,
        )
        sums[lane] = jnp.concatenate([logit_part, square_part], axis=0)
        for k in range(1, 4):
            sum_copy(lax.rem(lane + k, 4), lane).start()

    def finish_sums():
        for k in range(1, 4):
            source = lax.rem(lane + k, 4)
            sum_copy(source, source).wait_recv()
        added = (sums[0] + sums[1]) + (sums[2] + sums[3])
        inverse = lax.rsqrt(added[experts : experts + 1] / features + norm_eps)
        logits = added[:experts] * inverse
        inside = picked > 0.0
        top = jnp.max(jnp.where(inside, logits, -jnp.inf), axis=0, keepdims=True)
        lifted = jnp.where(inside, jnp.exp(jnp.where(inside, logits - top, 0.0)), 0.0)
        mix = lifted / jnp.sum(lifted, axis=0, keepdims=True)
        rest = jnp.broadcast_to(inverse, (8 - count, length))
        for d in range(4):
            my_mixes[d] = jnp.concatenate([mix[d * count : (d + 1) * count], rest], axis=0)
        mixes[z] = my_mixes[z]
        for k in range(1, 4):
            table_copy(1, lax.rem(z + k, 4), z).start()

    def remote(kind, u, source, target, other):
        return pltpu.make_async_remote_copy(
            src_ref=source,
            dst_ref=target,
            send_sem=tp_send.at[kind, u],
            recv_sem=tp_recv.at[kind, u],
            device_id={"tp": other},
            device_id_type=MESH,
        )

    def tp_copies(u):
        return [
            remote(0, u, sent.at[u, 1 - core], first.at[u], partner),
            remote(1, u, pair.at[u], second.at[u], across),
            remote(2, u, acts.at[u, core, chip], acts.at[u, core, chip], across),
            remote(3, u, acts.at[u, core, chip], acts.at[u, core, chip], partner),
            remote(4, u, acts.at[u, core, 1 - chip], acts.at[u, core, 1 - chip], partner),
        ]

    outside = (z == 0) | (z == 3)
    rows_half = length // 4

    def near_copy(part):
        return pltpu.make_async_remote_copy(
            src_ref=leaving.at[3, part],
            dst_ref=coming.at[0, part],
            send_sem=rs_send.at[3, part],
            recv_sem=rs_recv.at[0, part],
            device_id={"ep": source_of(z, 3)},
            device_id_type=MESH,
        )

    def relay_copy(rank, part):
        return pltpu.make_async_remote_copy(
            src_ref=leaving.at[rank, part],
            dst_ref=relayed.at[rank, part],
            send_sem=rs_send.at[rank, part],
            recv_sem=relay_recv.at[rank, part],
            device_id={"ep": source_of(z, 3)},
            device_id_type=MESH,
        )

    def far_copy(rank, part):
        return pltpu.make_async_remote_copy(
            src_ref=leaving.at[rank, part],
            dst_ref=coming.at[1, part],
            send_sem=rs_send.at[rank, part],
            recv_sem=rs_recv.at[1, part],
            device_id={"ep": source_of(z, rank)},
            device_id_type=MESH,
        )

    def part_rows(part):
        return pl.ds(part * rows_half, rows_half)

    def leave(rank):
        source = source_of(z, rank)

        @when((rank == 3) | outside)
        def _():
            for part in range(4):
                leaving[rank, part] = total[source, part_rows(part)].astype(bf16)

        @when(rank == 3)
        def _():
            for part in range(4):
                near_copy(part).start()

        @when((rank < 3) & outside)
        def _():
            for part in range(4):
                relay_copy(rank, part).start()

    def relay_on(rank, some_parts=range(4)):
        source = source_of(z, rank)

        @when(jnp.logical_not(outside))
        def _():
            for part in some_parts:
                relay_copy(rank, part).wait_recv()
                leaving[rank, part] = (
                    total[source, part_rows(part)] + relayed[rank, part].astype(f32)
                ).astype(bf16)
                far_copy(rank, part).start()

    def row_of(tables, source, row):
        table = tables[source]
        rows = lax.broadcasted_iota(jnp.int32, table.shape, 0)
        return jnp.sum(jnp.where(rows == row, table, 0.0), axis=0, keepdims=True)

    places = lax.broadcasted_iota(jnp.int32, (cap, length), 0).astype(f32)

    def multiply_in(u):
        rank, source, j = unit_of(z, u)

        @when((rank > 0) & (j == 0))
        def _():
            table_copy(0, source, source).wait_recv()

        pick = (places == row_of(seats, source, j)).astype(bf16)
        rows = jnp.dot(pick, blocks[source], preferred_element_type=f32).astype(bf16)
        for kind, weights in enumerate((w_gate, w_up)):
            part = jnp.dot(rows, weights[j], preferred_element_type=f32).astype(bf16)
            for q in range(4):
                sent[u, q % 2, q // 2, :, kind * quarter : (kind + 1) * quarter] = part[
                    :, q * quarter : (q + 1) * quarter
                ]
        tp_copies(u)[0].start()

    def add_pair(u):
        copies = tp_copies(u)
        copies[0].wait_recv()
        both = sent[u, core, 1 - chip].astype(f32) + first[u, 1 - chip].astype(f32)
        pair[u] = both.astype(bf16)
        copies[1].start()

    def activate(u):
        rank, source, j = unit_of(z, u)

        @when((rank > 0) & (j == 0))
        def _():
            table_copy(1, source, source).wait_recv()

        scale_row = row_of(mixes, source, count)
        factor = jnp.sum(
            jnp.where(places == row_of(seats, source, j), scale_row, 0.0), axis=1, keepdims=True
        )
        copies = tp_copies(u)
        copies[1].wait_recv()
        value = (
            sent[u, core, chip].astype(f32)
            + first[u, chip].astype(f32)
            + second[u].astype(f32)
        ) * factor
        gate = value[:, :quarter]
        acts[u, core, chip] = (gate / (1.0 + jnp.exp(-gate)) * value[:, quarter:]).astype(bf16)
        copies[2].start()
        copies[3].start()

    def forward(u):
        copies = tp_copies(u)
        copies[2].wait_recv()
        copies[4].start()

    def multiply_out(u):
        rank, source, j = unit_of(z, u)
        copies = tp_copies(u)
        copies[3].wait_recv()
        copies[4].wait_recv()

        joined = jnp.concatenate([acts[u, q % 2, q // 2] for q in range(4)], axis=1)
        result = jnp.dot(joined, w_down[j], preferred_element_type=f32).astype(bf16)
        share = jnp.where(
            places == row_of(seats, source, j), row_of(mixes, source, j), 0.0
        ).astype(bf16)
        total[source] += lax.dot_general(
            share, result, (((0,), (0,)), ((), ())), preferred_element_type=f32
        )

        @when((rank > 0) & (j == count - 1))
        def _():
            leave(rank)

    def tick(i, carry):
        @when(i == 2)
        def _():
            finish_sums()

        @when(i == 18)
        def _():
            relay_on(1)

        @when(i == units + 4)
        def _():
            relay_on(2, range(2))

        for h, at in ((1, 3), (2, 7), (3, 11)):
            @when(i == at)
            def _():
                hop(h)

        for stage_of, delay in (
            (multiply_in, 0), (activate, 2), (forward, 4), (multiply_out, 5), (add_pair, 0),
        ):
            @when((i >= delay) & (i < units + delay))
            def _():
                stage_of(i - delay)

        @when(i == 0)
        def _():
            start_sums()

        return carry

    lax.fori_loop(0, units + 5, tick, 0)

    relay_on(2, range(2, 4))
    for part in range(4):
        rows = part_rows(part)
        answer = resid[rows, :].astype(f32) + total[z, rows]
        near_copy(part).wait_recv()
        answer = answer + coming[0, part].astype(f32)
        far_copy(1, part).wait_recv()
        out[rows, :] = (answer + coming[1, part].astype(f32)).astype(bf16)

    def settle(u, carry):
        for copy in tp_copies(u):
            copy.wait_send()
        return carry

    lax.fori_loop(0, units, settle, 0)
    for k in range(1, 4):
        other = lax.rem(z + k, 4)
        table_copy(0, other, z).wait_send()
        table_copy(1, other, z).wait_send()
        for part in range(4):
            near_copy(part).wait_send() if k == 3 else far_copy(k, part).wait_send()
    for h in range(3):
        hop_pair(h, lambda copy: copy.wait_send())
    for k in range(1, 4):
        doc_copy(lax.rem(z + k, 4), z).wait_send()
        sum_copy(lax.rem(lane + k, 4), lane).wait_send()
    for c in range(chunks):
        @when(moves)
        def _():
            swap_copy(c, z).wait_send()

        for copy in att_copies(c):
            copy.wait_send()
    for b in range(4):
        for p in range(2):
            @when(z < b)
            def _():
                up_copy(b, p).wait_send()

            @when(z > b)
            def _():
                down_copy(b, p).wait_send()


def fused_layer(
    question_q, question_kv, doc_kv, doc_lens, query_docs, ctx_pos, hidden, out_proj,
    norm_gain, router_weight, w_gate_up, w_down, expert_ids,
):
    bf16 = jnp.bfloat16
    f32 = jnp.float32
    length, heads, head_dim = question_q.shape
    width = hidden.shape[1]
    experts = router_weight.shape[1]
    pool_dev, doc_max = doc_kv.shape[:2]
    count = w_gate_up.shape[0]
    inner = w_gate_up.shape[3]
    capacity = length * expert_ids.shape[1] // experts
    units = 4 * count
    quarter = inner // 4
    chunks = 4
    some = heads // chunks
    vmem = pltpu.VMEM
    smem = pltpu.SMEM
    dma = pltpu.SemaphoreType.DMA
    block = (4, length, width)
    gain = norm_gain.reshape(width // 128, 128)
    router = jnp.swapaxes(router_weight, 0, 1)
    ids = jnp.swapaxes(expert_ids, 0, 1)
    return pl.pallas_call(
        layer_kernel,
        out_shape=jax.ShapeDtypeStruct((length, width), bf16),
        in_specs=[pl.BlockSpec(memory_space=pl.ANY)] * 13,
        out_specs=pl.BlockSpec(memory_space=vmem),
        scratch_shapes=[
            vmem(question_q.shape, bf16),
            vmem((length, 2, head_dim), bf16),
            vmem((pool_dev, doc_max, 2, head_dim), bf16),
            smem(doc_lens.shape, jnp.int32),
            smem(query_docs.shape, jnp.int32),
            smem(ctx_pos.shape, jnp.int32),
            vmem(hidden.shape, bf16),
            vmem(gain.shape, bf16),
            vmem(router.shape, bf16),
            vmem(ids.shape, jnp.int32),
            dma((10,)),
            vmem(out_proj.shape, bf16),
            vmem((4, 2, length, head_dim), bf16),
            vmem((4, 2, length, head_dim), bf16),
            vmem((heads, length, head_dim), bf16),
            vmem((5 * length, head_dim), bf16),
            vmem((5 * length, head_dim), bf16),
            vmem((chunks, some, length, head_dim), bf16),
            vmem((4, chunks, some, length, head_dim), bf16),
            vmem(block, f32),
            vmem((4, 2, length // 2, width), bf16),
            vmem((4, 2, length // 2, width), bf16),
            vmem((4, 2, length // 2, width), bf16),
            vmem((4, 2, length // 2, width), bf16),
            vmem((4, experts + 8, length), f32),
            dma,
            dma((4,)),
            dma((4,)),
            dma((chunks,)),
            dma((chunks,)),
            dma((3, chunks)),
            dma((3, chunks)),
            dma((4, 2)),
            dma((4, 2)),
            dma((4, 2)),
            dma((4, 2)),
            dma((4,)),
            dma((4,)),
            vmem((2, width // 2, 2, inner), bf16),
            vmem((count, width, inner), bf16),
            vmem((count, width, inner), bf16),
            vmem(w_down.shape, bf16),
            vmem((length, width), bf16),
            vmem((4, 8, length), f32),
            vmem((4, 8, length), f32),
            vmem(block, bf16),
            vmem((4, 8, length), f32),
            vmem((4, 8, length), f32),
            vmem((units, 2, 2, capacity, 2 * quarter), bf16),
            vmem((units, 2, capacity, 2 * quarter), bf16),
            vmem((units, capacity, 2 * quarter), bf16),
            vmem((units, capacity, 2 * quarter), bf16),
            vmem((units, 2, 2, capacity, quarter), bf16),
            vmem(block, f32),
            vmem((4, 4, length // 4, width), bf16),
            vmem((4, 4, length // 4, width), bf16),
            vmem((2, 4, length // 4, width), bf16),
            dma((2,)),
            dma,
            dma((3,)),
            dma((3,)),
            dma((4,)),
            dma((2, 4)),
            dma((2, 4)),
            dma((5, units)),
            dma((5, units)),
            dma((4, 4)),
            dma((4, 4)),
            dma((2, 4)),
        ],
        compiler_params=pltpu.CompilerParams(
            collective_id=0, has_side_effects=True, vmem_limit_bytes=60 << 20
        ),
    )(
        question_q, question_kv, doc_kv, doc_lens, query_docs, ctx_pos, hidden, gain, router,
        ids, out_proj, w_gate_up, w_down,
    )


def feed_forward(arrived, w_gate_up, w_down):
    term = jnp.einsum("erd,edgh->hegr", arrived, w_gate_up, preferred_element_type=jnp.float32)
    summed = lax.psum_scatter(
        term.astype(jnp.bfloat16), "tp", scatter_dimension=0, tiled=True
    ).astype(jnp.float32)
    activated = (jax.nn.silu(summed[:, :, 0]) * summed[:, :, 1]).astype(jnp.bfloat16)
    piece = lax.all_gather(activated, "tp", axis=0, tiled=True)
    return jnp.einsum(
        "her,ehd->erd", piece, w_down, preferred_element_type=jnp.float32
    ).astype(jnp.bfloat16)


def per_device(
    question_q,
    question_kv,
    doc_kv,
    doc_lens,
    query_docs,
    ctx_pos,
    hidden,
    out_proj,
    norm_gain,
    router_weight,
    w_gate_up,
    w_down,
    expert_ids,
):
    lanes = lax.axis_size("tp")
    groups = lax.axis_size("ep")
    lane = lax.axis_index("tp")
    device = lax.axis_index("ep")
    length, heads_here, head_dim = question_q.shape
    kv_heads = question_kv.shape[1]
    if lanes == 4 and groups == 4:
        return fused_layer(
            question_q, question_kv, doc_kv, doc_lens, query_docs, ctx_pos, hidden, out_proj,
            norm_gain, router_weight, w_gate_up, w_down, expert_ids,
        )
    kv_pick = lane * kv_heads // lanes
    scale = head_dim ** (-0.5)
    docs_per = query_docs.shape[1]
    row_pos = lax.dynamic_index_in_dim(ctx_pos, device, 0, keepdims=False)
    question_pos = row_pos[docs_per] + jnp.arange(length, dtype=jnp.int32)
    queries = rotate(question_q, question_pos).astype(jnp.bfloat16)
    own_kv = lax.dynamic_index_in_dim(question_kv, kv_pick, 1, keepdims=False)
    own_keys = rotate(own_kv[:, 0], question_pos).astype(jnp.bfloat16)
    own_values = own_kv[:, 1]
    causal = jnp.arange(length)[:, None] >= jnp.arange(length)[None, :]
    doc_keys, doc_values, valid = fetch_context(
        doc_kv, doc_lens, query_docs, row_pos, device, kv_pick
    )
    keys = jnp.concatenate([doc_keys, own_keys], axis=0)
    values = jnp.concatenate([doc_values, own_values], axis=0)
    allowed = jnp.concatenate(
        [jnp.broadcast_to(valid[None, :], (length, valid.shape[0])), causal], axis=1
    )
    scores = jnp.einsum("ihd,jd->hij", queries, keys, preferred_element_type=jnp.float32) * scale
    scores = jnp.where(allowed[None], scores, -jnp.inf)
    ceiling = jnp.max(scores, axis=-1, keepdims=True)
    probs = jnp.exp(scores - ceiling)
    denominator = jnp.sum(probs, axis=-1, keepdims=True)
    mixed = jnp.einsum(
        "hij,jd->hid", probs.astype(jnp.bfloat16), values, preferred_element_type=jnp.float32
    )
    attended = (
        jnp.transpose(mixed / denominator, (1, 0, 2))
        .reshape(length, heads_here * head_dim)
        .astype(jnp.bfloat16)
    )
    width_here = hidden.shape[1]
    projected = project(attended, out_proj)
    residual_wide = narrow(hidden.astype(jnp.float32) + projected).astype(jnp.float32)
    gain = norm_gain.astype(jnp.float32)
    squares, logit_part = lax.psum(
        (
            jnp.sum(residual_wide * residual_wide, axis=1),
            jnp.dot(
                residual_wide * gain[None, :],
                router_weight.astype(jnp.float32),
                precision=lax.Precision.HIGHEST,
            ),
        ),
        "tp",
    )
    inv_rms = lax.rsqrt(squares / D + norm_eps)
    normed = (residual_wide * inv_rms[:, None] * gain[None, :]).astype(jnp.bfloat16)
    logits = logit_part * inv_rms[:, None]
    local_experts = w_gate_up.shape[0]
    capacity = length * expert_ids.shape[1] // (local_experts * groups)
    experts = logits.shape[1]
    chosen = jnp.any(expert_ids[:, :, None] == jnp.arange(experts, dtype=jnp.int32), axis=1)
    top = jnp.max(jnp.where(chosen, logits, -jnp.inf), axis=1, keepdims=True)
    raised = jnp.where(chosen, jnp.exp(jnp.where(chosen, logits - top, 0.0)), 0.0)
    mix = raised / jnp.sum(raised, axis=1, keepdims=True)
    mix_high = mix.astype(jnp.bfloat16)
    mix_low = (mix - mix_high.astype(jnp.float32)).astype(jnp.bfloat16)
    notes = jnp.concatenate([chosen.astype(jnp.bfloat16), mix_high, mix_low], axis=1)
    notes = jnp.pad(notes, ((0, 0), (0, -notes.shape[1] % 128)))
    packed = lax.all_gather(jnp.concatenate([normed, notes], axis=1), "ep", axis=0)
    normed_all = packed[:, :, :width_here]

    def mine(index):
        start = width_here + index * experts + device * local_experts
        return lax.dynamic_slice_in_dim(packed, start, local_experts, axis=2)

    member = mine(0) > 0
    share_high = jnp.swapaxes(mine(1), 1, 2)
    share_low = jnp.swapaxes(mine(2), 1, 2)
    earlier = jnp.arange(length)[:, None] > jnp.arange(length)[None, :]
    rank = jnp.einsum(
        "nm,sme->sen",
        earlier.astype(jnp.bfloat16),
        member.astype(jnp.bfloat16),
        preferred_element_type=jnp.float32,
    )
    seat = jnp.where(jnp.swapaxes(member, 1, 2), rank.astype(jnp.int32), -1)
    picks = (seat[:, :, None, :] == jnp.arange(capacity, dtype=jnp.int32)[:, None]).astype(
        jnp.bfloat16
    )
    arrived = jnp.einsum(
        "secn,snd->escd", picks, normed_all, preferred_element_type=jnp.float32
    ).astype(jnp.bfloat16)
    rows = groups * capacity
    arrived = arrived.reshape(local_experts, rows, width_here)
    expert_out = feed_forward(arrived, w_gate_up, w_down)
    weights = jnp.stack([picks * share_high[:, :, None, :], picks * share_low[:, :, None, :]])
    partial = jnp.einsum(
        "psecn,escd->snd",
        weights,
        expert_out.reshape(local_experts, groups, capacity, width_here),
        preferred_element_type=jnp.float32,
    )
    combined = lax.psum_scatter(
        partial.astype(jnp.bfloat16).reshape(groups * length, width_here),
        "ep",
        scatter_dimension=0,
        tiled=True,
    )
    return (residual_wide + combined.astype(jnp.float32)).astype(jnp.bfloat16)


def solution(mesh):
    placed = (
        P(("grp", "ep"), "tp", None),
        P(("grp", "ep"), None, None, None),
        P(("grp", "ep"), None, None, None, None),
        P("grp"),
        P("grp", None),
        P("grp", None),
        P(("grp", "ep"), "tp"),
        P("ep", "tp"),
        P("tp"),
        P("tp", None),
        P("ep", "tp", None, None),
        P("ep", None, "tp"),
        P(("grp", "ep"), None),
    )
    return jax.shard_map(
        per_device, mesh=mesh, in_specs=placed, out_specs=P(("grp", "ep"), "tp"), check_vma=False
    )
```
